128 devices in a mesh: ctx: 16 (over x_lo, z, core), mp: 4 (over y), rep: 2 (over x_hi).
Axes of the slice: x: 4 (x_hi: 2, x_lo: 2; x = x_hi * 2 + x_lo), y: 4, z: 4, core: 2. Of those that a mesh axis runs over, the one named last changes fastest.
Arguments:
- token_pages: bfloat16 [128, 128, 2048], P('ctx'), may hold values from -13 to 13
- page_table: int32 [128], P('ctx'), may hold values from 0 to 7, as said below
- live_flags: int32 [128], P('ctx'), may hold values from 0 to 1, as said below
- lengths: int32 [32], replicated, may hold values from 1 to 1024, as said below
- decay_floor: float32 [2048], P(('mp', 'rep')), may hold values from 0.85 to 0.9998
- mixer_gain: float32 [2048], replicated, may hold values from 0.5 to 1.5
- feed_gain: float32 [2048], replicated, may hold values from 0.5 to 1.5
- trainer_mixer_in: float32 [3, 2048, 2048], P(None, ('ctx', 'mp')), may hold values from -0.125 to 0.125
- trainer_mixer_out: float32 [2048, 2048], P(None, ('ctx', 'mp')), may hold values from -0.125 to 0.125
- trainer_gate_up: float32 [2, 2048, 5632], P(None, ('ctx', 'mp')), may hold values from -0.125 to 0.125
- trainer_down: float32 [5632, 2048], P(None, ('ctx', 'mp')), may hold values from -0.078125 to 0.078125
Outputs:
- layer_output: bfloat16 [16384, 2048], P(('ctx', 'rep'), 'mp')
The draws below stay inside these ranges and needn't reach their ends.
Inputs may be any that keep to these rules, and one draw needn't show every extreme that they name: `page_table`: within each device's block of 8 entries every value 0 to 7 appears once. `live_flags`: in each device's block of 8 flags at least half (rounded down, and never fewer than one) are ones, and some device's block is all ones. The lengths sum to 128 times the number of ones in live_flags; one prompt has exactly 1024 tokens.
All inputs are finite; a program needn't handle non-finite values.
Results may differ from the reference program's by a relative error of at most 0.015.
Values may be sent and summed in bfloat16 or wider, within the bound.
A program may use at most 192 MiB of HBM per device.

```python
import math
import jax
import jax.numpy as jnp
from jax import lax

D = 2048
HEADS = 16
FF = 5632
PAGE = 128
PAGES_DEV = 8
PROMPTS = 32
TOKENS = 16384
PAGES = 128
N_CTX = 16


def pages_and_lengths(key):
    folded = jax.random.fold_in(key, 91)
    key_count, key_full, key_rank, key_shift, key_roll = jax.random.split(folded, 5)
    groups = PAGES // PAGES_DEV
    counts = jax.random.randint(key_count, (groups,), max(1, PAGES_DEV // 2), PAGES_DEV + 1).astype(jnp.int32)
    full_one = jax.random.randint(key_full, (), 0, groups)
    counts = jnp.where(jnp.arange(groups) == full_one, PAGES_DEV, counts).astype(jnp.int32)
    ranking = jax.vmap(lambda subkey: jax.random.permutation(subkey, PAGES_DEV))(jax.random.split(key_rank, groups))
    live_marks = (ranking < counts[:, None]).astype(jnp.int32).reshape(PAGES)
    live_total = (jnp.sum(counts) * PAGE).astype(jnp.int32)
    longest = 2 * TOKENS // PROMPTS
    others = PROMPTS - 1
    rest = (live_total - longest).astype(jnp.int32)
    share = (rest // others).astype(jnp.int32)
    extra = (rest % others).astype(jnp.int32)
    slots = jnp.arange(others, dtype=jnp.int32)
    base = (share + (slots < extra).astype(jnp.int32)).astype(jnp.int32)
    pairs = others // 2
    reach = (share // 2).astype(jnp.int32)
    unit = jax.random.randint(key_shift, (pairs,), 0, 1 << 20).astype(jnp.int32)
    shift = (unit % (2 * reach + 1) - reach).astype(jnp.int32)
    moved = jnp.zeros((others,), jnp.int32)
    moved = moved.at[0:2 * pairs:2].set(shift).at[1:2 * pairs:2].set(-shift)
    rest_lengths = (base + moved).astype(jnp.int32)
    lengths = jnp.concatenate([jnp.full((1,), longest, jnp.int32), rest_lengths])
    offset = jax.random.randint(key_roll, (), 0, PROMPTS)
    lengths = jnp.roll(lengths, offset).astype(jnp.int32)
    return (live_marks, lengths)


def draw_live_flags(key, part):
    return pages_and_lengths(key)[0]


def draw_lengths(key, part):
    return pages_and_lengths(key)[1]


def draw_page_table(key, part):
    groups = PAGES // PAGES_DEV
    subkeys = jax.random.split(jax.random.fold_in(key, 17), groups)
    ranking = jax.vmap(lambda subkey: jax.random.permutation(subkey, PAGES_DEV))(subkeys)
    return ranking.astype(jnp.int32).reshape(PAGES)


def draw_decay_floor(key, part):
    key_level, key_jitter = jax.random.split(jax.random.fold_in(key, 23))
    head_dim = D // HEADS
    head_level = jax.random.uniform(key_level, (HEADS, 1), jnp.float32, 0.0, 1.0)
    lowest_log = math.log(0.0003)
    highest_log = math.log(0.1)
    jitter = jnp.exp(jax.random.uniform(key_jitter, (HEADS, head_dim), jnp.float32, -0.35, 0.35))
    return (1.0 - jnp.exp(lowest_log + head_level * (highest_log - lowest_log)) * jitter).reshape(D)


def draw_token_pages(key, part):
    key_scale, key_values = jax.random.split(jax.random.fold_in(key, 5), 2)
    scales = 0.3 * jnp.exp(jax.random.uniform(key_scale, (PAGES, PAGE, 1), jnp.float32, 0.0, math.log(10.0)))
    entries = jnp.clip(jax.random.normal(key_values, (PAGES, PAGE, D), jnp.float32), -4.0, 4.0)
    return (scales * entries).astype(jnp.bfloat16)


def block_levels(stream_key, dims, cuts, smallest, top_value):
    loudness, own = 1.0, jax.random.fold_in(stream_key, 6)
    for dim, shards_of in cuts:
        heights = jnp.exp(jax.random.uniform(jax.random.fold_in(own, dim), (shards_of,), jnp.float32, smallest / len(cuts), top_value / len(cuts)))
        loudness = loudness * jnp.repeat(heights, dims[dim] // shards_of).reshape([-1 if axis == dim else 1 for axis in range(len(dims))])
    return loudness


def gaussian(key, shape, scale, bound, cuts=(), kind=jnp.bfloat16):
    drawn = scale * jax.random.normal(key, shape, jnp.float32)
    if cuts:
        drawn = drawn * block_levels(key, shape, cuts, -0.22, 0.18)
    return jnp.clip(drawn, -bound, bound).astype(kind)


def setup_inputs(seed: int = 0) -> dict:
    splits = jax.random.split(jax.random.key(seed), 12)
    token_pages = draw_token_pages(jax.random.fold_in(splits[11], 71), 0)
    page_table = draw_page_table(jax.random.fold_in(splits[11], 71), 0)
    live_flags = draw_live_flags(jax.random.fold_in(splits[11], 71), 0)
    lengths = draw_lengths(jax.random.fold_in(splits[11], 71), 0)
    decay_floor = draw_decay_floor(jax.random.fold_in(splits[11], 71), 0)
    mixer_gain = jnp.clip(1.0 + 0.1 * jax.random.normal(splits[5], (D,), jnp.float32), 0.5, 1.5)
    feed_gain = jnp.clip(1.0 + 0.1 * jax.random.normal(splits[6], (D,), jnp.float32), 0.5, 1.5)
    trainer_mixer_in = gaussian(splits[7], (3, D, D), D ** -0.5, 0.125, ((1, 64),), jnp.float32)
    trainer_mixer_out = gaussian(splits[8], (D, D), D ** -0.5, 0.125, ((1, 64),), jnp.float32)
    trainer_gate_up = gaussian(splits[9], (2, D, FF), D ** -0.5, 0.125, ((1, 64),), jnp.float32)
    trainer_down = gaussian(splits[10], (FF, D), FF ** -0.5, 0.078125, ((1, 64),), jnp.float32)
    return {"token_pages": token_pages, "page_table": page_table, "live_flags": live_flags, "lengths": lengths, "decay_floor": decay_floor, "mixer_gain": mixer_gain, "feed_gain": feed_gain, "trainer_mixer_in": trainer_mixer_in, "trainer_mixer_out": trainer_mixer_out, "trainer_gate_up": trainer_gate_up, "trainer_down": trainer_down}


norm_eps = 1e-05

def rms_scale(values_in, gain):
    mean_sq = lax.optimization_barrier(jnp.mean(values_in * values_in, axis=-1, keepdims=True))
    return values_in * lax.rsqrt(mean_sq + norm_eps) * gain

def block_recurrence(queries, keys_in, values_in, log_decay, reset_count, state_init, count_init):
    highest = lax.Precision.HIGHEST

    def advance(carried_in, block_data):
        state, count_before = carried_in
        q_block, k_block, v_block, decay_block, count_block = block_data
        cumulative = jnp.cumsum(decay_block, axis=0)
        q_scaled = q_block * jnp.exp(cumulative)
        k_scaled = k_block * jnp.exp(-cumulative)
        scores = jnp.einsum('thd,shd->hts', q_scaled, k_scaled, precision=highest)
        positions = jnp.arange(count_block.shape[0])
        allowed = (positions[:, None] >= positions[None, :]) & (count_block[:, None] == count_block[None, :])
        scores = jnp.where(allowed[None], scores, 0.0)
        outputs = jnp.einsum('hts,shd->thd', scores, v_block, precision=highest)
        from_state = jnp.einsum('thd,hde->the', q_scaled, state, precision=highest)
        outputs = outputs + jnp.where((count_block == count_before)[:, None, None], from_state, 0.0)
        last_count = count_block[-1]
        final_cum = cumulative[-1]
        weight_keys = k_block * jnp.exp(final_cum[None] - cumulative) * (count_block == last_count).astype(k_block.dtype)[:, None, None]
        retained = jnp.where(last_count == count_before, jnp.exp(final_cum)[:, :, None] * state, 0.0)
        state_next = retained + jnp.einsum('thd,the->hde', weight_keys, v_block, precision=highest)
        return ((state_next, last_count), outputs)
    final_carry, outputs_all = lax.scan(advance, (state_init, count_init), (queries, keys_in, values_in, log_decay, reset_count))
    return (outputs_all, final_carry[0])

def reference(token_pages, page_table, live_flags, lengths, decay_floor, mixer_gain, feed_gain, trainer_mixer_in, trainer_mixer_out, trainer_gate_up, trainer_down):
    head_dim = D // HEADS
    table = page_table.reshape(N_CTX, PAGES_DEV).astype(jnp.int32)
    paged = token_pages.reshape(N_CTX, PAGES_DEV, PAGE, D)
    ordered = jnp.take_along_axis(paged, table[:, :, None, None], axis=1).reshape(TOKENS, D)
    live_tokens = jnp.repeat(live_flags, PAGE).astype(jnp.int32)
    before = (jnp.cumsum(live_tokens) - live_tokens).astype(jnp.int32)
    starts = (jnp.cumsum(lengths) - lengths).astype(jnp.int32)
    resets = (live_tokens == 1) & jnp.any(before[:, None] == starts[None, :], axis=1)
    reset_count = jnp.cumsum(resets.astype(jnp.int32)).astype(jnp.int32)
    live_float = live_tokens.astype(jnp.float32)[:, None]
    w_query = trainer_mixer_in[0].astype(jnp.bfloat16)
    w_forget = trainer_mixer_in[1].astype(jnp.bfloat16)
    w_value = trainer_mixer_in[2].astype(jnp.bfloat16)
    w_output = trainer_mixer_out.astype(jnp.bfloat16)
    w_gate = trainer_gate_up[0].astype(jnp.bfloat16)
    w_up = trainer_gate_up[1].astype(jnp.bfloat16)
    w_down = trainer_down.astype(jnp.bfloat16)
    normed = rms_scale(ordered.astype(jnp.float32), mixer_gain).astype(jnp.bfloat16)
    queries = jax.nn.silu(jnp.dot(normed, w_query, preferred_element_type=jnp.float32))
    forget = decay_floor + (1.0 - decay_floor) * jax.nn.sigmoid(jnp.dot(normed, w_forget, preferred_element_type=jnp.float32))
    log_decay = jnp.log(forget) * live_float
    keys_in = (1.0 - forget) * live_float
    values_in = jnp.dot(normed, w_value, preferred_element_type=jnp.float32)
    blocks = TOKENS // PAGE
    shape_blocks = (blocks, PAGE, HEADS, head_dim)
    outputs_all, unused_state = block_recurrence(queries.reshape(shape_blocks), keys_in.reshape(shape_blocks), values_in.reshape(shape_blocks), log_decay.reshape(shape_blocks), reset_count.reshape(blocks, PAGE), jnp.zeros((HEADS, head_dim, head_dim), jnp.float32), jnp.zeros((), jnp.int32))
    mixed = outputs_all.reshape(TOKENS, HEADS, head_dim)
    head_normed = (mixed * lax.rsqrt(lax.optimization_barrier(jnp.mean(mixed * mixed, axis=-1, keepdims=True)) + norm_eps)).reshape(TOKENS, D).astype(jnp.bfloat16)
    residual = ordered.astype(jnp.float32) + jnp.dot(head_normed, w_output, preferred_element_type=jnp.float32)
    feed_in = rms_scale(residual, feed_gain).astype(jnp.bfloat16)
    gate = jnp.dot(feed_in, w_gate, preferred_element_type=jnp.float32)
    upward = jnp.dot(feed_in, w_up, preferred_element_type=jnp.float32)
    hidden = (jax.nn.silu(gate) * upward).astype(jnp.bfloat16)
    result = residual + jnp.dot(hidden, w_down, preferred_element_type=jnp.float32)
    return jnp.where(live_tokens[:, None] == 1, result, 0.0).astype(jnp.bfloat16)
```

```python
import functools

import jax
import jax.numpy as jnp
from jax import lax
from jax.experimental import pallas as pl
from jax.experimental.pallas import tpu as pltpu
from jax.sharding import PartitionSpec as P

D = 2048
HEADS = 16
PAGE = 128
EPS = 1e-05
VMEM_LIMIT = 60 * 1024 * 1024
NT = (((1,), (1,)), ((), ()))
TN = (((0,), (0,)), ((), ()))
F32 = jnp.float32
BF16 = jnp.bfloat16


def remote(src, dst, ssem, rsem, **where):
    return pltpu.make_async_remote_copy(
        src_ref=src,
        dst_ref=dst,
        send_sem=ssem,
        recv_sem=rsem,
        device_id=where,
        device_id_type=pl.DeviceIdType.MESH,
    )


def dot(a, b, dims=None):
    if dims is None:
        return jnp.dot(a, b, preferred_element_type=F32)
    return lax.dot_general(a, b, dims, preferred_element_type=F32)


def ring_neighbours():
    mp = lax.axis_size("mp")
    me = lax.axis_index("mp")
    return lax.rem(me + mp - 1, mp), me, lax.rem(me + 1, mp), lax.rem(me + 2, mp)


class Ring:
    def __init__(self, view, rows, ssem, rsem, base):
        self.view, self.rows, self.half = view, rows, rows // 2
        self.ssem, self.rsem, self.base = ssem, rsem, base

    def copy(self, owner, row, count, k, to):
        ref = self.view(owner, row, count)
        return remote(
            ref, ref, self.ssem.at[self.base + k], self.rsem.at[self.base + k], mp=to
        )

    def start(self):
        left, me, right, _ = ring_neighbours()
        self.copy(me, 0, self.rows, 0, right).start()
        self.copy(me, 0, self.rows, 1, left).start()

    def relay(self):
        left, me, right, _ = ring_neighbours()
        self.copy(left, 0, self.rows, 0, right).wait_recv()
        self.copy(left, 0, self.half, 2, right).start()
        self.copy(right, 0, self.rows, 1, left).wait_recv()
        self.copy(right, self.half, self.half, 3, left).start()

    def finish(self):
        left, me, right, far = ring_neighbours()
        self.copy(far, 0, self.half, 2, right).wait_recv()
        self.copy(far, self.half, self.half, 3, left).wait_recv()
        self.copy(me, 0, self.rows, 0, right).wait_send()
        self.copy(me, 0, self.rows, 1, left).wait_send()
        self.copy(left, 0, self.half, 2, right).wait_send()
        self.copy(right, self.half, self.half, 3, left).wait_send()


def greet(peers):
    barrier = pltpu.get_barrier_semaphore()
    for where in peers:
        pl.semaphore_signal(
            barrier, inc=1, device_id=where, device_id_type=pl.DeviceIdType.MESH
        )
    pl.semaphore_wait(barrier, len(peers))


def mixer_kernel(
    n_ctx, blocks,
    rel_ref, w_hbm, x_ref, floor_ref, live_ref, upto_ref, out_ref,
    w_ref, q_ref, k_ref, v_ref, ctot_ref, cnt_ref, st_ref, dec_ref, run_ref, mix_ref,
    msg_ref, in_ref, oth_ref, w_sem, s_sem, r_sem, p_ssem, p_rsem, g_ssem, g_rsem,
):
    width = 2 * PAGE
    ctx, rep = lax.axis_index("ctx"), lax.axis_index("rep")
    left, me, right, _ = ring_neighbours()
    wcopy = pltpu.make_async_copy(w_hbm.at[:, pl.ds(0, PAGE), :], w_ref, w_sem)
    wcopy.start()
    peers = [dict(ctx=lax.rem(ctx + o, n_ctx)) for o in range(1, n_ctx)]
    greet(peers + [dict(mp=left), dict(mp=right), dict(rep=1 - rep)])

    upto = upto_ref[...]
    count = jnp.zeros(upto.shape, F32)
    for j in range(rel_ref.shape[0]):
        start = rel_ref[j]
        count = count + jnp.where((start >= 0) & (start < upto), 1.0, 0.0)
    cnt_ref[pl.ds(0, 1), :] = jnp.zeros((1, PAGE), F32)
    for b in range(blocks):
        cnt_ref[pl.ds(b + 1, 1), :] = count[b : b + 1, :]
    run_ref[...] = jnp.zeros_like(run_ref)
    dec_ref[...] = jnp.ones_like(dec_ref)
    row = lax.broadcasted_iota(jnp.int32, (PAGE, PAGE), 0)
    col = lax.broadcasted_iota(jnp.int32, (PAGE, PAGE), 1)
    lower = row >= col
    tri = jnp.where(lower, 1.0, 0.0).astype(BF16)
    tri = jnp.concatenate([tri, tri], axis=1)
    floor = floor_ref[...]
    wcopy.wait()

    def wide(b):
        return jnp.broadcast_to(cnt_ref[pl.ds(b + 1, 1), :], (PAGE, PAGE))

    def ends(b):
        return cnt_ref[pl.ds(b, 1), :][:, PAGE - 1 :], cnt_ref[pl.ds(b + 1, 1), :][:, PAGE - 1 :]

    def project(i, _):
        rows = pl.ds(pl.multiple_of(i * 256, 256), 256)
        x = x_ref[rows, :]
        w = w_ref[...].reshape(D, 3 * width)
        p = dot(x, w)
        pq, pf, pv = p[:, :width], p[:, width : 2 * width], p[:, 2 * width :]
        q = pq / (1.0 + jnp.exp(-pq))
        forget = floor + (1.0 - floor) / (1.0 + jnp.exp(-pf))
        logd, key = jnp.log(forget), 1.0 - forget
        v_ref[rows, :] = pv.astype(BF16)
        for half in range(2):
            b = 2 * i + half
            part = slice(half * PAGE, (half + 1) * PAGE)
            here = pl.ds(pl.multiple_of(b * PAGE, PAGE), PAGE)
            live = live_ref[pl.ds(b, 1), :]
            live = jnp.concatenate([live, live], axis=1)
            lg, kk = logd[part] * live, key[part] * live
            hi = lg.astype(BF16)
            lo = (lg - hi.astype(F32)).astype(BF16)
            c = dot(tri, jnp.concatenate([hi, lo], axis=0))
            final = c[PAGE - 1 :, :]
            before, last = ends(b)
            keep = jnp.where(wide(b).T == last, 1.0, 0.0)
            keep = jnp.concatenate([keep, keep], axis=1)
            same = jnp.where(before == last, 1.0, 0.0)
            decay = jnp.exp(final) * same
            q_ref[here, :] = (q[part] * jnp.exp(c)).astype(BF16)
            k_ref[here, :] = (kk * jnp.exp(-c)).astype(BF16)
            ke = (kk * jnp.exp(final - c) * keep).astype(BF16)
            dec = dec_ref[...]
            ctot_ref[pl.ds(b, 1), :] = dec
            dec_ref[...] = dec * decay
            for h in range(2):
                lanes = slice(h * PAGE, (h + 1) * PAGE)
                state = run_ref[h]
                st_ref[b, h] = state
                add = dot(v_ref[here, lanes], ke[:, lanes], TN)
                run_ref[h] = state * decay[:, lanes] + add
        return 0

    lax.fori_loop(0, blocks // 2, project, 0)

    dec = dec_ref[...]
    for h in range(2):
        lanes = slice(h * PAGE, (h + 1) * PAGE)
        msg_ref[h, pl.ds(0, PAGE), :] = run_ref[h].astype(BF16)
        hi = dec[:, lanes].astype(BF16)
        lo = (dec[:, lanes] - hi.astype(F32)).astype(BF16)
        first = lax.broadcasted_iota(jnp.int32, (16, PAGE), 0)
        both = jnp.where(first == 0, hi.astype(F32), jnp.where(first == 1, lo.astype(F32), 0.0))
        msg_ref[h, pl.ds(PAGE, 16), :] = both.astype(BF16)

    def state_copy(o):
        return remote(
            msg_ref, in_ref.at[o - 1], s_sem.at[o - 1], r_sem.at[o - 1],
            ctx=lax.rem(ctx + o, n_ctx),
        )

    for o in range(1, n_ctx):
        state_copy(o).start()

    def within(b, _):
        here = pl.ds(pl.multiple_of(b * PAGE, PAGE), PAGE)
        rowwise = wide(b)
        allowed = lower & (rowwise.T == rowwise)
        for h in range(2):
            lanes = slice(h * PAGE, (h + 1) * PAGE)
            scores = dot(q_ref[here, lanes], k_ref[here, lanes], NT)
            scores = jnp.where(allowed, scores, 0.0).astype(BF16)
            mix_ref[here, lanes] = dot(scores, v_ref[here, lanes])
        return 0

    lax.fori_loop(0, blocks, within, 0)

    for o in range(1, n_ctx):
        state_copy(o).wait_recv()
    run_ref[...] = jnp.zeros_like(run_ref)

    def fold(i, _):
        o = n_ctx - 1 - i
        ahead = jnp.where(o <= ctx, 1.0, 0.0)
        for h in range(2):
            tail = in_ref[o - 1, h, pl.ds(PAGE, 16), :].astype(F32)
            decay = tail[0:1, :] + tail[1:2, :]
            state = run_ref[h]
            longer = state * decay + in_ref[o - 1, h, pl.ds(0, PAGE), :].astype(F32)
            run_ref[h] = state + ahead * (longer - state)
        return 0

    lax.fori_loop(0, n_ctx - 1, fold, 0)

    def outputs(b, dst, dst_row, dst_lane):
        here = pl.ds(pl.multiple_of(b * PAGE, PAGE), PAGE)
        before, _ = ends(b)
        open_rows = wide(b).T == before
        total = ctot_ref[pl.ds(b, 1), :]
        for h in range(2):
            lanes = slice(h * PAGE, (h + 1) * PAGE)
            state = st_ref[b, h] + total[:, lanes] * run_ref[h]
            old = dot(q_ref[here, lanes], state.astype(BF16), NT)
            mixed = mix_ref[here, lanes] + jnp.where(open_rows, old, 0.0)
            scale = lax.rsqrt(jnp.mean(mixed * mixed, axis=-1, keepdims=True) + EPS)
            dst[dst_row, pl.ds(dst_lane + h * PAGE, PAGE)] = (mixed * scale).astype(BF16)

    per_half = blocks // 2

    def other_half(j, _):
        outputs((1 - rep) * per_half + j, oth_ref, pl.ds(pl.multiple_of(j * PAGE, PAGE), PAGE), 0)
        return 0

    lax.fori_loop(0, per_half, other_half, 0)

    def lane_of(owner, which):
        return pl.multiple_of((owner * 2 + which) * width, width)

    swap = remote(
        oth_ref, out_ref.at[:, pl.ds(lane_of(me, rep), width)], p_ssem, p_rsem, rep=1 - rep
    )
    swap.start()
    mine = lane_of(me, rep)

    def own_half(j, _):
        outputs(rep * per_half + j, out_ref, pl.ds(pl.multiple_of(j * PAGE, PAGE), PAGE), mine)
        return 0

    lax.fori_loop(0, per_half, own_half, 0)

    def view(which):
        return lambda owner, r, n: out_ref.at[pl.ds(r, n), pl.ds(lane_of(owner, which), width)]

    half_rows = per_half * PAGE
    ring_a = Ring(view(rep), half_rows, g_ssem, g_rsem, 0)
    ring_b = Ring(view(1 - rep), half_rows, g_ssem, g_rsem, 4)
    ring_a.start()
    swap.wait_recv()
    ring_b.start()
    ring_a.relay()
    ring_b.relay()
    ring_a.finish()
    ring_b.finish()
    swap.wait_send()
    for o in range(1, n_ctx):
        state_copy(o).wait_send()


def out_kernel(
    head_ref, wo_ref, ord_ref, gain_ref, x_ref, ss_ref, res_ref, x_ssem, x_rsem, q_ssem, q_rsem
):
    left, me, right, _ = ring_neighbours()
    greet([dict(mp=left), dict(mp=right)])
    rows = head_ref.shape[0]
    res = ord_ref[...].astype(F32) + dot(head_ref[...], wo_ref[...], NT)
    res_ref[...] = res
    x_ref[me] = (res * gain_ref[...]).astype(BF16)
    ring = Ring(lambda owner, r, n: x_ref.at[owner, pl.ds(r, n), :], rows, x_ssem, x_rsem, 0)
    ring.start()
    sq = res * res
    hi = sq.astype(BF16)
    lo = (sq - hi.astype(F32)).astype(BF16)
    ones = jnp.ones((8, sq.shape[1]), BF16)
    ss_ref[me] = dot(ones, hi, NT) + dot(ones, lo, NT)
    _, _, _, far = ring_neighbours()

    def ss_copy(k, to):
        return remote(ss_ref.at[me], ss_ref.at[me], q_ssem.at[k], q_rsem.at[k], mp=to)

    def ss_wait(k, owner, to):
        return remote(ss_ref.at[owner], ss_ref.at[owner], q_ssem.at[k], q_rsem.at[k], mp=to)

    ss_copy(0, right).start()
    ss_copy(1, left).start()
    ring.relay()
    ss_wait(0, left, right).wait_recv()
    ss_wait(2, left, right).start()
    ss_wait(1, right, left).wait_recv()
    ring.finish()
    ss_wait(2, far, right).wait_recv()
    ss_copy(0, right).wait_send()
    ss_copy(1, left).wait_send()
    ss_wait(2, left, right).wait_send()


def ffn_kernel(
    hidden_cols, live_ref, ffn_hbm, x_ref, ss_ref, res_ref, out_ref,
    wg_ref, wd_ref, hid_ref, rs_ref, part_ref, send_ref, in_ref, w_sem, s_ssem, s_rsem,
):
    left, me, right, far = ring_neighbours()
    n_mp = ffn_hbm.shape[1]
    tiles = hidden_cols // PAGE
    rows = x_ref.shape[1]
    half = rows // 2
    per = ffn_hbm.shape[0] // n_mp
    copies = []
    for y in range(n_mp):
        copies.append(
            pltpu.make_async_copy(
                ffn_hbm.at[:, y, :, pl.ds(0, 2 * hidden_cols)], wg_ref.at[y], w_sem.at[y]
            )
        )
    copies.append(
        pltpu.make_async_copy(
            ffn_hbm.at[:, :, :, pl.ds(2 * hidden_cols, hidden_cols)], wd_ref, w_sem.at[n_mp]
        )
    )
    for c in copies:
        c.start()
    greet([dict(mp=left), dict(mp=right)])
    ss = ss_ref[0]
    for y in range(1, n_mp):
        ss = ss + ss_ref[y]
    scale = lax.rsqrt(ss / D + EPS)[0:1, :]
    rs_ref[...] = jnp.broadcast_to(scale, (PAGE, rows)).T
    for c in copies[:n_mp]:
        c.wait()

    def tile(j, _):
        lanes = pl.ds(pl.multiple_of(j * 256, 256), 256)
        acc = None
        for y in range(n_mp):
            w = wg_ref[y, :, :, lanes].reshape(D // n_mp, 256)
            term = dot(x_ref[y], w)
            acc = term if acc is None else acc + term
        rs = rs_ref[...]
        g, u = acc[:, :PAGE] * rs, acc[:, PAGE:] * rs
        hid_ref[:, pl.ds(pl.multiple_of(j * PAGE, PAGE), PAGE)] = (
            g / (1.0 + jnp.exp(-g)) * u
        ).astype(BF16)
        return 0

    lax.fori_loop(0, tiles, tile, 0)
    copies[n_mp].wait()

    def partial(owner):
        first = pl.ds(owner * per, per)
        w = wd_ref[first, :, :, :]
        for y in range(n_mp):
            wy = w[:, y].reshape(per * w.shape[2], hidden_cols)
            part_ref[:, pl.ds(y * PAGE, PAGE)] = dot(hid_ref[...], wy, NT)
        mine = pl.ds(pl.multiple_of(me * PAGE, PAGE), PAGE)
        theirs = pl.ds(pl.multiple_of(owner * PAGE, PAGE), PAGE)
        part_ref[:, mine] = part_ref[:, mine] + res_ref[:, theirs]

    def hop(slot, r, n, k, to):
        return remote(
            send_ref.at[slot, pl.ds(r, n), :], in_ref.at[k, pl.ds(r, n), :],
            s_ssem.at[k], s_rsem.at[k], mp=to,
        )

    far_r = hop(0, 0, half, 0, right)
    far_l = hop(0, half, half, 1, left)
    partial(far)
    send_ref[0] = part_ref[...].astype(BF16)
    far_r.start()
    far_l.start()
    near_r = hop(1, 0, rows, 2, right)
    near_l = hop(2, 0, rows, 3, left)
    partial(right)
    far_r.wait_recv()
    send_ref[1, pl.ds(0, half), :] = (
        part_ref[pl.ds(0, half), :] + in_ref[0, pl.ds(0, half), :].astype(F32)
    ).astype(BF16)
    send_ref[1, pl.ds(half, half), :] = part_ref[pl.ds(half, half), :].astype(BF16)
    near_r.start()
    partial(left)
    far_l.wait_recv()
    send_ref[2, pl.ds(half, half), :] = (
        part_ref[pl.ds(half, half), :] + in_ref[1, pl.ds(half, half), :].astype(F32)
    ).astype(BF16)
    send_ref[2, pl.ds(0, half), :] = part_ref[pl.ds(0, half), :].astype(BF16)
    near_l.start()
    partial(me)
    near_r.wait_recv()
    near_l.wait_recv()
    for p in range(rows // PAGE):
        r = pl.ds(p * PAGE, PAGE)
        total = part_ref[r, :] + in_ref[2, r, :].astype(F32) + in_ref[3, r, :].astype(F32)
        out_ref[r, :] = jnp.where(live_ref[p] == 1, total, 0.0).astype(BF16)
    far_r.wait_send()
    far_l.wait_send()
    near_r.wait_send()
    near_l.wait_send()


VM = pl.BlockSpec(memory_space=pltpu.VMEM)
SM = pl.BlockSpec(memory_space=pltpu.SMEM)
HB = pl.BlockSpec(memory_space=pl.ANY)


def params(cid):
    return pltpu.CompilerParams(
        collective_id=cid, has_side_effects=True, vmem_limit_bytes=VMEM_LIMIT
    )


def shards(
    token_pages, page_table, live_flags, lengths, decay_floor, mixer_gain, feed_gain,
    trainer_mixer_in, trainer_mixer_out, trainer_gate_up, trainer_down,
):
    n_mp, n_rep, n_ctx = lax.axis_size("mp"), lax.axis_size("rep"), lax.axis_size("ctx")
    m, r, ctx = lax.axis_index("mp"), lax.axis_index("rep"), lax.axis_index("ctx")
    pages, page, _ = token_pages.shape
    tokens = pages * page
    half = tokens // n_rep
    wl = trainer_mixer_in.shape[1]
    cols = decay_floor.shape[0]
    hid = trainer_gate_up.shape[2] // n_mp
    block = D // n_mp

    mixer = lax.dynamic_index_in_dim(
        trainer_mixer_in.reshape(3, wl, n_mp, n_rep, cols), r, 3, keepdims=False
    ).astype(BF16)
    mixer = jnp.transpose(mixer, (2, 1, 0, 3)).reshape(n_mp, wl, 3 * cols)
    got = lax.all_to_all(mixer, "mp", split_axis=0, concat_axis=0, tiled=True)
    live_total = jnp.sum(live_flags)
    note = jnp.broadcast_to(live_total.astype(BF16), (16, 3 * cols))
    sent = jnp.concatenate([got.reshape(n_mp * wl, 3 * cols), note], axis=0)
    w_qfv = lax.all_gather(sent, "ctx", axis=0)

    wo = lax.all_gather(trainer_mixer_out.astype(BF16).T, "ctx", axis=0, tiled=True)

    gate_up = trainer_gate_up.astype(BF16).reshape(2, wl, n_mp, hid // PAGE, PAGE)
    gate_up = jnp.transpose(gate_up, (2, 1, 3, 0, 4)).reshape(n_mp, wl, 2 * hid)
    down = jnp.transpose(trainer_down.astype(BF16).reshape(n_mp, hid, wl), (0, 2, 1))
    feed = jnp.concatenate([gate_up, down], axis=2)
    feed, _ = lax.optimization_barrier((feed, got))
    feed = lax.all_to_all(feed, "mp", split_axis=0, concat_axis=0, tiled=True)
    ffn = lax.all_gather(feed, "ctx", axis=0)

    ordered = jnp.take(token_pages, page_table, axis=0).reshape(tokens, D)
    wide = ordered.astype(F32)
    normed = (
        wide * lax.rsqrt(jnp.mean(wide * wide, axis=-1, keepdims=True) + EPS) * mixer_gain
    ).astype(BF16)
    lane = jnp.arange(block)
    source = (lane // wl) * (wl * n_mp) + m * wl + lane % wl
    pick = (jnp.arange(D)[:, None] == source[None, :]).astype(BF16)
    ord_half = lax.dynamic_slice_in_dim(ordered, r * half, half, 0)
    ord_cols = jnp.dot(ord_half, pick, preferred_element_type=F32).astype(BF16)
    gain_cols = jnp.take(feed_gain, source).reshape(1, block)
    live_rows = jnp.broadcast_to(live_flags.astype(F32)[:, None], (pages, page))
    page_at = (jnp.cumsum(live_flags) - live_flags) * page
    upto = page_at[:, None] + live_flags[:, None] * (jnp.arange(page, dtype=jnp.int32)[None] + 1)

    counts = w_qfv[:, n_mp * wl, 0].astype(F32)
    base = jnp.sum(jnp.where(jnp.arange(n_ctx) < ctx, counts, 0.0)).astype(jnp.int32) * page
    rel = (jnp.cumsum(lengths) - lengths - base).astype(jnp.int32)

    heads = pl.pallas_call(
        functools.partial(mixer_kernel, n_ctx, pages),
        out_shape=jax.ShapeDtypeStruct((half, D), BF16),
        in_specs=[SM, HB, VM, VM, VM, VM],
        out_specs=VM,
        scratch_shapes=[
            pltpu.VMEM((n_ctx, PAGE, 3 * cols), BF16),
            pltpu.VMEM((tokens, cols), BF16),
            pltpu.VMEM((tokens, cols), BF16),
            pltpu.VMEM((tokens, cols), BF16),
            pltpu.VMEM((pages, cols), F32),
            pltpu.VMEM((16, PAGE), F32),
            pltpu.VMEM((pages, 2, PAGE, PAGE), F32),
            pltpu.VMEM((1, cols), F32),
            pltpu.VMEM((2, PAGE, PAGE), F32),
            pltpu.VMEM((tokens, cols), F32),
            pltpu.VMEM((2, PAGE + 16, PAGE), BF16),
            pltpu.VMEM((n_ctx - 1, 2, PAGE + 16, PAGE), BF16),
            pltpu.VMEM((half, cols), BF16),
            pltpu.SemaphoreType.DMA(()),
            pltpu.SemaphoreType.DMA((n_ctx - 1,)),
            pltpu.SemaphoreType.DMA((n_ctx - 1,)),
            pltpu.SemaphoreType.DMA(()),
            pltpu.SemaphoreType.DMA(()),
            pltpu.SemaphoreType.DMA((8,)),
            pltpu.SemaphoreType.DMA((8,)),
        ],
        compiler_params=params(0),
        name="mixer",
    )(rel, w_qfv, normed, decay_floor.reshape(1, cols), live_rows, upto)

    x_all, ss_all, res = pl.pallas_call(
        out_kernel,
        out_shape=(
            jax.ShapeDtypeStruct((n_mp, half, block), BF16),
            jax.ShapeDtypeStruct((n_mp, 8, half), F32),
            jax.ShapeDtypeStruct((half, block), F32),
        ),
        in_specs=[VM] * 4,
        out_specs=(VM, VM, VM),
        scratch_shapes=[
            pltpu.SemaphoreType.DMA((4,)),
            pltpu.SemaphoreType.DMA((4,)),
            pltpu.SemaphoreType.DMA((3,)),
            pltpu.SemaphoreType.DMA((3,)),
        ],
        compiler_params=params(1),
        name="out_proj",
    )(heads, wo, ord_cols, gain_cols)

    live_half = lax.dynamic_slice_in_dim(live_flags, r * (pages // n_rep), pages // n_rep, 0)
    final = pl.pallas_call(
        functools.partial(ffn_kernel, hid),
        out_shape=jax.ShapeDtypeStruct((half, block), BF16),
        in_specs=[SM, HB, VM, VM, VM],
        out_specs=VM,
        scratch_shapes=[
            pltpu.VMEM((n_mp, n_ctx, wl, 2 * hid), BF16),
            pltpu.VMEM((n_ctx, n_mp, wl, hid), BF16),
            pltpu.VMEM((half, hid), BF16),
            pltpu.VMEM((half, PAGE), F32),
            pltpu.VMEM((half, block), F32),
            pltpu.VMEM((3, half, block), BF16),
            pltpu.VMEM((4, half, block), BF16),
            pltpu.SemaphoreType.DMA((n_mp + 1,)),
            pltpu.SemaphoreType.DMA((4,)),
            pltpu.SemaphoreType.DMA((4,)),
        ],
        compiler_params=params(2),
        name="ffn",
    )(live_half, ffn, x_all, ss_all, res)
    per = n_ctx // n_mp
    at = (lane // wl % n_mp) * (per * wl) + lane // (wl * n_mp) * wl + lane % wl
    order = (lane[:, None] == at[None, :]).astype(BF16)
    return jnp.dot(final, order, preferred_element_type=F32).astype(BF16)


def solution(mesh):
    in_specs = (
        P("ctx", None, None),
        P("ctx"),
        P("ctx"),
        P(),
        P(("mp", "rep")),
        P(),
        P(),
        P(None, ("ctx", "mp"), None),
        P(None, ("ctx", "mp")),
        P(None, ("ctx", "mp"), None),
        P(None, ("ctx", "mp")),
    )
    out_specs = P(("ctx", "rep"), "mp")
    return jax.shard_map(shards, mesh=mesh, in_specs=in_specs, out_specs=out_specs, check_vma=False)
```

```python
import functools

import jax
import jax.numpy as jnp
from jax import lax
from jax.experimental import pallas as pl
from jax.experimental.pallas import tpu as pltpu
from jax.sharding import PartitionSpec as P

D = 2048
HEADS = 16
PAGE = 128
EPS = 1e-05
VMEM_LIMIT = 60 * 1024 * 1024
NT = (((1,), (1,)), ((), ()))
TN = (((0,), (0,)), ((), ()))
F32 = jnp.float32
BF16 = jnp.bfloat16


def remote(src, dst, ssem, rsem, **where):
    return pltpu.make_async_remote_copy(
        src_ref=src,
        dst_ref=dst,
        send_sem=ssem,
        recv_sem=rsem,
        device_id=where,
        device_id_type=pl.DeviceIdType.MESH,
    )


def dot(a, b, dims=None):
    if dims is None:
        return jnp.dot(a, b, preferred_element_type=F32)
    return lax.dot_general(a, b, dims, preferred_element_type=F32)


def ring_neighbours():
    mp = lax.axis_size("mp")
    me = lax.axis_index("mp")
    return lax.rem(me + mp - 1, mp), me, lax.rem(me + 1, mp), lax.rem(me + 2, mp)


class Ring:
    def __init__(self, view, rows, ssem, rsem, base):
        self.view, self.rows, self.half = view, rows, rows // 2
        self.ssem, self.rsem, self.base = ssem, rsem, base

    def copy(self, owner, row, count, k, to):
        ref = self.view(owner, row, count)
        return remote(
            ref, ref, self.ssem.at[self.base + k], self.rsem.at[self.base + k], mp=to
        )

    def start(self):
        left, me, right, _ = ring_neighbours()
        self.copy(me, 0, self.rows, 0, right).start()
        self.copy(me, 0, self.rows, 1, left).start()

    def relay(self):
        left, me, right, _ = ring_neighbours()
        self.copy(left, 0, self.rows, 0, right).wait_recv()
        self.copy(left, 0, self.half, 2, right).start()
        self.copy(right, 0, self.rows, 1, left).wait_recv()
        self.copy(right, self.half, self.half, 3, left).start()

    def finish(self):
        left, me, right, far = ring_neighbours()
        self.copy(far, 0, self.half, 2, right).wait_recv()
        self.copy(far, self.half, self.half, 3, left).wait_recv()
        self.copy(me, 0, self.rows, 0, right).wait_send()
        self.copy(me, 0, self.rows, 1, left).wait_send()
        self.copy(left, 0, self.half, 2, right).wait_send()
        self.copy(right, self.half, self.half, 3, left).wait_send()


class Bulk:
    def __init__(self, w, pack, both, ysend, yrecv, zsend, zrecv, xsend, xrecv, csend, crecv):
        self.w, self.pack, self.both = w, pack, both
        self.ys, self.yr, self.zs, self.zr = ysend, yrecv, zsend, zrecv
        self.xs, self.xr, self.cs, self.cr = xsend, xrecv, csend, crecv
        self.started = []
        n_ctx = lax.axis_size("ctx")
        self.n_z = n_ctx // 4
        c = lax.axis_index("ctx")
        self.core, self.z, self.x = lax.rem(c, 2), lax.rem(c // 2, self.n_z), c // (2 * self.n_z)
        self.mp, self.me = lax.axis_size("mp"), lax.axis_index("mp")
        self.rep = lax.axis_index("rep")
        self.rows = w.shape[2]
        self.top, self.bottom = pl.ds(0, self.rows // 2), pl.ds(self.rows // 2, self.rows // 2)
        self.all = pl.ds(0, self.rows)

    def ctx(self, xr=0, dz=0, other=0):
        x = self.x if xr == 0 else 1 - self.x
        core = self.core if other == 0 else 1 - self.core
        return x * (2 * self.n_z) + lax.rem(self.z + dz + self.n_z, self.n_z) * 2 + core

    def owner(self, i):
        return lax.rem(self.me + self.mp - (0, 1, 3, 2)[i], self.mp) if self.pack is not None else 0

    def piece(self, i, rows, xr=0, zr=0, other=0):
        return self.w.at[self.ctx(xr, (0, -1, 1, 2)[zr], other), self.owner(i), rows, :]

    def go(self, copy):
        copy.start()
        self.started.append(copy)

    def y_copy(self, i):
        d = (0, 1, 3, 2)[i]
        to = lax.rem(self.me + d, self.mp)
        return remote(
            self.pack.at[to], self.w.at[self.ctx(), self.me], self.ys.at[i - 1], self.yr.at[i - 1],
            mp=to,
        )

    def y_start(self):
        for i in (1, 2, 3):
            self.go(self.y_copy(i))

    def z_copy(self, i, k, zr, rows):
        ref = self.piece(i, rows, 0, zr)
        to = self.ctx(0, 1 if k in (0, 2) else -1)
        return remote(ref, ref, self.zs.at[i, k], self.zr.at[i, k], ctx=to)

    def x_copies(self, i, zr, xr):
        if self.both:
            a, b = self.piece(i, self.top, xr, zr), self.piece(i, self.bottom, xr, zr)
        else:
            a, b = self.piece(i, self.all, xr, zr), None
        out = [remote(a, a, self.xs.at[i, zr, 0], self.xr.at[i, zr, 0], ctx=self.ctx(1))]
        if b is not None:
            out.append(
                remote(
                    b, b, self.xs.at[i, zr, 1], self.xr.at[i, zr, 1],
                    ctx=self.ctx(1), rep=1 - self.rep,
                )
            )
        return out

    def c_copy(self, i, xr, zr, other=0):
        ref = self.piece(i, self.all, xr, zr, other)
        return remote(
            ref, ref, self.cs.at[i, xr, zr], self.cr.at[i, xr, zr], ctx=self.ctx(0, 0, 1)
        )

    def onward(self, i, zr):
        for copy in self.x_copies(i, zr, 0):
            self.go(copy)
        self.go(self.c_copy(i, 0, zr))

    def z_start(self, i):
        if i:
            self.y_copy(i).wait_recv()
        self.go(self.z_copy(i, 0, 0, self.all))
        self.go(self.z_copy(i, 1, 0, self.all))
        self.onward(i, 0)

    def z_relay(self, i):
        self.z_copy(i, 0, 1, self.all).wait_recv()
        self.go(self.z_copy(i, 2, 1, self.top))
        self.z_copy(i, 1, 2, self.all).wait_recv()
        self.go(self.z_copy(i, 3, 2, self.bottom))
        self.onward(i, 1)
        self.onward(i, 2)

    def z_far(self, i):
        self.z_copy(i, 2, 3, self.top).wait_recv()
        self.z_copy(i, 3, 3, self.bottom).wait_recv()
        self.onward(i, 3)

    def x_take(self, i, zr):
        for copy in self.x_copies(i, zr, 1):
            copy.wait_recv()
        self.go(self.c_copy(i, 1, zr))

    def c_take(self, i):
        for xr in range(2):
            for zr in range(4):
                self.c_copy(i, xr, zr, 1).wait_recv()

    def drain(self):
        for copy in self.started:
            copy.wait_send()


def greet(peers):
    barrier = pltpu.get_barrier_semaphore()
    for where in peers:
        pl.semaphore_signal(
            barrier, inc=1, device_id=where, device_id_type=pl.DeviceIdType.MESH
        )
    pl.semaphore_wait(barrier, len(peers))


def layer_kernel(
    n_ctx, pages,
    pt_ref, live_ref, len_ref, tok_ref, floor_ref, mgain_ref, fgain_ref,
    tin_ref, tout_ref, tgu_ref, tdn_ref,
    out_ref,
    wq_ref, wo_ref, wf_ref, pkq_ref, pkf_ref, x_ref, ord_ref,
    q_ref, k_ref, v_ref, ctot_ref, cnt_ref, st_ref, dec_ref, run_ref, mix_ref,
    msg_ref, in_ref, num_ref, nin_ref, oth_ref, head_ref, xall_ref, ss_ref, res_ref,
    hid_ref, rs_ref, part_ref, send_ref, rin_ref,
    *sems,
):
    (n_ssem, n_rsem, s_sem, r_sem, p_ssem, p_rsem, g_ssem, g_rsem, a_ssem, a_rsem,
     b_ssem, b_rsem, t_ssem, t_rsem) = sems[:14]
    sq, so, sf = sems[14:22], sems[22:28], sems[28:36]
    width = 2 * PAGE
    cols, hid = width, tdn_ref.shape[1] // 4
    ctx, rep = lax.axis_index("ctx"), lax.axis_index("rep")
    left, me, right, far = ring_neighbours()
    half_pages = pages // 2
    rows = half_pages * PAGE
    wl = tin_ref.shape[1]
    bq = Bulk(wq_ref, pkq_ref, False, *sq)
    bo = Bulk(wo_ref, None, True, None, None, *so)
    bf = Bulk(wf_ref, pkf_ref, True, *sf)

    for y in range(4):
        for t in range(3):
            lane = pl.multiple_of((y * 2 + rep) * cols, cols)
            pkq_ref[y, :, pl.ds(t * cols, cols)] = tin_ref[t, :, pl.ds(lane, cols)].astype(BF16)
    wq_ref[ctx, me] = pkq_ref[me]

    peers = [dict(ctx=lax.rem(ctx + o, n_ctx)) for o in range(1, n_ctx)]
    greet(
        peers
        + [dict(mp=left), dict(mp=right), dict(mp=far), dict(rep=1 - rep)]
        + [dict(ctx=bq.ctx(1), rep=1 - rep)]
    )
    bq.y_start()
    bq.z_start(0)

    row8 = lax.broadcasted_iota(jnp.int32, (pages, PAGE), 0)
    lane8 = lax.broadcasted_iota(jnp.int32, (pages, PAGE), 1)
    upto = jnp.zeros((pages, PAGE), jnp.int32)
    alive = jnp.zeros((pages, PAGE), F32)
    so_far = jnp.int32(0)
    for b in range(pages):
        flag = live_ref[b]
        upto = jnp.where(row8 == b, so_far * PAGE + flag * (lane8 + 1), upto)
        alive = jnp.where(row8 == b, flag.astype(F32), alive)
        so_far = so_far + flag
    num_ref[...] = jnp.zeros((pages, PAGE), jnp.int32) + so_far * PAGE

    def num_copy(o):
        return remote(
            num_ref, nin_ref.at[o - 1], n_ssem.at[o - 1], n_rsem.at[o - 1],
            ctx=lax.rem(ctx + o, n_ctx),
        )

    for o in range(1, n_ctx):
        num_copy(o).start()

    wo_ref[ctx, 0] = tout_ref[...].astype(BF16)
    for y in range(4):
        for j in range(hid // PAGE):
            for t in range(2):
                pkf_ref[y, :, pl.ds(j * 2 * PAGE + t * PAGE, PAGE)] = tgu_ref[
                    t, :, pl.ds(y * hid + j * PAGE, PAGE)
                ].astype(BF16)
        pkf_ref[y, :, pl.ds(2 * hid, hid)] = tdn_ref[:, pl.ds(y * hid, hid)].astype(BF16)
    wf_ref[ctx, me] = pkf_ref[me]
    bf.y_start()

    def norm(b):
        x = tok_ref[pt_ref[b]].astype(F32)
        scale = lax.rsqrt(jnp.mean(x * x, axis=-1, keepdims=True) + EPS)
        x_ref[pl.ds(b * PAGE, PAGE), :] = (x * scale * mgain_ref[...]).astype(BF16)

    lane1 = lax.broadcasted_iota(jnp.int32, (1, PAGE), 1) // wl

    def my_columns(read, t):
        tile = None
        for k in range(4):
            turned = pltpu.roll(read(t * 4 + k), lax.rem(wl * (k + 4) - wl * me, PAGE), 1)
            tile = turned if tile is None else jnp.where(lane1 == k, turned, tile)
        return tile

    def pick(j):
        page = pt_ref[rep * half_pages + j]
        for t in range(4):
            tile = my_columns(
                lambda c: tok_ref[page, :, pl.ds(c * PAGE, PAGE)].astype(F32), t
            )
            ord_ref[pl.ds(j * PAGE, PAGE), pl.ds(t * PAGE, PAGE)] = tile

    norm(0)
    bq.z_start(1)
    bq.z_start(2)
    bo.z_start(0)
    bf.z_start(0)
    norm(1)
    norm(2)
    bq.z_start(3)
    bq.z_relay(0)
    norm(3)
    bq.z_relay(1)
    bq.z_relay(2)
    norm(4)
    norm(5)
    bq.z_relay(3)
    bq.z_far(0)
    norm(6)
    bq.z_far(1)
    bq.z_far(2)
    norm(7)
    bq.z_far(3)

    for o in range(1, n_ctx):
        num_copy(o).wait_recv()
    base = jnp.zeros((pages, PAGE), jnp.int32)
    for o in range(1, n_ctx):
        base = base + jnp.where(o <= ctx, nin_ref[o - 1], 0)
    count = jnp.zeros((pages, PAGE), F32)
    start = jnp.int32(0)
    for j in range(len_ref.shape[0]):
        count = count + jnp.where((base <= start) & (start < base + upto), 1.0, 0.0)
        start = start + len_ref[j]
    cnt_ref[pl.ds(0, 1), :] = jnp.zeros((1, PAGE), F32)
    for b in range(pages):
        cnt_ref[pl.ds(b + 1, 1), :] = count[b : b + 1, :]
    run_ref[...] = jnp.zeros_like(run_ref)
    dec_ref[...] = jnp.ones_like(dec_ref)
    row = lax.broadcasted_iota(jnp.int32, (PAGE, PAGE), 0)
    col = lax.broadcasted_iota(jnp.int32, (PAGE, PAGE), 1)
    lower = row >= col
    tri = jnp.where(lower, 1.0, 0.0).astype(BF16)
    tri = jnp.concatenate([tri, tri], axis=1)
    floor = floor_ref[...]
    for i in range(4):
        for zr in range(4):
            bq.x_take(i, zr)
    for i in range(4):
        bq.c_take(i)

    def wide(b):
        return jnp.broadcast_to(cnt_ref[pl.ds(b + 1, 1), :], (PAGE, PAGE))

    def ends(b):
        return cnt_ref[pl.ds(b, 1), :][:, PAGE - 1 :], cnt_ref[pl.ds(b + 1, 1), :][:, PAGE - 1 :]

    def project(i):
        here2 = pl.ds(i * 256, 256)
        p = dot(x_ref[here2, :], wq_ref[...].reshape(D, 3 * width))
        pq, pf, pv = p[:, :width], p[:, width : 2 * width], p[:, 2 * width :]
        q = pq / (1.0 + jnp.exp(-pq))
        forget = floor + (1.0 - floor) / (1.0 + jnp.exp(-pf))
        logd, key = jnp.log(forget), 1.0 - forget
        v_ref[here2, :] = pv.astype(BF16)
        for h2 in range(2):
            b = 2 * i + h2
            part = slice(h2 * PAGE, (h2 + 1) * PAGE)
            here = pl.ds(b * PAGE, PAGE)
            live = alive[b : b + 1, :]
            live = jnp.concatenate([live, live], axis=1)
            lg, kk = logd[part] * live, key[part] * live
            hi = lg.astype(BF16)
            lo = (lg - hi.astype(F32)).astype(BF16)
            c = dot(tri, jnp.concatenate([hi, lo], axis=0))
            final = c[PAGE - 1 :, :]
            before, last = ends(b)
            keep = jnp.where(wide(b).T == last, 1.0, 0.0)
            keep = jnp.concatenate([keep, keep], axis=1)
            same = jnp.where(before == last, 1.0, 0.0)
            decay = jnp.exp(final) * same
            q_ref[here, :] = (q[part] * jnp.exp(c)).astype(BF16)
            k_ref[here, :] = (kk * jnp.exp(-c)).astype(BF16)
            ke = (kk * jnp.exp(final - c) * keep).astype(BF16)
            dec = dec_ref[...]
            ctot_ref[pl.ds(b, 1), :] = dec
            dec_ref[...] = dec * decay
            for h in range(2):
                lanes = slice(h * PAGE, (h + 1) * PAGE)
                state = run_ref[h]
                st_ref[b, h] = state
                add = dot(v_ref[here, lanes], ke[:, lanes], TN)
                run_ref[h] = state * decay[:, lanes] + add

    project(0)
    bf.z_start(1)
    bf.z_start(2)
    project(1)
    bf.z_start(3)
    bo.z_relay(0)
    bf.z_relay(0)
    project(2)
    bo.z_far(0)
    bf.z_relay(1)
    project(3)

    dec = dec_ref[...]
    for h in range(2):
        lanes = slice(h * PAGE, (h + 1) * PAGE)
        msg_ref[h, pl.ds(0, PAGE), :] = run_ref[h].astype(BF16)
        hi = dec[:, lanes].astype(BF16)
        lo = (dec[:, lanes] - hi.astype(F32)).astype(BF16)
        first = lax.broadcasted_iota(jnp.int32, (16, PAGE), 0)
        both = jnp.where(first == 0, hi.astype(F32), jnp.where(first == 1, lo.astype(F32), 0.0))
        msg_ref[h, pl.ds(PAGE, 16), :] = both.astype(BF16)

    def state_copy(o):
        return remote(
            msg_ref, in_ref.at[o - 1], s_sem.at[o - 1], r_sem.at[o - 1],
            ctx=lax.rem(ctx + o, n_ctx),
        )

    for o in range(1, n_ctx):
        state_copy(o).start()
    bf.z_relay(2)

    def within(b, _):
        here = pl.ds(pl.multiple_of(b * PAGE, PAGE), PAGE)
        rowwise = wide(b)
        allowed = lower & (rowwise.T == rowwise)
        for h in range(2):
            lanes = slice(h * PAGE, (h + 1) * PAGE)
            scores = dot(q_ref[here, lanes], k_ref[here, lanes], NT)
            scores = jnp.where(allowed, scores, 0.0).astype(BF16)
            mix_ref[here, lanes] = dot(scores, v_ref[here, lanes])
        return 0

    lax.fori_loop(0, pages, within, 0)
    bf.z_relay(3)
    bf.z_far(0)
    for j in range(half_pages):
        pick(j)

    for o in range(1, n_ctx):
        state_copy(o).wait_recv()
    run_ref[...] = jnp.zeros_like(run_ref)

    def fold(i, _):
        o = n_ctx - 1 - i
        ahead = jnp.where(o <= ctx, 1.0, 0.0)
        for h in range(2):
            tail = in_ref[o - 1, h, pl.ds(PAGE, 16), :].astype(F32)
            decay = tail[0:1, :] + tail[1:2, :]
            state = run_ref[h]
            longer = state * decay + in_ref[o - 1, h, pl.ds(0, PAGE), :].astype(F32)
            run_ref[h] = state + ahead * (longer - state)
        return 0

    lax.fori_loop(0, n_ctx - 1, fold, 0)

    def outputs(b, dst, dst_row, dst_lane):
        here = pl.ds(pl.multiple_of(b * PAGE, PAGE), PAGE)
        before, _ = ends(b)
        open_rows = wide(b).T == before
        total = ctot_ref[pl.ds(b, 1), :]
        for h in range(2):
            lanes = slice(h * PAGE, (h + 1) * PAGE)
            state = st_ref[b, h] + total[:, lanes] * run_ref[h]
            old = dot(q_ref[here, lanes], state.astype(BF16), NT)
            mixed = mix_ref[here, lanes] + jnp.where(open_rows, old, 0.0)
            scale = lax.rsqrt(jnp.mean(mixed * mixed, axis=-1, keepdims=True) + EPS)
            dst[dst_row, pl.ds(dst_lane + h * PAGE, PAGE)] = (mixed * scale).astype(BF16)

    def other_half(j, _):
        outputs((1 - rep) * half_pages + j, oth_ref, pl.ds(pl.multiple_of(j * PAGE, PAGE), PAGE), 0)
        return 0

    lax.fori_loop(0, half_pages, other_half, 0)

    def lane_of(owner, which):
        return pl.multiple_of((owner * 2 + which) * width, width)

    swap = remote(
        oth_ref, head_ref.at[:, pl.ds(lane_of(me, rep), width)], p_ssem, p_rsem, rep=1 - rep
    )
    swap.start()
    mine = lane_of(me, rep)

    def own_half(j, _):
        outputs(rep * half_pages + j, head_ref, pl.ds(pl.multiple_of(j * PAGE, PAGE), PAGE), mine)
        return 0

    lax.fori_loop(0, half_pages, own_half, 0)

    def view(which):
        return lambda owner, r, n: head_ref.at[pl.ds(r, n), pl.ds(lane_of(owner, which), width)]

    ring_a = Ring(view(rep), rows, g_ssem, g_rsem, 0)
    ring_b = Ring(view(1 - rep), rows, g_ssem, g_rsem, 4)
    ring_a.start()
    bf.z_far(1)
    swap.wait_recv()
    ring_b.start()
    bf.z_far(2)
    ring_a.relay()
    bf.z_far(3)
    for zr in range(4):
        bo.x_take(0, zr)
    ring_b.relay()
    bo.c_take(0)
    for zr in range(4):
        bf.x_take(0, zr)
    gain = jnp.concatenate(
        [my_columns(lambda c: jnp.broadcast_to(fgain_ref[:, pl.ds(c * PAGE, PAGE)], (8, PAGE)), t)[0:1] for t in range(4)],
        axis=1,
    )
    ring_a.finish()
    ring_b.finish()

    res = ord_ref[...] + dot(head_ref[...], wo_ref[...].reshape(4 * PAGE, D), NT)
    xall_ref[me] = (res * gain).astype(BF16)
    ring = Ring(lambda owner, r, n: xall_ref.at[owner, pl.ds(r, n), :], rows, a_ssem, a_rsem, 0)
    ring.start()
    sqr = res * res
    hi = sqr.astype(BF16)
    lo = (sqr - hi.astype(F32)).astype(BF16)
    ones = jnp.ones((8, sqr.shape[1]), BF16)
    ss_ref[me] = dot(ones, hi, NT) + dot(ones, lo, NT)

    def ss_copy(k, owner, to):
        return remote(ss_ref.at[owner], ss_ref.at[owner], b_ssem.at[k], b_rsem.at[k], mp=to)

    ss_copy(0, me, right).start()
    ss_copy(1, me, left).start()
    ord_ref[...] = res
    for i in range(1, 4):
        for zr in range(4):
            bf.x_take(i, zr)
    for t in range(4):
        tile = ord_ref[:, pl.ds(t * PAGE, PAGE)]
        for k in range(4):
            turned = pltpu.roll(tile, lax.rem(wl * (4 - k) + wl * me, PAGE), 1)
            res_ref[:, pl.ds((t * 4 + k) * PAGE, PAGE)] = jnp.where(lane1 == me, turned, 0.0)
    ring.relay()
    ss_copy(0, left, right).wait_recv()
    ss_copy(2, left, right).start()
    ss_copy(1, right, left).wait_recv()
    for i in range(4):
        bf.c_take(i)
    ss_copy(2, far, right).wait_recv()
    ring.finish()

    ss = ss_ref[0]
    for y in range(1, 4):
        ss = ss + ss_ref[y]
    scale = lax.rsqrt(ss / D + EPS)[0:1, :]
    rs_ref[...] = jnp.broadcast_to(scale, (PAGE, rows)).T

    def tile(j, _):
        lanes = pl.ds(pl.multiple_of(j * 256, 256), 256)
        acc = None
        for y in range(4):
            w = wf_ref[:, y, :, lanes].reshape(D // 4, 256)
            term = dot(xall_ref[y], w)
            acc = term if acc is None else acc + term
        rs = rs_ref[...]
        g, u = acc[:, :PAGE] * rs, acc[:, PAGE:] * rs
        hid_ref[:, pl.ds(pl.multiple_of(j * PAGE, PAGE), PAGE)] = (
            g / (1.0 + jnp.exp(-g)) * u
        ).astype(BF16)
        return 0

    lax.fori_loop(0, hid // PAGE, tile, 0)

    def partial(owner):
        w = wf_ref[pl.ds(owner * 4, 4), :, :, pl.ds(2 * hid, hid)].reshape(4 * PAGE, hid)
        theirs = pl.ds(pl.multiple_of(owner * 4 * PAGE, PAGE), 4 * PAGE)
        part_ref[...] = res_ref[:, theirs] + dot(hid_ref[...], w, NT)

    half = rows // 2

    def hop(slot, r, n, k, to):
        return remote(
            send_ref.at[slot, pl.ds(r, n), :], rin_ref.at[k, pl.ds(r, n), :],
            t_ssem.at[k], t_rsem.at[k], mp=to,
        )

    far_r = hop(0, 0, half, 0, right)
    far_l = hop(0, half, half, 1, left)
    partial(far)
    send_ref[0] = part_ref[...].astype(BF16)
    far_r.start()
    far_l.start()
    near_r = hop(1, 0, rows, 2, right)
    near_l = hop(2, 0, rows, 3, left)
    upper, under = pl.ds(0, half), pl.ds(half, half)
    partial(right)
    far_r.wait_recv()
    send_ref[1, upper, :] = (part_ref[upper, :] + rin_ref[0, upper, :].astype(F32)).astype(BF16)
    send_ref[1, under, :] = part_ref[under, :].astype(BF16)
    near_r.start()
    partial(left)
    far_l.wait_recv()
    send_ref[2, under, :] = (part_ref[under, :] + rin_ref[1, under, :].astype(F32)).astype(BF16)
    send_ref[2, upper, :] = part_ref[upper, :].astype(BF16)
    near_l.start()
    partial(me)
    near_r.wait_recv()
    near_l.wait_recv()
    for p in range(half_pages):
        r = pl.ds(p * PAGE, PAGE)
        total = part_ref[r, :] + rin_ref[2, r, :].astype(F32) + rin_ref[3, r, :].astype(F32)
        out_ref[r, :] = jnp.where(live_ref[rep * half_pages + p] == 1, total, 0.0).astype(BF16)

    far_r.wait_send()
    far_l.wait_send()
    near_r.wait_send()
    near_l.wait_send()
    ss_copy(0, me, right).wait_send()
    ss_copy(1, me, left).wait_send()
    ss_copy(2, left, right).wait_send()
    swap.wait_send()
    for o in range(1, n_ctx):
        state_copy(o).wait_send()
        num_copy(o).wait_send()
    for bulk in (bq, bo, bf):
        bulk.drain()


VM = pl.BlockSpec(memory_space=pltpu.VMEM)
SM = pl.BlockSpec(memory_space=pltpu.SMEM)


def shards(
    token_pages, page_table, live_flags, lengths, decay_floor, mixer_gain, feed_gain,
    trainer_mixer_in, trainer_mixer_out, trainer_gate_up, trainer_down,
):
    n_ctx = lax.axis_size("ctx")
    pages, page, _ = token_pages.shape
    tokens, half = pages * page, pages * page // 2
    wl = trainer_mixer_in.shape[1]
    cols = decay_floor.shape[0]
    hid = trainer_gate_up.shape[2] // 4
    block = D // 4
    dma = pltpu.SemaphoreType.DMA

    def bulk_sems(n, y):
        near = [dma((3,)), dma((3,))] if y else []
        return near + [
            dma((n, 4)), dma((n, 4)), dma((n, 4, 2)), dma((n, 4, 2)), dma((n, 2, 4)), dma((n, 2, 4)),
        ]

    return pl.pallas_call(
        functools.partial(layer_kernel, n_ctx, pages),
        out_shape=jax.ShapeDtypeStruct((half, block), BF16),
        in_specs=[SM, SM, SM] + [VM] * 8,
        out_specs=VM,
        scratch_shapes=[
            pltpu.VMEM((n_ctx, 4, wl, 3 * cols), BF16),
            pltpu.VMEM((n_ctx, 1, wl, D), BF16),
            pltpu.VMEM((n_ctx, 4, wl, 3 * hid), BF16),
            pltpu.VMEM((4, wl, 3 * cols), BF16),
            pltpu.VMEM((4, wl, 3 * hid), BF16),
            pltpu.VMEM((tokens, D), BF16),
            pltpu.VMEM((half, block), F32),
            pltpu.VMEM((tokens, cols), BF16),
            pltpu.VMEM((tokens, cols), BF16),
            pltpu.VMEM((tokens, cols), BF16),
            pltpu.VMEM((pages, cols), F32),
            pltpu.VMEM((16, PAGE), F32),
            pltpu.VMEM((pages, 2, PAGE, PAGE), F32),
            pltpu.VMEM((1, cols), F32),
            pltpu.VMEM((2, PAGE, PAGE), F32),
            pltpu.VMEM((tokens, cols), F32),
            pltpu.VMEM((2, PAGE + 16, PAGE), BF16),
            pltpu.VMEM((n_ctx - 1, 2, PAGE + 16, PAGE), BF16),
            pltpu.VMEM((pages, PAGE), jnp.int32),
            pltpu.VMEM((n_ctx - 1, pages, PAGE), jnp.int32),
            pltpu.VMEM((half, cols), BF16),
            pltpu.VMEM((half, D), BF16),
            pltpu.VMEM((4, half, block), BF16),
            pltpu.VMEM((4, 8, half), F32),
            pltpu.VMEM((half, D), F32),
            pltpu.VMEM((half, hid), BF16),
            pltpu.VMEM((half, PAGE), F32),
            pltpu.VMEM((half, block), F32),
            pltpu.VMEM((3, half, block), BF16),
            pltpu.VMEM((4, half, block), BF16),
            dma((n_ctx - 1,)), dma((n_ctx - 1,)), dma((n_ctx - 1,)), dma((n_ctx - 1,)),
            dma(()), dma(()), dma((8,)), dma((8,)), dma((4,)), dma((4,)),
            dma((3,)), dma((3,)), dma((4,)), dma((4,)),
        ]
        + bulk_sems(4, True) + bulk_sems(1, False) + bulk_sems(4, True),
        compiler_params=pltpu.CompilerParams(
            collective_id=0, has_side_effects=True, vmem_limit_bytes=VMEM_LIMIT
        ),
        name="layer",
    )(
        page_table, live_flags, lengths, token_pages, decay_floor.reshape(1, cols),
        mixer_gain.reshape(1, D), feed_gain.reshape(1, D),
        trainer_mixer_in, trainer_mixer_out.T, trainer_gate_up, trainer_down.T,
    )


def solution(mesh):
    in_specs = (
        P("ctx", None, None),
        P("ctx"),
        P("ctx"),
        P(),
        P(("mp", "rep")),
        P(),
        P(),
        P(None, ("ctx", "mp"), None),
        P(None, ("ctx", "mp")),
        P(None, ("ctx", "mp"), None),
        P(None, ("ctx", "mp")),
    )
    out_specs = P(("ctx", "rep"), "mp")
    return jax.shard_map(shards, mesh=mesh, in_specs=in_specs, out_specs=out_specs, check_vma=False)
```

```python
import functools

import jax
import jax.numpy as jnp
from jax import lax
from jax.experimental import pallas as pl
from jax.experimental.pallas import tpu as pltpu
from jax.sharding import PartitionSpec as P

D = 2048
HEADS = 16
PAGE = 128
EPS = 1e-05
VMEM_LIMIT = 60 * 1024 * 1024
NT = (((1,), (1,)), ((), ()))
TN = (((0,), (0,)), ((), ()))
F32 = jnp.float32
BF16 = jnp.bfloat16


def remote(src, dst, ssem, rsem, **where):
    return pltpu.make_async_remote_copy(
        src_ref=src,
        dst_ref=dst,
        send_sem=ssem,
        recv_sem=rsem,
        device_id=where,
        device_id_type=pl.DeviceIdType.MESH,
    )


def dot(a, b, dims=None):
    if dims is None:
        return jnp.dot(a, b, preferred_element_type=F32)
    return lax.dot_general(a, b, dims, preferred_element_type=F32)


def ring_neighbours():
    mp = lax.axis_size("mp")
    me = lax.axis_index("mp")
    return lax.rem(me + mp - 1, mp), me, lax.rem(me + 1, mp), lax.rem(me + 2, mp)


class Ring:
    def __init__(self, view, rows, ssem, rsem, base):
        self.view, self.rows, self.half = view, rows, rows // 2
        self.ssem, self.rsem, self.base = ssem, rsem, base

    def copy(self, owner, row, count, k, to):
        ref = self.view(owner, row, count)
        return remote(
            ref, ref, self.ssem.at[self.base + k], self.rsem.at[self.base + k], mp=to
        )

    def start(self):
        left, me, right, _ = ring_neighbours()
        self.copy(me, 0, self.rows, 0, right).start()
        self.copy(me, 0, self.rows, 1, left).start()

    def relay(self):
        left, me, right, _ = ring_neighbours()
        self.copy(left, 0, self.rows, 0, right).wait_recv()
        self.copy(left, 0, self.half, 2, right).start()
        self.copy(right, 0, self.rows, 1, left).wait_recv()
        self.copy(right, self.half, self.half, 3, left).start()

    def finish(self):
        left, me, right, far = ring_neighbours()
        self.copy(far, 0, self.half, 2, right).wait_recv()
        self.copy(far, self.half, self.half, 3, left).wait_recv()
        self.copy(me, 0, self.rows, 0, right).wait_send()
        self.copy(me, 0, self.rows, 1, left).wait_send()
        self.copy(left, 0, self.half, 2, right).wait_send()
        self.copy(right, self.half, self.half, 3, left).wait_send()


class Bulk:
    def __init__(self, w, pack, ysend, yrecv, zsend, zrecv, xsend, xrecv, csend, crecv):
        self.w, self.pack = w, pack
        self.ys, self.yr, self.zs, self.zr = ysend, yrecv, zsend, zrecv
        self.xs, self.xr, self.cs, self.cr = xsend, xrecv, csend, crecv
        self.started = []
        self.at = Place()
        self.mp, self.me = lax.axis_size("mp"), lax.axis_index("mp")
        self.rows = w.shape[2]
        self.top, self.bottom = pl.ds(0, self.rows // 2), pl.ds(self.rows // 2, self.rows // 2)
        self.all = pl.ds(0, self.rows)

    def owner(self, i):
        return lax.rem(self.me + self.mp - (0, 1, 3, 2)[i], self.mp) if self.pack is not None else 0

    def piece(self, i, rows, xr=0, zr=0, other=0):
        return self.w.at[self.at.ctx(xr, (0, -1, 1, 2)[zr], other), self.owner(i), rows, :]

    def go(self, copy):
        copy.start()
        self.started.append(copy)

    def y_copy(self, i):
        d = (0, 1, 3, 2)[i]
        to = lax.rem(self.me + d, self.mp)
        return remote(
            self.pack.at[to], self.w.at[self.at.ctx(), self.me], self.ys.at[i - 1],
            self.yr.at[i - 1], mp=to,
        )

    def y_start(self):
        for i in (1, 2, 3):
            self.go(self.y_copy(i))

    def z_copy(self, i, xr, k, zr, rows):
        ref = self.piece(i, rows, xr, zr)
        to = self.at.ctx(0, 1 if k in (0, 2) else -1)
        return remote(ref, ref, self.zs.at[i, xr, k], self.zr.at[i, xr, k], ctx=to)

    def x_copies(self, i, zr, xr):
        a, b = self.piece(i, self.top, xr, zr), self.piece(i, self.bottom, xr, zr)
        return [
            remote(a, a, self.xs.at[i, zr, 0], self.xr.at[i, zr, 0], **self.at.same()),
            remote(b, b, self.xs.at[i, zr, 1], self.xr.at[i, zr, 1], **self.at.cross()),
        ]

    def c_copy(self, i, xr, zr, other=0):
        ref = self.piece(i, self.all, xr, zr, other)
        return remote(
            ref, ref, self.cs.at[i, xr, zr], self.cr.at[i, xr, zr], **self.at.sibling()
        )

    def x_go(self, i, zr):
        for copy in self.x_copies(i, zr, 0):
            self.go(copy)

    def x_take(self, i, zr):
        for copy in self.x_copies(i, zr, 1):
            copy.wait_recv()
        self.go(self.c_copy(i, 1, zr))

    def y_take(self, i):
        self.y_copy(i).wait_recv()

    def z_start(self, i, xr=0):
        self.go(self.z_copy(i, xr, 0, 0, self.all))
        self.go(self.z_copy(i, xr, 1, 0, self.all))
        if xr == 0:
            self.go(self.c_copy(i, 0, 0))

    def z_relay(self, i, xr=0):
        self.z_copy(i, xr, 0, 1, self.all).wait_recv()
        self.go(self.z_copy(i, xr, 2, 1, self.top))
        self.go(self.c_copy(i, xr, 1))
        self.z_copy(i, xr, 1, 2, self.all).wait_recv()
        self.go(self.z_copy(i, xr, 3, 2, self.bottom))
        self.go(self.c_copy(i, xr, 2))

    def z_far(self, i, xr=0):
        self.z_copy(i, xr, 2, 3, self.top).wait_recv()
        self.z_copy(i, xr, 3, 3, self.bottom).wait_recv()
        self.go(self.c_copy(i, xr, 3))

    def c_take(self, i):
        for xr in range(2):
            for zr in range(4):
                self.c_copy(i, xr, zr, 1).wait_recv()

    def drain(self):
        for copy in self.started:
            copy.wait_send()


class RepBulk(Bulk):
    def __init__(self, w, pack, wx, packx, ysx, yrx, zsx, zrx, *sems):
        super().__init__(w, pack, *sems)
        self.wx, self.packx = wx, packx
        self.ysx, self.yrx, self.zsx, self.zrx = ysx, yrx, zsx, zrx

    def extra(self, i, zr):
        return self.wx.at[self.at.zi((0, -1, 1, 2)[zr]), self.owner(i)]

    def yx_copy(self, i):
        to = lax.rem(self.me + (0, 1, 3, 2)[i], self.mp)
        return remote(
            self.packx.at[to], self.wx.at[self.at.zi(0), self.me], self.ysx.at[i - 1],
            self.yrx.at[i - 1], mp=to,
        )

    def y_start(self):
        for i in (1, 2, 3):
            self.go(self.y_copy(i))
            self.go(self.yx_copy(i))

    def y_take(self, i):
        self.y_copy(i).wait_recv()
        self.yx_copy(i).wait_recv()

    def zx_copy(self, i, k, zr):
        ref = self.extra(i, zr)
        to = self.at.ctx(0, 1 if k == 0 or (k == 2 and i % 2 == 0) else -1)
        return remote(ref, ref, self.zsx.at[i, k], self.zrx.at[i, k], ctx=to)

    def x_copies(self, i, zr, xr):
        a = self.piece(i, self.top, xr, zr)
        b = self.extra(i, zr)
        dst = self.piece(i, self.bottom, xr, zr)
        return [
            remote(a, a, self.xs.at[i, zr, 0], self.xr.at[i, zr, 0], **self.at.same()),
            remote(b, dst, self.xs.at[i, zr, 1], self.xr.at[i, zr, 1], **self.at.cross()),
        ]

    def z_start(self, i, xr=0):
        super().z_start(i)
        self.go(self.zx_copy(i, 0, 0))
        self.go(self.zx_copy(i, 1, 0))
        self.x_go(i, 0)

    def z_relay(self, i, xr=0):
        super().z_relay(i)
        self.zx_copy(i, 0, 1).wait_recv()
        self.zx_copy(i, 1, 2).wait_recv()
        self.go(self.zx_copy(i, 2, 1 if i % 2 == 0 else 2))
        self.x_go(i, 1)
        self.x_go(i, 2)

    def z_far(self, i, xr=0):
        super().z_far(i)
        self.zx_copy(i, 2, 3).wait_recv()
        self.x_go(i, 3)


class Place:
    def __init__(self):
        c = lax.axis_index("ctx")
        self.n_z = lax.axis_size("ctx") // 4
        self.core, self.z, self.x = lax.rem(c, 2), lax.rem(c // 2, self.n_z), c // (2 * self.n_z)
        self.rep = lax.axis_index("rep")

    def zi(self, dz):
        return lax.rem(self.z + dz + self.n_z, self.n_z)

    def ctx(self, xr=0, dz=0, other=0):
        x = self.x if xr == 0 else 1 - self.x
        core = self.core if other == 0 else 1 - self.core
        return x * (2 * self.n_z) + self.zi(dz) * 2 + core

    def same(self):
        return dict(ctx=self.ctx(1))

    def cross(self):
        return dict(ctx=self.ctx(1), rep=1 - self.rep)

    def sibling(self):
        return dict(ctx=self.ctx(0, 0, 1))


def greet(peers):
    barrier = pltpu.get_barrier_semaphore()
    for where in peers:
        pl.semaphore_signal(
            barrier, inc=1, device_id=where, device_id_type=pl.DeviceIdType.MESH
        )
    pl.semaphore_wait(barrier, len(peers))


def layer_kernel(
    n_ctx, pages,
    pt_ref, live_ref, len_ref, floor_ref, mgain_ref, fgain_ref,
    tin_ref, tok_hbm, tout_hbm, tgu_hbm, tdn_hbm,
    out_ref,
    tok_ref, tout_ref, tgu_ref, tdn_ref,
    wq_ref, wqx_ref, wo_ref, wf_ref, pkq_ref, pkqx_ref, pkf_ref, x_ref, ord_ref,
    q_ref, k_ref, v_ref, ctot_ref, cnt_ref, st_ref, dec_ref, run_ref, mix_ref,
    msg_ref, in_ref, num_ref, nin_ref, oth_ref, via_ref, head_ref, xall_ref, ss_ref, res_ref,
    hid_ref, rs_ref, part_ref, send_ref, rin_ref,
    *sems,
):
    (l_sem, n_ssem, n_rsem, s_sem, r_sem, p_ssem, p_rsem, g_ssem, g_rsem, a_ssem, a_rsem,
     b_ssem, b_rsem, t_ssem, t_rsem) = sems[:15]
    sq, so, sf = sems[15:27], sems[27:33], sems[33:41]
    width = 2 * PAGE
    cols, hid = width, tdn_ref.shape[1] // 4
    ctx, rep = lax.axis_index("ctx"), lax.axis_index("rep")
    left, me, right, far = ring_neighbours()
    half_pages = pages // 2
    rows = half_pages * PAGE
    wl = tin_ref.shape[1]
    at = Place()
    bq = RepBulk(wq_ref, pkq_ref, wqx_ref, pkqx_ref, *sq)
    bo = Bulk(wo_ref, None, None, None, *so)
    bf = Bulk(wf_ref, pkf_ref, *sf)
    loads = [
        pltpu.make_async_copy(a, b, l_sem.at[k])
        for k, (a, b) in enumerate(
            [(tgu_hbm, tgu_ref), (tdn_hbm, tdn_ref), (tout_hbm, tout_ref), (tok_hbm, tok_ref)]
        )
    ]
    for load in loads:
        load.start()

    for y in range(4):
        for t in range(3):
            lane = pl.multiple_of((y * 2 + rep) * cols, cols)
            pkq_ref[y, :, pl.ds(t * cols, cols)] = tin_ref[t, :, pl.ds(lane, cols)].astype(BF16)
            lane = pl.multiple_of((y * 2 + 1 - rep) * cols, cols)
            pkqx_ref[y, :, pl.ds(t * cols, cols)] = tin_ref[
                t, pl.ds(wl // 2, wl // 2), pl.ds(lane, cols)
            ].astype(BF16)
    wq_ref[ctx, me] = pkq_ref[me]
    wqx_ref[at.z, me] = pkqx_ref[me]

    greet(
        [at.sibling(), at.same(), at.cross()]
        + [dict(ctx=at.ctx(0, dz)) for dz in (1, 2, 3)]
        + [dict(mp=left), dict(mp=right), dict(mp=far)]
    )
    bq.y_start()
    bq.z_start(0)

    row8 = lax.broadcasted_iota(jnp.int32, (pages, PAGE), 0)
    lane8 = lax.broadcasted_iota(jnp.int32, (pages, PAGE), 1)
    upto = jnp.zeros((pages, PAGE), jnp.int32)
    alive = jnp.zeros((pages, PAGE), F32)
    so_far = jnp.int32(0)
    for b in range(pages):
        flag = live_ref[b]
        upto = jnp.where(row8 == b, so_far * PAGE + flag * (lane8 + 1), upto)
        alive = jnp.where(row8 == b, flag.astype(F32), alive)
        so_far = so_far + flag
    def num_copy(k):
        to = at.sibling() if k == 0 else at.same() if k == 4 else dict(ctx=at.ctx(0, k))
        src = num_ref.at[0 if k == 0 else 2 if k == 4 else 1]
        return remote(src, nin_ref.at[k], n_ssem.at[k], n_rsem.at[k], **to)

    num_ref[0] = jnp.zeros((pages, PAGE), jnp.int32) + so_far * PAGE
    num_copy(0).start()

    for load in loads[:3]:
        load.wait()
    wo_ref[ctx, 0] = tout_ref[...].astype(BF16)
    for y in range(4):
        for j in range(hid // PAGE):
            for t in range(2):
                pkf_ref[y, :, pl.ds(j * 2 * PAGE + t * PAGE, PAGE)] = tgu_ref[
                    t, :, pl.ds(y * hid + j * PAGE, PAGE)
                ].astype(BF16)
        pkf_ref[y, :, pl.ds(2 * hid, hid)] = tdn_ref[:, pl.ds(y * hid, hid)].astype(BF16)
    wf_ref[ctx, me] = pkf_ref[me]
    bf.y_start()
    bf.x_go(0, 0)
    bo.x_go(0, 0)
    loads[3].wait()

    def norm(b):
        x = tok_ref[pt_ref[b]].astype(F32)
        scale = lax.rsqrt(jnp.mean(x * x, axis=-1, keepdims=True) + EPS)
        x_ref[pl.ds(b * PAGE, PAGE), :] = (x * scale * mgain_ref[...]).astype(BF16)

    lane1 = lax.broadcasted_iota(jnp.int32, (1, PAGE), 1) // wl

    def my_columns(read, t):
        tile = None
        for k in range(4):
            turned = pltpu.roll(read(t * 4 + k), lax.rem(wl * (k + 4) - wl * me, PAGE), 1)
            tile = turned if tile is None else jnp.where(lane1 == k, turned, tile)
        return tile

    def pick(j):
        page = pt_ref[rep * half_pages + j]
        for t in range(4):
            tile = my_columns(
                lambda c: tok_ref[page, :, pl.ds(c * PAGE, PAGE)].astype(F32), t
            )
            ord_ref[pl.ds(j * PAGE, PAGE), pl.ds(t * PAGE, PAGE)] = tile

    norm(0)
    bq.y_take(1)
    bq.z_start(1)
    bq.y_take(2)
    bq.z_start(2)
    num_copy(0).wait_recv()
    num_ref[1] = num_ref[0] + nin_ref[0]
    for k in (1, 2, 3):
        num_copy(k).start()
    norm(1)
    norm(2)
    bq.y_take(3)
    bq.z_start(3)
    bq.z_relay(0)
    norm(3)
    for k in (1, 2, 3):
        num_copy(k).wait_recv()
    num_ref[2] = num_ref[1] + nin_ref[1] + nin_ref[2] + nin_ref[3]
    num_copy(4).start()
    norm(4)
    bq.z_relay(1)
    bq.z_relay(2)
    norm(5)
    norm(6)
    bq.z_relay(3)
    bf.z_start(0)
    bo.z_start(0)
    norm(7)
    bq.z_far(0)
    bq.z_far(1)
    bq.z_far(2)
    bq.z_far(3)
    bf.x_take(0, 0)
    bf.z_start(0, 1)
    bo.x_take(0, 0)
    bo.z_start(0, 1)
    num_copy(4).wait_recv()
    base = jnp.where(at.core == 1, nin_ref[0], 0) + jnp.where(at.x == 1, nin_ref[4], 0)
    for k in (1, 2, 3):
        base = base + jnp.where(k <= at.z, nin_ref[k], 0)
    count = jnp.zeros((pages, PAGE), F32)
    start = jnp.int32(0)
    for j in range(len_ref.shape[0]):
        count = count + jnp.where((base <= start) & (start < base + upto), 1.0, 0.0)
        start = start + len_ref[j]
    cnt_ref[pl.ds(0, 1), :] = jnp.zeros((1, PAGE), F32)
    for b in range(pages):
        cnt_ref[pl.ds(b + 1, 1), :] = count[b : b + 1, :]
    run_ref[...] = jnp.zeros_like(run_ref)
    dec_ref[...] = jnp.ones_like(dec_ref)
    row = lax.broadcasted_iota(jnp.int32, (PAGE, PAGE), 0)
    col = lax.broadcasted_iota(jnp.int32, (PAGE, PAGE), 1)
    lower = row >= col
    tri = jnp.where(lower, 1.0, 0.0).astype(BF16)
    tri = jnp.concatenate([tri, tri], axis=1)
    floor = floor_ref[...]
    for i in range(4):
        for zr in range(4):
            bq.x_take(i, zr)
    for i in range(4):
        bq.c_take(i)

    def wide(b):
        return jnp.broadcast_to(cnt_ref[pl.ds(b + 1, 1), :], (PAGE, PAGE))

    def ends(b):
        return cnt_ref[pl.ds(b, 1), :][:, PAGE - 1 :], cnt_ref[pl.ds(b + 1, 1), :][:, PAGE - 1 :]

    def project(i):
        here2 = pl.ds(i * 256, 256)
        p = dot(x_ref[here2, :], wq_ref[...].reshape(D, 3 * width))
        pq, pf, pv = p[:, :width], p[:, width : 2 * width], p[:, 2 * width :]
        q = pq / (1.0 + jnp.exp(-pq))
        forget = floor + (1.0 - floor) / (1.0 + jnp.exp(-pf))
        logd, key = jnp.log(forget), 1.0 - forget
        v_ref[here2, :] = pv.astype(BF16)
        for h2 in range(2):
            b = 2 * i + h2
            part = slice(h2 * PAGE, (h2 + 1) * PAGE)
            here = pl.ds(b * PAGE, PAGE)
            live = alive[b : b + 1, :]
            live = jnp.concatenate([live, live], axis=1)
            lg, kk = logd[part] * live, key[part] * live
            hi = lg.astype(BF16)
            lo = (lg - hi.astype(F32)).astype(BF16)
            c = dot(tri, jnp.concatenate([hi, lo], axis=0))
            final = c[PAGE - 1 :, :]
            before, last = ends(b)
            keep = jnp.where(wide(b).T == last, 1.0, 0.0)
            keep = jnp.concatenate([keep, keep], axis=1)
            same = jnp.where(before == last, 1.0, 0.0)
            decay = jnp.exp(final) * same
            q_ref[here, :] = (q[part] * jnp.exp(c)).astype(BF16)
            k_ref[here, :] = (kk * jnp.exp(-c)).astype(BF16)
            ke = (kk * jnp.exp(final - c) * keep).astype(BF16)
            dec = dec_ref[...]
            ctot_ref[pl.ds(b, 1), :] = dec
            dec_ref[...] = dec * decay
            for h in range(2):
                lanes = slice(h * PAGE, (h + 1) * PAGE)
                state = run_ref[h]
                st_ref[b, h] = state
                add = dot(v_ref[here, lanes], ke[:, lanes], TN)
                run_ref[h] = state * decay[:, lanes] + add

    def block_in(ref):
        tail = ref[pl.ds(PAGE, 16), :].astype(F32)
        return ref[pl.ds(0, PAGE), :].astype(F32), tail[0:1, :] + tail[1:2, :]

    def block_out(ref, block):
        state, decay = block
        ref[pl.ds(0, PAGE), :] = state.astype(BF16)
        hi = decay.astype(BF16)
        lo = (decay - hi.astype(F32)).astype(BF16)
        line = lax.broadcasted_iota(jnp.int32, (16, PAGE), 0)
        both = jnp.where(line == 0, hi.astype(F32), jnp.where(line == 1, lo.astype(F32), 0.0))
        ref[pl.ds(PAGE, 16), :] = both.astype(BF16)

    def join(early, late):
        return early[0] * late[1] + late[0], early[1] * late[1]

    def choose(flag, a, b):
        return jnp.where(flag, a[0], b[0]), jnp.where(flag, a[1], b[1])

    def state_copy(k):
        to = at.sibling() if k in (0, 5) else at.same() if k == 4 else dict(ctx=at.ctx(0, k))
        src = msg_ref.at[{0: 0, 4: 2, 5: 3}.get(k, 1)]
        return remote(src, in_ref.at[k], s_sem.at[k], r_sem.at[k], **to)

    def local_block(h):
        return run_ref[h], dec_ref[:, pl.ds(pl.multiple_of(h * PAGE, PAGE), PAGE)]

    project(0)
    bf.y_take(1)
    bf.z_start(1)
    bf.x_go(1, 0)
    project(1)
    project(2)
    bo.z_relay(0)
    project(3)
    block_out(msg_ref.at[0], local_block(1 - at.core))
    state_copy(0).start()

    def within(b, _):
        here = pl.ds(pl.multiple_of(b * PAGE, PAGE), PAGE)
        rowwise = wide(b)
        allowed = lower & (rowwise.T == rowwise)
        for h in range(2):
            lanes = slice(h * PAGE, (h + 1) * PAGE)
            scores = dot(q_ref[here, lanes], k_ref[here, lanes], NT)
            scores = jnp.where(allowed, scores, 0.0).astype(BF16)
            mix_ref[here, lanes] = dot(scores, v_ref[here, lanes])
        return 0

    lax.fori_loop(0, 2, within, 0)
    state_copy(0).wait_recv()
    own, sib = local_block(at.core), block_in(in_ref.at[0])
    first, second = choose(at.core == 0, own, sib), choose(at.core == 0, sib, own)
    chip = join(first, second)
    block_out(msg_ref.at[1], chip)
    for k in (1, 2, 3):
        state_copy(k).start()
    lax.fori_loop(2, pages, within, 0)
    for k in (1, 2, 3):
        state_copy(k).wait_recv()
    whole = (jnp.zeros((PAGE, PAGE), F32), jnp.ones((1, PAGE), F32))
    ahead = whole
    for z in range(at.n_z):
        there = block_in(msg_ref.at[1])
        for k in (1, 2, 3):
            there = choose(lax.rem(at.z + at.n_z - z, at.n_z) == k, block_in(in_ref.at[k]), there)
        whole = join(whole, there)
        ahead = choose(z < at.z, whole, ahead)
    block_out(msg_ref.at[2], whole)
    state_copy(4).start()
    bf.z_relay(0, 0)
    bf.z_relay(0, 1)
    for j in range(half_pages):
        pick(j)
    state_copy(4).wait_recv()
    before = choose(at.x == 1, block_in(in_ref.at[4]), (jnp.zeros((PAGE, PAGE), F32), jnp.ones((1, PAGE), F32)))
    enter0 = join(before, ahead)
    enter1 = join(enter0, first)
    block_out(msg_ref.at[3], choose(at.core == 0, enter1, enter0))
    state_copy(5).start()
    run_ref[at.core] = choose(at.core == 0, enter0, enter1)[0]
    state_copy(5).wait_recv()
    run_ref[1 - at.core] = block_in(in_ref.at[5])[0]

    def outputs(b, dst, dst_row, dst_lane):
        here = pl.ds(pl.multiple_of(b * PAGE, PAGE), PAGE)
        before, _ = ends(b)
        open_rows = wide(b).T == before
        total = ctot_ref[pl.ds(b, 1), :]
        for h in range(2):
            lanes = slice(h * PAGE, (h + 1) * PAGE)
            state = st_ref[b, h] + total[:, lanes] * run_ref[h]
            old = dot(q_ref[here, lanes], state.astype(BF16), NT)
            mixed = mix_ref[here, lanes] + jnp.where(open_rows, old, 0.0)
            scale = lax.rsqrt(jnp.mean(mixed * mixed, axis=-1, keepdims=True) + EPS)
            dst[dst_row, pl.ds(dst_lane + h * PAGE, PAGE)] = (mixed * scale).astype(BF16)

    def other_half(j, _):
        outputs((1 - rep) * half_pages + j, oth_ref, pl.ds(pl.multiple_of(j * PAGE, PAGE), PAGE), 0)
        return 0

    lax.fori_loop(0, half_pages, other_half, 0)

    def lane_of(owner, which):
        return pl.multiple_of((owner * 2 + which) * width, width)

    quarter = rows // 2

    def swap_out(k):
        to = at.same() if k == 0 else at.cross()
        return remote(
            oth_ref.at[pl.ds(k * quarter, quarter), :], via_ref.at[k], p_ssem.at[k], p_rsem.at[k], **to
        )

    def swap_on(k):
        to = at.cross() if k == 0 else at.same()
        which = rep if k == 0 else 1 - rep
        return remote(
            via_ref.at[k],
            head_ref.at[pl.ds(k * quarter, quarter), pl.ds(lane_of(me, which), width)],
            p_ssem.at[2 + k], p_rsem.at[2 + k], **to,
        )

    swap_out(0).start()
    swap_out(1).start()
    mine = lane_of(me, rep)

    def own_half(j, _):
        outputs(rep * half_pages + j, head_ref, pl.ds(pl.multiple_of(j * PAGE, PAGE), PAGE), mine)
        return 0

    lax.fori_loop(0, half_pages, own_half, 0)

    def view(which):
        return lambda owner, r, n: head_ref.at[pl.ds(r, n), pl.ds(lane_of(owner, which), width)]

    ring_a = Ring(view(rep), rows, g_ssem, g_rsem, 0)
    ring_b = Ring(view(1 - rep), rows, g_ssem, g_rsem, 4)
    ring_a.start()
    swap_out(0).wait_recv()
    swap_on(0).start()
    swap_out(1).wait_recv()
    swap_on(1).start()
    bf.y_take(2)
    bf.z_start(2)
    bf.z_far(0, 0)
    bf.z_far(0, 1)
    bo.z_relay(0, 1)
    bo.z_far(0)
    bf.x_go(2, 0)
    bf.z_relay(1)
    bf.x_go(1, 1)
    swap_on(0).wait_recv()
    swap_on(1).wait_recv()
    ring_b.start()
    ring_a.relay()
    bf.y_take(3)
    bf.z_start(3)
    bf.x_go(1, 2)
    bf.x_go(3, 0)
    bf.z_relay(2)
    bf.x_go(2, 1)
    ring_b.relay()
    bo.z_far(0, 1)
    bf.z_far(1)
    bf.x_go(1, 3)
    bf.z_relay(3)
    bf.x_go(2, 2)
    bf.x_go(3, 1)
    bf.x_go(3, 2)
    bf.z_far(2)
    bf.x_go(2, 3)
    bo.c_take(0)
    gain = jnp.concatenate(
        [my_columns(lambda c: jnp.broadcast_to(fgain_ref[:, pl.ds(c * PAGE, PAGE)], (8, PAGE)), t)[0:1] for t in range(4)],
        axis=1,
    )
    ring_a.finish()
    ring_b.finish()

    res = ord_ref[...] + dot(head_ref[...], wo_ref[...].reshape(4 * PAGE, D), NT)
    xall_ref[me] = (res * gain).astype(BF16)
    ring = Ring(lambda owner, r, n: xall_ref.at[owner, pl.ds(r, n), :], rows, a_ssem, a_rsem, 0)
    ring.start()
    sqr = res * res
    hi = sqr.astype(BF16)
    lo = (sqr - hi.astype(F32)).astype(BF16)
    ones = jnp.ones((8, sqr.shape[1]), BF16)
    ss_ref[me] = dot(ones, hi, NT) + dot(ones, lo, NT)

    def ss_copy(k, owner, to):
        return remote(ss_ref.at[owner], ss_ref.at[owner], b_ssem.at[k], b_rsem.at[k], mp=to)

    ss_copy(0, me, right).start()
    ss_copy(1, me, left).start()
    ord_ref[...] = res
    ord_ref[...] = res
    for t in range(4):
        tile = ord_ref[:, pl.ds(t * PAGE, PAGE)]
        for k in range(4):
            turned = pltpu.roll(tile, lax.rem(wl * (4 - k) + wl * me, PAGE), 1)
            res_ref[:, pl.ds((t * 4 + k) * PAGE, PAGE)] = jnp.where(lane1 == me, turned, 0.0)
    ring.relay()
    ss_copy(0, left, right).wait_recv()
    ss_copy(2, left, right).start()
    ss_copy(1, right, left).wait_recv()
    bf.z_far(3)
    bf.x_go(3, 3)
    for i in range(1, 4):
        for zr in range(4):
            bf.x_take(i, zr)
    for i in range(4):
        bf.c_take(i)
    ss_copy(2, far, right).wait_recv()
    ring.finish()

    ss = ss_ref[0]
    for y in range(1, 4):
        ss = ss + ss_ref[y]
    scale = lax.rsqrt(ss / D + EPS)[0:1, :]
    rs_ref[...] = jnp.broadcast_to(scale, (PAGE, rows)).T

    def tile(j, _):
        lanes = pl.ds(pl.multiple_of(j * 256, 256), 256)
        acc = None
        for y in range(4):
            w = wf_ref[:, y, :, lanes].reshape(D // 4, 256)
            term = dot(xall_ref[y], w)
            acc = term if acc is None else acc + term
        rs = rs_ref[...]
        g, u = acc[:, :PAGE] * rs, acc[:, PAGE:] * rs
        hid_ref[:, pl.ds(pl.multiple_of(j * PAGE, PAGE), PAGE)] = (
            g / (1.0 + jnp.exp(-g)) * u
        ).astype(BF16)
        return 0

    lax.fori_loop(0, hid // PAGE, tile, 0)

    def partial(owner):
        w = wf_ref[pl.ds(owner * 4, 4), :, :, pl.ds(2 * hid, hid)].reshape(4 * PAGE, hid)
        theirs = pl.ds(pl.multiple_of(owner * 4 * PAGE, PAGE), 4 * PAGE)
        part_ref[...] = res_ref[:, theirs] + dot(hid_ref[...], w, NT)

    half = rows // 2

    def hop(slot, r, n, k, to):
        return remote(
            send_ref.at[slot, pl.ds(r, n), :], rin_ref.at[k, pl.ds(r, n), :],
            t_ssem.at[k], t_rsem.at[k], mp=to,
        )

    far_r = hop(0, 0, half, 0, right)
    far_l = hop(0, half, half, 1, left)
    partial(far)
    send_ref[0] = part_ref[...].astype(BF16)
    far_r.start()
    far_l.start()
    near_r = hop(1, 0, rows, 2, right)
    near_l = hop(2, 0, rows, 3, left)
    upper, under = pl.ds(0, half), pl.ds(half, half)
    partial(right)
    far_r.wait_recv()
    send_ref[1, upper, :] = (part_ref[upper, :] + rin_ref[0, upper, :].astype(F32)).astype(BF16)
    send_ref[1, under, :] = part_ref[under, :].astype(BF16)
    near_r.start()
    partial(left)
    far_l.wait_recv()
    send_ref[2, under, :] = (part_ref[under, :] + rin_ref[1, under, :].astype(F32)).astype(BF16)
    send_ref[2, upper, :] = part_ref[upper, :].astype(BF16)
    near_l.start()
    partial(me)
    near_r.wait_recv()
    near_l.wait_recv()
    for p in range(half_pages):
        r = pl.ds(p * PAGE, PAGE)
        total = part_ref[r, :] + rin_ref[2, r, :].astype(F32) + rin_ref[3, r, :].astype(F32)
        out_ref[r, :] = jnp.where(live_ref[rep * half_pages + p] == 1, total, 0.0).astype(BF16)

    far_r.wait_send()
    far_l.wait_send()
    near_r.wait_send()
    near_l.wait_send()
    ss_copy(0, me, right).wait_send()
    ss_copy(1, me, left).wait_send()
    ss_copy(2, left, right).wait_send()
    for k in range(2):
        swap_out(k).wait_send()
        swap_on(k).wait_send()
    for k in range(6):
        state_copy(k).wait_send()
    for k in range(5):
        num_copy(k).wait_send()
    for bulk in (bq, bo, bf):
        bulk.drain()


VM = pl.BlockSpec(memory_space=pltpu.VMEM)
HB = pl.BlockSpec(memory_space=pl.ANY)
SM = pl.BlockSpec(memory_space=pltpu.SMEM)


def shards(
    token_pages, page_table, live_flags, lengths, decay_floor, mixer_gain, feed_gain,
    trainer_mixer_in, trainer_mixer_out, trainer_gate_up, trainer_down,
):
    n_ctx = lax.axis_size("ctx")
    pages, page, _ = token_pages.shape
    tokens, half = pages * page, pages * page // 2
    wl = trainer_mixer_in.shape[1]
    cols = decay_floor.shape[0]
    hid = trainer_gate_up.shape[2] // 4
    block = D // 4
    dma = pltpu.SemaphoreType.DMA

    def bulk_sems(n, y):
        near = [dma((3,)), dma((3,))] if y else []
        return near + [
            dma((n, 2, 4)), dma((n, 2, 4)), dma((n, 4, 2)), dma((n, 4, 2)),
            dma((n, 2, 4)), dma((n, 2, 4)),
        ]

    return pl.pallas_call(
        functools.partial(layer_kernel, n_ctx, pages),
        out_shape=jax.ShapeDtypeStruct((half, block), BF16),
        in_specs=[SM, SM, SM] + [VM] * 4 + [HB] * 4,
        out_specs=VM,
        scratch_shapes=[
            pltpu.VMEM((pages, page, D), BF16),
            pltpu.VMEM((wl, D), F32),
            pltpu.VMEM((2, wl, 4 * hid), F32),
            pltpu.VMEM((wl, 4 * hid), F32),
            pltpu.VMEM((n_ctx, 4, wl, 3 * cols), BF16),
            pltpu.VMEM((4, 4, wl // 2, 3 * cols), BF16),
            pltpu.VMEM((n_ctx, 1, wl, D), BF16),
            pltpu.VMEM((n_ctx, 4, wl, 3 * hid), BF16),
            pltpu.VMEM((4, wl, 3 * cols), BF16),
            pltpu.VMEM((4, wl // 2, 3 * cols), BF16),
            pltpu.VMEM((4, wl, 3 * hid), BF16),
            pltpu.VMEM((tokens, D), BF16),
            pltpu.VMEM((half, block), F32),
            pltpu.VMEM((tokens, cols), BF16),
            pltpu.VMEM((tokens, cols), BF16),
            pltpu.VMEM((tokens, cols), BF16),
            pltpu.VMEM((pages, cols), F32),
            pltpu.VMEM((16, PAGE), F32),
            pltpu.VMEM((pages, 2, PAGE, PAGE), F32),
            pltpu.VMEM((1, cols), F32),
            pltpu.VMEM((2, PAGE, PAGE), F32),
            pltpu.VMEM((tokens, cols), F32),
            pltpu.VMEM((4, PAGE + 16, PAGE), BF16),
            pltpu.VMEM((6, PAGE + 16, PAGE), BF16),
            pltpu.VMEM((3, pages, PAGE), jnp.int32),
            pltpu.VMEM((5, pages, PAGE), jnp.int32),
            pltpu.VMEM((half, cols), BF16),
            pltpu.VMEM((2, half // 2, cols), BF16),
            pltpu.VMEM((half, D), BF16),
            pltpu.VMEM((4, half, block), BF16),
            pltpu.VMEM((4, 8, half), F32),
            pltpu.VMEM((half, D), F32),
            pltpu.VMEM((half, hid), BF16),
            pltpu.VMEM((half, PAGE), F32),
            pltpu.VMEM((half, block), F32),
            pltpu.VMEM((3, half, block), BF16),
            pltpu.VMEM((4, half, block), BF16),
            dma((4,)), dma((5,)), dma((5,)), dma((6,)), dma((6,)),
            dma((4,)), dma((4,)), dma((8,)), dma((8,)), dma((4,)), dma((4,)),
            dma((3,)), dma((3,)), dma((4,)), dma((4,)),
        ]
        + [dma((3,)), dma((3,)), dma((4, 3)), dma((4, 3))]
        + bulk_sems(4, True) + bulk_sems(1, False) + bulk_sems(4, True),
        compiler_params=pltpu.CompilerParams(
            collective_id=0, has_side_effects=True, vmem_limit_bytes=VMEM_LIMIT
        ),
        name="layer",
    )(
        page_table, live_flags, lengths, decay_floor.reshape(1, cols),
        mixer_gain.reshape(1, D), feed_gain.reshape(1, D),
        trainer_mixer_in, token_pages, trainer_mixer_out.T, trainer_gate_up, trainer_down.T,
    )


def solution(mesh):
    in_specs = (
        P("ctx", None, None),
        P("ctx"),
        P("ctx"),
        P(),
        P(("mp", "rep")),
        P(),
        P(),
        P(None, ("ctx", "mp"), None),
        P(None, ("ctx", "mp")),
        P(None, ("ctx", "mp"), None),
        P(None, ("ctx", "mp")),
    )
    out_specs = P(("ctx", "rep"), "mp")
    return jax.shard_map(shards, mesh=mesh, in_specs=in_specs, out_specs=out_specs, check_vma=False)
```

```python
import functools

import jax
import jax.numpy as jnp
from jax import lax
from jax.experimental import pallas as pl
from jax.experimental.pallas import tpu as pltpu
from jax.sharding import PartitionSpec as P

D = 2048
HEADS = 16
PAGE = 128
EPS = 1e-05
VMEM_LIMIT = 67043328
NT = (((1,), (1,)), ((), ()))
TN = (((0,), (0,)), ((), ()))
F32 = jnp.float32
BF16 = jnp.bfloat16


def remote(src, dst, ssem, rsem, **where):
    return pltpu.make_async_remote_copy(
        src_ref=src,
        dst_ref=dst,
        send_sem=ssem,
        recv_sem=rsem,
        device_id=where,
        device_id_type=pl.DeviceIdType.MESH,
    )


def dot(a, b, dims=None):
    if dims is None:
        return jnp.dot(a, b, preferred_element_type=F32)
    return lax.dot_general(a, b, dims, preferred_element_type=F32)


def ring_neighbours():
    mp = lax.axis_size("mp")
    me = lax.axis_index("mp")
    return lax.rem(me + mp - 1, mp), me, lax.rem(me + 1, mp), lax.rem(me + 2, mp)


class Ring:
    def __init__(self, view, rows, whole, ssem, rsem, n):
        self.view, self.half, self.whole = view, rows // 2, whole
        self.ssem, self.rsem, self.n = ssem, rsem, n

    def copy(self, owner, part, k):
        left, _, right, _ = ring_neighbours()
        ref = self.view(owner, part * self.half, self.half)
        return remote(
            ref, ref, self.ssem.at[self.n], self.rsem.at[self.n, k // 2],
            mp=right if k % 2 == 0 else left,
        )

    def take(self, stage):
        left, _, right, _ = ring_neighbours()
        ref = self.view(0, 0, 2 * self.half)
        remote(ref, ref, self.ssem.at[self.n], self.rsem.at[self.n, stage], mp=right).wait_recv()

    def start(self):
        _, me, _, _ = ring_neighbours()
        for k, part in enumerate((0, 1, 1, 0)):
            self.copy(me, part, k).start()

    def relay(self):
        left, _, right, _ = ring_neighbours()
        self.take(0)
        self.copy(left, 0, 4).start()
        self.copy(right, 1, 5).start()

    def near(self):
        self.take(1)

    def finish(self):
        _, _, right, _ = ring_neighbours()
        self.take(2)
        remote(
            self.whole, self.whole, self.ssem.at[self.n], self.rsem.at[self.n, 2], mp=right
        ).wait_send()


class Bulk:
    def __init__(self, hold, w, pack, ysend, yrecv, send, near, far, xrecv, crecv):
        self.w, self.pack = w, pack
        self.ys, self.yr, self.send, self.zn, self.zf = ysend, yrecv, send, near, far
        self.xr, self.cr = xrecv, crecv
        self.pending, self.hold = [], hold
        self.at = Place()
        self.mp, self.me = lax.axis_size("mp"), lax.axis_index("mp")
        self.rows = w.shape[2]
        self.top, self.bottom = pl.ds(0, self.rows // 2), pl.ds(self.rows // 2, self.rows // 2)
        self.all = pl.ds(0, self.rows)

    def span(self, n):
        if self.w.shape[1] == 1:
            return self.w.at[pl.ds(0, n)]
        return self.w.at[0, pl.ds(0, n)] if n < 4 else self.w.at[pl.ds(0, n // 4)]

    def wait_in(self, ref, sem):
        remote(ref, ref, self.send, sem, **self.at.sibling()).wait_recv()

    def wait_out(self, ref, sem):
        remote(ref, ref, sem, self.cr.at[0], **self.at.sibling()).wait_send()

    def owner(self, i):
        return lax.rem(self.me + self.mp - (0, 1, 3, 2)[i], self.mp) if self.pack is not None else 0

    def piece(self, i, rows, xr=0, zr=0, other=0):
        return self.w.at[self.at.ctx(xr, (0, -1, 1, 2)[zr], other), self.owner(i), rows, :]

    def go(self, copy):
        copy.start()

    def y_copy(self, i):
        d = (0, 1, 3, 2)[i]
        to = lax.rem(self.me + d, self.mp)
        return remote(
            self.pack.at[to], self.w.at[self.at.ctx(), self.me], self.ys, self.yr.at[i - 1], mp=to,
        )

    def y_start(self, which=(1, 2, 3)):
        for i in which:
            self.go(self.y_copy(i))

    def z_copy(self, i, xr, k, zr, rows):
        ref = self.piece(i, rows, xr, zr)
        to = self.at.ctx(0, 1 if k in (0, 2) else -1)
        got = (self.zn if k < 2 else self.zf).at[i, xr]
        return remote(ref, ref, self.send, got, ctx=to)

    def x_copies(self, i, zr, xr):
        a, b = self.piece(i, self.top, xr, zr), self.piece(i, self.bottom, xr, zr)
        return [
            remote(a, a, self.send, self.xr.at[i, zr], **self.at.same()),
            remote(b, b, self.send, self.xr.at[i, zr], **self.at.cross()),
        ]

    def c_sem(self, i, xr):
        return self.cr.at[i]

    def c_copy(self, i, xr, zr):
        ref = self.piece(i, self.all, xr, zr)
        return remote(ref, ref, self.send, self.c_sem(i, xr), **self.at.sibling())

    def c_go(self, i, xr, zr):
        if self.hold:
            self.pending.append((i, xr, zr))
        else:
            self.go(self.c_copy(i, xr, zr))

    def flush(self, hold):
        for piece in self.pending:
            self.go(self.c_copy(*piece))
        self.pending, self.hold = [], hold

    def x_go(self, i, zr):
        for copy in self.x_copies(i, zr, 0):
            self.go(copy)

    def x_take(self, i, zr):
        self.wait_in(self.piece(i, self.all, 1, zr), self.xr.at[i, zr])
        self.c_go(i, 1, zr)

    def y_take(self, i):
        self.y_copy(i).wait_recv()

    def z_start(self, i, xr=0):
        self.go(self.z_copy(i, xr, 0, 0, self.all))
        self.go(self.z_copy(i, xr, 1, 0, self.all))
        if xr == 0:
            self.c_go(i, 0, 0)

    def z_relay(self, i, xr=0):
        self.wait_in(self.span(2), self.zn.at[i, xr])
        self.go(self.z_copy(i, xr, 2, 1, self.top))
        self.go(self.z_copy(i, xr, 3, 2, self.bottom))
        self.c_go(i, xr, 1)
        self.c_go(i, xr, 2)

    def z_far(self, i, xr=0):
        self.wait_in(self.piece(i, self.all, xr, 3), self.zf.at[i, xr])
        self.c_go(i, xr, 3)

    def c_take(self, i):
        self.wait_in(self.span(8), self.cr.at[i])

    def drain(self):
        if self.pack is None:
            self.wait_out(self.span(15), self.send)
        else:
            self.wait_out(self.span(60), self.send)
            self.wait_out(self.span(3), self.ys)


class RepBulk(Bulk):
    def __init__(self, w, pack, wx, packx, ysx, yrx, zsx, znx, zfx, *sems):
        super().__init__(False, w, pack, *sems)
        self.wx, self.packx = wx, packx
        self.ysx, self.yrx, self.zsx, self.znx, self.zfx = ysx, yrx, zsx, znx, zfx

    def extra(self, i, zr):
        return self.wx.at[self.at.zi((0, -1, 1, 2)[zr]), self.owner(i)]

    def yx_copy(self, i):
        to = lax.rem(self.me + (0, 1, 3, 2)[i], self.mp)
        return remote(
            self.packx.at[to], self.wx.at[self.at.zi(0), self.me], self.ysx, self.yrx.at[i - 1],
            mp=to,
        )

    def y_start(self, which=(1, 2, 3)):
        for i in which:
            self.go(self.y_copy(i))
            self.go(self.yx_copy(i))

    def y_take(self, i):
        self.y_copy(i).wait_recv()
        self.yx_copy(i).wait_recv()

    def zx_copy(self, i, k, zr):
        ref = self.extra(i, zr)
        to = self.at.ctx(0, 1 if k == 0 or (k == 2 and i % 2 == 0) else -1)
        return remote(ref, ref, self.zsx, (self.znx if k < 2 else self.zfx).at[i], ctx=to)

    def x_copies(self, i, zr, xr):
        a = self.piece(i, self.top, xr, zr)
        b = self.extra(i, zr)
        dst = self.piece(i, self.bottom, xr, zr)
        return [
            remote(a, a, self.send, self.xr.at[i, zr], **self.at.same()),
            remote(b, dst, self.send, self.xr.at[i, zr], **self.at.cross()),
        ]

    def c_sem(self, i, xr):
        return self.cr.at[xr]

    def c_take(self, xr):
        self.wait_in(self.span(16), self.cr.at[xr])

    def z_start(self, i, xr=0):
        super().z_start(i)
        self.go(self.zx_copy(i, 0, 0))
        self.go(self.zx_copy(i, 1, 0))
        self.x_go(i, 0)

    def z_relay(self, i, xr=0):
        super().z_relay(i)
        self.wait_in(self.wx.at[0, pl.ds(0, 2)], self.znx.at[i])
        self.go(self.zx_copy(i, 2, 1 if i % 2 == 0 else 2))
        self.x_go(i, 1)
        self.x_go(i, 2)

    def z_far(self, i, xr=0):
        super().z_far(i)
        self.zx_copy(i, 2, 3).wait_recv()
        self.x_go(i, 3)

    def drain(self):
        super().drain()
        self.wait_out(self.wx.at[pl.ds(0, 3)], self.zsx)
        self.wait_out(self.wx.at[0, pl.ds(0, 3)], self.ysx)


class Place:
    def __init__(self):
        c = lax.axis_index("ctx")
        self.n_z = lax.axis_size("ctx") // 4
        self.core, self.z, self.x = lax.rem(c, 2), lax.rem(c // 2, self.n_z), c // (2 * self.n_z)
        self.rep = lax.axis_index("rep")

    def zi(self, dz):
        return lax.rem(self.z + dz + self.n_z, self.n_z)

    def ctx(self, xr=0, dz=0, other=0):
        x = self.x if xr == 0 else 1 - self.x
        core = self.core if other == 0 else 1 - self.core
        return x * (2 * self.n_z) + self.zi(dz) * 2 + core

    def same(self):
        return dict(ctx=self.ctx(1))

    def cross(self):
        return dict(ctx=self.ctx(1), rep=1 - self.rep)

    def sibling(self):
        return dict(ctx=self.ctx(0, 0, 1))


def greet(peers):
    barrier = pltpu.get_barrier_semaphore()
    for where in peers:
        pl.semaphore_signal(
            barrier, inc=1, device_id=where, device_id_type=pl.DeviceIdType.MESH
        )
    pl.semaphore_wait(barrier, len(peers))


def layer_kernel(
    n_ctx, pages,
    pt_ref, live_ref, len_ref, floor_ref, mgain_ref, fgain_ref,
    tin_ref, tok_hbm, tout_hbm, tgu_hbm, tdn_hbm,
    out_ref,
    tok_ref, tout_ref, tgu_ref, tdn_ref,
    wq_ref, wqx_ref, wo_ref, wf_ref, pkq_ref, pkqx_ref, pkf_ref, x_ref, ord_ref,
    q_ref, k_ref, v_ref, ctot_ref, cnt_ref, st_ref, dec_ref, run_ref, mix_ref,
    msg_ref, in_ref, num_ref, nin_ref, oth_ref, via_ref, head_ref, xall_ref, ss_ref, res_ref,
    hid_ref, rs_ref, acc_ref, send_ref, rin_ref,
    *sems,
):
    (l_sem, n_ssem, n_rsem, s_sem, r_sem, p_ssem, p_rsem, g_ssem, g_rsem, a_ssem, a_rsem,
     b_ssem, b_rsem, t_ssem, t_rsem) = sems[:15]
    sq, so, sf = sems[15:27], sems[27:32], sems[32:39]
    width = 2 * PAGE
    cols, hid = width, tdn_ref.shape[1] // 4
    ctx, rep = lax.axis_index("ctx"), lax.axis_index("rep")
    left, me, right, far = ring_neighbours()
    half_pages = pages // 2
    rows = half_pages * PAGE
    wl = tin_ref.shape[1]
    at = Place()
    bq = RepBulk(wq_ref, pkq_ref, wqx_ref, pkqx_ref, *sq)
    bo = Bulk(True, wo_ref, None, None, None, *so)
    bf = Bulk(True, wf_ref, pkf_ref, *sf)
    loads = [
        pltpu.make_async_copy(a, b, l_sem.at[k])
        for k, (a, b) in enumerate(
            [(tgu_hbm, tgu_ref), (tdn_hbm, tdn_ref), (tout_hbm, tout_ref), (tok_hbm, tok_ref)]
        )
    ]
    for load in loads:
        load.start()

    for y in range(4):
        for t in range(3):
            lane = pl.multiple_of((y * 2 + rep) * cols, cols)
            pkq_ref[y, :, pl.ds(t * cols, cols)] = tin_ref[t, :, pl.ds(lane, cols)].astype(BF16)
            lane = pl.multiple_of((y * 2 + 1 - rep) * cols, cols)
            pkqx_ref[y, :, pl.ds(t * cols, cols)] = tin_ref[
                t, pl.ds(wl // 2, wl // 2), pl.ds(lane, cols)
            ].astype(BF16)
    wq_ref[ctx, me] = pkq_ref[me]
    wqx_ref[at.z, me] = pkqx_ref[me]

    greet(
        [at.sibling(), at.same(), at.cross()]
        + [dict(ctx=at.ctx(0, dz)) for dz in (1, 2, 3)]
        + [dict(mp=left), dict(mp=right), dict(mp=far)]
    )
    bq.y_start((1, 2))
    bq.z_start(0)

    row8 = lax.broadcasted_iota(jnp.int32, (pages, PAGE), 0)
    lane8 = lax.broadcasted_iota(jnp.int32, (pages, PAGE), 1)
    upto = jnp.zeros((pages, PAGE), jnp.int32)
    alive = jnp.zeros((pages, PAGE), F32)
    so_far = jnp.int32(0)
    for b in range(pages):
        flag = live_ref[b]
        upto = jnp.where(row8 == b, so_far * PAGE + flag * (lane8 + 1), upto)
        alive = jnp.where(row8 == b, flag.astype(F32), alive)
        so_far = so_far + flag
    def num_copy(k):
        to = at.sibling() if k == 0 else at.same() if k == 4 else dict(ctx=at.ctx(0, k))
        src = num_ref.at[0 if k == 0 else 2 if k == 4 else 1]
        return remote(src, nin_ref.at[k], n_ssem, n_rsem.at[(k + 2) // 3], **to)

    num_ref[0] = jnp.zeros((pages, PAGE), jnp.int32) + so_far * PAGE
    num_copy(0).start()

    for load in loads[:3]:
        load.wait()
    wo_ref[ctx, 0] = tout_ref[...].astype(BF16)
    for y in range(4):
        for j in range(hid // PAGE):
            for t in range(2):
                pkf_ref[y, :, pl.ds(j * 2 * PAGE + t * PAGE, PAGE)] = tgu_ref[
                    t, :, pl.ds(y * hid + j * PAGE, PAGE)
                ].astype(BF16)
        pkf_ref[y, :, pl.ds(2 * hid, hid)] = tdn_ref[:, pl.ds(y * hid, hid)].astype(BF16)
    wf_ref[ctx, me] = pkf_ref[me]
    bf.x_go(0, 0)
    bo.x_go(0, 0)
    loads[3].wait()

    def norm(b):
        x = tok_ref[pt_ref[b]].astype(F32)
        scale = lax.rsqrt(jnp.mean(x * x, axis=-1, keepdims=True) + EPS)
        x_ref[pl.ds(b * PAGE, PAGE), :] = (x * scale * mgain_ref[...]).astype(BF16)

    lane1 = lax.broadcasted_iota(jnp.int32, (1, PAGE), 1) // wl

    def my_columns(read, t):
        tile = None
        for k in range(4):
            turned = pltpu.roll(read(t * 4 + k), lax.rem(wl * (k + 4) - wl * me, PAGE), 1)
            tile = turned if tile is None else jnp.where(lane1 == k, turned, tile)
        return tile

    def pick(j):
        page = pt_ref[rep * half_pages + j]
        for t in range(4):
            tile = my_columns(
                lambda c: tok_ref[page, :, pl.ds(c * PAGE, PAGE)].astype(F32), t
            )
            ord_ref[pl.ds(j * PAGE, PAGE), pl.ds(t * PAGE, PAGE)] = tile

    def project_first(part):
        near = pl.ds(pl.multiple_of(at.x * (D // 2), D // 2), D // 2)
        w = wq_ref[pl.ds(at.x * (n_ctx // 2), n_ctx // 2)].reshape(D // 2, 3 * width)
        x = x_ref[pl.ds(part * rows, rows), near]
        for t in range(3):
            acc_ref[part * 3 + t] = dot(x, w[:, t * width : (t + 1) * width])

    norm(0)
    norm(1)
    norm(2)
    bq.y_start((3,))
    bq.y_take(1)
    bq.z_start(1)
    bq.y_take(2)
    bq.z_start(2)
    num_copy(0).wait_recv()
    num_ref[1] = num_ref[0] + nin_ref[0]
    for k in (1, 2, 3):
        num_copy(k).start()
    norm(3)
    norm(4)
    bq.y_take(3)
    bq.z_start(3)
    bf.y_start((1, 2))
    bq.z_relay(0)
    bf.y_start((3,))
    norm(5)
    bq.x_take(0, 0)
    bq.z_relay(1)
    bq.z_relay(2)
    norm(6)
    bq.x_take(1, 0)
    norm(7)
    bq.x_take(2, 0)
    bq.z_relay(3)
    bo.z_start(0)
    bq.x_take(0, 1)
    bq.x_take(0, 2)
    bq.x_take(3, 0)
    there = nin_ref.at[pl.ds(1, 3)]
    remote(there, there, n_ssem, n_rsem.at[1], **at.sibling()).wait_recv()
    num_ref[2] = num_ref[1] + nin_ref[1] + nin_ref[2] + nin_ref[3]
    num_copy(4).start()
    bq.z_far(0)
    bq.x_take(1, 1)
    bq.x_take(1, 2)
    bq.z_far(1)
    bq.x_take(2, 1)
    bq.x_take(2, 2)
    bq.z_far(2)
    bq.x_take(3, 1)
    bq.x_take(3, 2)
    bq.x_take(0, 3)
    bq.z_far(3)
    bq.x_take(1, 3)
    bo.x_take(0, 0)
    bo.z_start(0, 1)
    bf.y_take(1)
    bf.z_start(1)
    bf.y_take(2)
    bq.c_take(0)
    project_first(0)
    bq.x_take(2, 3)
    bq.x_take(3, 3)
    project_first(1)
    num_copy(4).wait_recv()
    base = jnp.where(at.core == 1, nin_ref[0], 0) + jnp.where(at.x == 1, nin_ref[4], 0)
    for k in (1, 2, 3):
        base = base + jnp.where(k <= at.z, nin_ref[k], 0)
    count = jnp.zeros((pages, PAGE), F32)
    start = jnp.int32(0)
    for j in range(len_ref.shape[0]):
        count = count + jnp.where((base <= start) & (start < base + upto), 1.0, 0.0)
        start = start + len_ref[j]
    cnt_ref[pl.ds(0, 1), :] = jnp.zeros((1, PAGE), F32)
    for b in range(pages):
        cnt_ref[pl.ds(b + 1, 1), :] = count[b : b + 1, :]
    run_ref[...] = jnp.zeros_like(run_ref)
    dec_ref[...] = jnp.ones_like(dec_ref)
    row = lax.broadcasted_iota(jnp.int32, (PAGE, PAGE), 0)
    col = lax.broadcasted_iota(jnp.int32, (PAGE, PAGE), 1)
    lower = row >= col
    tri = jnp.where(lower, 1.0, 0.0).astype(BF16)
    tri = jnp.concatenate([tri, tri], axis=1)
    floor = floor_ref[...]
    bq.c_take(1)
    bf.x_take(0, 0)
    bf.flush(True)
    bo.flush(True)
    for i in (1, 2):
        bf.x_go(i, 0)

    def wide(b):
        return jnp.broadcast_to(cnt_ref[pl.ds(b + 1, 1), :], (PAGE, PAGE))

    def ends(b):
        return cnt_ref[pl.ds(b, 1), :][:, PAGE - 1 :], cnt_ref[pl.ds(b + 1, 1), :][:, PAGE - 1 :]

    def project(i):
        here2 = pl.ds(i * 256, 256)
        away = pl.ds(pl.multiple_of((1 - at.x) * (D // 2), D // 2), D // 2)
        w = wq_ref[pl.ds((1 - at.x) * (n_ctx // 2), n_ctx // 2)].reshape(D // 2, 3 * width)
        p = dot(x_ref[here2, away], w)
        pq, pf, pv = (
            p[:, t * width : (t + 1) * width] + acc_ref[i // 2 * 3 + t, pl.ds(i % 2 * 256, 256), :]
            for t in range(3)
        )
        q = pq / (1.0 + jnp.exp(-pq))
        forget = floor + (1.0 - floor) / (1.0 + jnp.exp(-pf))
        logd, key = jnp.log(forget), 1.0 - forget
        v_ref[here2, :] = pv.astype(BF16)
        for h2 in range(2):
            b = 2 * i + h2
            part = slice(h2 * PAGE, (h2 + 1) * PAGE)
            here = pl.ds(b * PAGE, PAGE)
            live = alive[b : b + 1, :]
            live = jnp.concatenate([live, live], axis=1)
            lg, kk = logd[part] * live, key[part] * live
            hi = lg.astype(BF16)
            lo = (lg - hi.astype(F32)).astype(BF16)
            c = dot(tri, jnp.concatenate([hi, lo], axis=0))
            final = c[PAGE - 1 :, :]
            before, last = ends(b)
            keep = jnp.where(wide(b).T == last, 1.0, 0.0)
            keep = jnp.concatenate([keep, keep], axis=1)
            same = jnp.where(before == last, 1.0, 0.0)
            decay = jnp.exp(final) * same
            q_ref[here, :] = (q[part] * jnp.exp(c)).astype(BF16)
            k_ref[here, :] = (kk * jnp.exp(-c)).astype(BF16)
            ke = (kk * jnp.exp(final - c) * keep).astype(BF16)
            dec = dec_ref[...]
            ctot_ref[pl.ds(b, 1), :] = dec
            dec_ref[...] = dec * decay
            for h in range(2):
                lanes = slice(h * PAGE, (h + 1) * PAGE)
                state = run_ref[h]
                st_ref[b, h] = state
                add = dot(v_ref[here, lanes], ke[:, lanes], TN)
                run_ref[h] = state * decay[:, lanes] + add

    def block_in(ref):
        tail = ref[pl.ds(PAGE, 16), :].astype(F32)
        return ref[pl.ds(0, PAGE), :].astype(F32), tail[0:1, :] + tail[1:2, :]

    def block_out(ref, block):
        state, decay = block
        ref[pl.ds(0, PAGE), :] = state.astype(BF16)
        hi = decay.astype(BF16)
        lo = (decay - hi.astype(F32)).astype(BF16)
        line = lax.broadcasted_iota(jnp.int32, (16, PAGE), 0)
        both = jnp.where(line == 0, hi.astype(F32), jnp.where(line == 1, lo.astype(F32), 0.0))
        ref[pl.ds(PAGE, 16), :] = both.astype(BF16)

    def join(early, late):
        return early[0] * late[1] + late[0], early[1] * late[1]

    def choose(flag, a, b):
        return jnp.where(flag, a[0], b[0]), jnp.where(flag, a[1], b[1])

    def state_copy(k):
        to = at.sibling() if k in (0, 5) else at.same() if k == 4 else dict(ctx=at.ctx(0, k))
        src = msg_ref.at[{0: 0, 4: 2, 5: 3}.get(k, 1)]
        return remote(src, in_ref.at[k], s_sem, r_sem.at[(0, 1, 1, 1, 2, 3)[k]], **to)

    def local_block(h):
        return run_ref[h], dec_ref[:, pl.ds(pl.multiple_of(h * PAGE, PAGE), PAGE)]

    project(0)
    project(1)
    project(2)
    bf.y_take(3)
    bf.x_go(3, 0)
    project(3)
    block_out(msg_ref.at[0], local_block(1 - at.core))
    state_copy(0).start()

    def within(b, _):
        here = pl.ds(pl.multiple_of(b * PAGE, PAGE), PAGE)
        rowwise = wide(b)
        allowed = lower & (rowwise.T == rowwise)
        for h in range(2):
            lanes = slice(h * PAGE, (h + 1) * PAGE)
            scores = dot(q_ref[here, lanes], k_ref[here, lanes], NT)
            scores = jnp.where(allowed, scores, 0.0).astype(BF16)
            mix_ref[here, lanes] = dot(scores, v_ref[here, lanes])
        return 0

    lax.fori_loop(0, 2, within, 0)
    state_copy(0).wait_recv()
    own, sib = local_block(at.core), block_in(in_ref.at[0])
    first, second = choose(at.core == 0, own, sib), choose(at.core == 0, sib, own)
    chip = join(first, second)
    block_out(msg_ref.at[1], chip)
    for k in (1, 2, 3):
        state_copy(k).start()
    bf.z_start(2)
    bf.z_start(3)
    lax.fori_loop(2, pages, within, 0)
    there = in_ref.at[pl.ds(1, 3)]
    remote(there, there, s_sem, r_sem.at[1], **at.sibling()).wait_recv()
    whole = (jnp.zeros((PAGE, PAGE), F32), jnp.ones((1, PAGE), F32))
    ahead = whole
    for z in range(at.n_z):
        there = block_in(msg_ref.at[1])
        for k in (1, 2, 3):
            there = choose(lax.rem(at.z + at.n_z - z, at.n_z) == k, block_in(in_ref.at[k]), there)
        whole = join(whole, there)
        ahead = choose(z < at.z, whole, ahead)
    block_out(msg_ref.at[2], whole)
    state_copy(4).start()
    bf.z_relay(1)
    bo.z_relay(0)
    bo.z_relay(0, 1)
    bf.x_go(1, 1)
    for j in range(half_pages):
        pick(j)
    state_copy(4).wait_recv()
    before = choose(at.x == 1, block_in(in_ref.at[4]), (jnp.zeros((PAGE, PAGE), F32), jnp.ones((1, PAGE), F32)))
    enter0 = join(before, ahead)
    enter1 = join(enter0, first)
    block_out(msg_ref.at[3], choose(at.core == 0, enter1, enter0))
    state_copy(5).start()
    run_ref[at.core] = choose(at.core == 0, enter0, enter1)[0]
    state_copy(5).wait_recv()
    run_ref[1 - at.core] = block_in(in_ref.at[5])[0]

    def outputs(b, dst, dst_row, dst_lane):
        here = pl.ds(pl.multiple_of(b * PAGE, PAGE), PAGE)
        before, _ = ends(b)
        open_rows = wide(b).T == before
        total = ctot_ref[pl.ds(b, 1), :]
        for h in range(2):
            lanes = slice(h * PAGE, (h + 1) * PAGE)
            state = st_ref[b, h] + total[:, lanes] * run_ref[h]
            old = dot(q_ref[here, lanes], state.astype(BF16), NT)
            mixed = mix_ref[here, lanes] + jnp.where(open_rows, old, 0.0)
            scale = lax.rsqrt(jnp.mean(mixed * mixed, axis=-1, keepdims=True) + EPS)
            dst[dst_row, pl.ds(dst_lane + h * PAGE, PAGE)] = (mixed * scale).astype(BF16)

    def lane_of(owner, which):
        return pl.multiple_of((owner * 2 + which) * width, width)

    def swap_out(k, n):
        to = at.same() if k == 0 else at.cross()
        return remote(
            oth_ref.at[pl.ds((2 * n + k) * PAGE, PAGE), :], via_ref.at[k, n],
            p_ssem, p_rsem.at[2 * k + n], **to,
        )

    def swap_on(k, n):
        to = at.cross() if k == 0 else at.same()
        which = rep if k == 0 else 1 - rep
        dst = head_ref.at[pl.ds((2 * n + k) * PAGE, PAGE), pl.ds(lane_of(me, which), width)]
        return remote(
            via_ref.at[k, n], dst, p_ssem, p_rsem.at[4 + n], **to
        )

    for n in range(2):
        for k in range(2):
            j = 2 * n + k
            outputs((1 - rep) * half_pages + j, oth_ref, pl.ds(j * PAGE, PAGE), 0)
            swap_out(k, n).start()
    bf.flush(False)
    bo.flush(False)
    bf.z_relay(2)
    bf.z_start(0)
    mine = lane_of(me, rep)
    part = rows // 2

    def own_half(j, _):
        outputs(rep * half_pages + j, head_ref, pl.ds(pl.multiple_of(j * PAGE, PAGE), PAGE), mine)
        return 0

    def view(which, n):
        return lambda owner, r, count: head_ref.at[
            pl.ds(n * part + r, count), pl.ds(lane_of(owner, which), width)
        ]

    three = head_ref.at[pl.ds(0, part), pl.ds(0, 3 * width)]
    ring_a = [Ring(view(rep, n), part, three, g_ssem, g_rsem, n) for n in range(2)]
    ring_b = [Ring(view(1 - rep, n), part, three, g_ssem, g_rsem, 2 + n) for n in range(2)]
    ring_x = [
        Ring(
            lambda owner, r, count, n=n: xall_ref.at[owner, pl.ds(n * part + r, count), :],
            part, xall_ref.at[pl.ds(0, 3), pl.ds(0, part), :], a_ssem, a_rsem, n,
        )
        for n in range(2)
    ]
    for n in range(2):
        lax.fori_loop(n * (half_pages // 2), (n + 1) * (half_pages // 2), own_half, 0)
        ring_a[n].start()
    for n in range(2):
        for k in range(2):
            swap_out(k, n).wait_recv()
            swap_on(k, n).start()
    bf.x_go(1, 2)
    bf.x_go(2, 1)
    bf.x_go(2, 2)
    bf.z_start(0, 1)
    ring_a[0].relay()
    remote(via_ref.at[0], via_ref.at[0], p_ssem, p_rsem.at[4], **at.sibling()).wait_recv()
    ring_b[0].start()
    ring_a[1].relay()
    remote(via_ref.at[0], via_ref.at[0], p_ssem, p_rsem.at[5], **at.sibling()).wait_recv()
    ring_b[0].relay()
    ring_b[1].start()
    bo.z_far(0)
    bo.z_far(0, 1)
    bf.z_relay(3)
    bf.z_far(1)
    bf.x_go(1, 3)
    ring_b[1].relay()
    bf.z_far(2)
    bf.x_go(2, 3)
    bf.x_go(3, 1)
    bf.x_go(3, 2)
    bo.c_take(0)
    for i in (1, 2, 3):
        bf.x_take(i, 0)
    gain = jnp.concatenate(
        [my_columns(lambda c: jnp.broadcast_to(fgain_ref[:, pl.ds(c * PAGE, PAGE)], (8, PAGE)), t)[0:1] for t in range(4)],
        axis=1,
    )

    def ss_copy(n, k, owner):
        ref = ss_ref.at[n, owner]
        to = left if k == 1 else right
        return remote(ref, ref, b_ssem.at[n], b_rsem.at[3 * n + k], mp=to)

    def out_proj(n):
        here = pl.ds(n * part, part)
        res = ord_ref[here, :] + dot(head_ref[here, :], wo_ref[...].reshape(4 * PAGE, D), NT)
        sqr = res * res
        hi = sqr.astype(BF16)
        lo = (sqr - hi.astype(F32)).astype(BF16)
        ones = jnp.ones((8, sqr.shape[1]), BF16)
        ss_ref[n, me] = dot(ones, hi, NT) + dot(ones, lo, NT)
        ss_copy(n, 0, me).start()
        ss_copy(n, 1, me).start()
        xall_ref[me, here, :] = (res * gain).astype(BF16)
        ring_x[n].start()
        for t in range(4):
            tile = res[:, t * PAGE : (t + 1) * PAGE]
            for k in range(4):
                turned = pltpu.roll(tile, lax.rem(wl * (4 - k) + wl * me, PAGE), 1)
                res_ref[here, pl.ds((t * 4 + k) * PAGE, PAGE)] = jnp.where(lane1 == me, turned, 0.0)

    def x_relay(n):
        ss_copy(n, 0, left).wait_recv()
        ss_copy(n, 2, left).start()
        ss_copy(n, 1, right).wait_recv()
        ring_x[n].relay()

    def x_rest(n):
        ring_x[n].near()
        ss_copy(n, 2, far).wait_recv()
        ring_x[n].finish()
        ss = ss_ref[n, 0]
        for y in range(1, 4):
            ss = ss + ss_ref[n, y]
        scale = lax.rsqrt(ss / D + EPS)[0:1, :]
        rs_ref[pl.ds(n * part, part), :] = jnp.broadcast_to(scale, (PAGE, part)).T

    for ring in (ring_a[0], ring_b[0]):
        ring.near()
        ring.finish()
    out_proj(0)
    bf.z_relay(0, 0)
    for ring in (ring_a[1], ring_b[1]):
        ring.near()
        ring.finish()
    out_proj(1)
    x_relay(0)
    bf.z_far(3)
    bf.x_go(3, 3)
    bf.z_relay(0, 1)
    bf.x_take(1, 1)
    bf.x_take(1, 2)
    bf.x_take(2, 1)
    bf.x_take(2, 2)
    x_relay(1)
    bf.z_far(0, 0)
    bf.x_take(1, 3)
    bf.x_take(2, 3)
    bf.x_take(3, 1)
    bf.x_take(3, 2)
    bf.x_take(3, 3)
    bf.z_far(0, 1)
    bq.drain()
    bo.drain()
    remote(v_ref, v_ref, p_ssem, p_rsem.at[0], **at.sibling()).wait_send()
    remote(in_ref, in_ref, s_sem, r_sem.at[0], **at.sibling()).wait_send()
    remote(nin_ref, nin_ref, n_ssem, n_rsem.at[0], **at.sibling()).wait_send()
    x_rest(0)
    for i in range(4):
        bf.c_take(i)

    def gate_up(n, first, last):
        here = pl.ds(n * part, part)
        for j in range(first, last):
            lanes = pl.ds(j * 256, 256)
            acc = None
            for y in range(4):
                term = dot(xall_ref[y, here, :], wf_ref[:, y, :, lanes].reshape(D // 4, 256))
                acc = term if acc is None else acc + term
            rs = rs_ref[here, :]
            g, u = acc[:, :PAGE] * rs, acc[:, PAGE:] * rs
            hid_ref[here, pl.ds(j * PAGE, PAGE)] = (g / (1.0 + jnp.exp(-g)) * u).astype(BF16)

    def block_of(owner):
        return pl.ds(pl.multiple_of(owner * 4 * PAGE, PAGE), 4 * PAGE)

    def partial(n, owner):
        here = pl.ds(n * part, part)
        w = wf_ref[pl.ds(owner * 4, 4), :, :, pl.ds(2 * hid, hid)].reshape(4 * PAGE, hid)
        res_ref[here, block_of(owner)] = res_ref[here, block_of(owner)] + dot(hid_ref[here, :], w, NT)

    half = part // 2

    class Reduce:
        def __init__(self, n):
            self.n = n
            self.upper, self.under = pl.ds(n * part, half), pl.ds(n * part + half, half)
            self.far_r = self.hop(0, self.upper, 0, 0, right)
            self.far_l = self.hop(0, self.under, 1, 1, left)
            self.near_r1 = self.hop(1, self.under, 2, 2, right)
            self.near_r2 = self.hop(1, self.upper, 2, 3, right)
            self.near_l1 = self.hop(2, self.upper, 3, 4, left)
            self.near_l2 = self.hop(2, self.under, 3, 5, left)

        def hop(self, slot, where, to_slot, k, to):
            return remote(
                send_ref.at[slot, where, :], rin_ref.at[to_slot, where, :],
                t_ssem.at[self.n], t_rsem.at[3 * self.n + min(k, 2)], mp=to,
            )

        def first(self):
            here = pl.ds(self.n * part, part)
            partial(self.n, far)
            send_ref[0, here, :] = res_ref[here, block_of(far)].astype(BF16)
            self.far_r.start()
            self.far_l.start()
            partial(self.n, right)
            send_ref[1, self.under, :] = res_ref[self.under, block_of(right)].astype(BF16)
            self.near_r1.start()
            partial(self.n, left)
            send_ref[2, self.upper, :] = res_ref[self.upper, block_of(left)].astype(BF16)
            self.near_l1.start()

        def second(self):
            self.far_r.wait_recv()
            send_ref[1, self.upper, :] = (
                res_ref[self.upper, block_of(right)] + rin_ref[0, self.upper, :].astype(F32)
            ).astype(BF16)
            self.near_r2.start()
            self.far_l.wait_recv()
            send_ref[2, self.under, :] = (
                res_ref[self.under, block_of(left)] + rin_ref[1, self.under, :].astype(F32)
            ).astype(BF16)
            self.near_l2.start()

        def last(self):
            two = rin_ref.at[pl.ds(0, 2), pl.ds(0, part), :]
            remote(two, two, t_ssem.at[self.n], t_rsem.at[3 * self.n + 2], mp=right).wait_recv()
            for p in range(half_pages // 2):
                page = self.n * (half_pages // 2) + p
                r = pl.ds(page * PAGE, PAGE)
                total = (
                    res_ref[r, block_of(me)] + rin_ref[2, r, :].astype(F32)
                    + rin_ref[3, r, :].astype(F32)
                )
                out_ref[r, :] = jnp.where(
                    live_ref[rep * half_pages + page] == 1, total, 0.0
                ).astype(BF16)

        def drain(self):
            three = send_ref.at[:, pl.ds(0, part), :]
            remote(three, three, t_ssem.at[self.n], t_rsem.at[3 * self.n], mp=right).wait_send()

    reduce = [Reduce(n) for n in range(2)]
    tiles = hid // PAGE
    gate_up(0, 0, tiles)
    reduce[0].first()
    x_rest(1)
    gate_up(1, 0, tiles // 2)
    reduce[0].second()
    gate_up(1, tiles // 2, tiles)
    reduce[1].first()
    partial(0, me)
    partial(1, me)
    reduce[1].second()
    bf.drain()
    for n in range(2):
        three = ss_ref.at[n, pl.ds(0, 3)]
        remote(three, three, b_ssem.at[n], b_rsem.at[0], mp=right).wait_send()
    reduce[0].last()
    reduce[1].last()
    for n in range(2):
        reduce[n].drain()


VM = pl.BlockSpec(memory_space=pltpu.VMEM)
HB = pl.BlockSpec(memory_space=pl.ANY)
SM = pl.BlockSpec(memory_space=pltpu.SMEM)


def shards(
    token_pages, page_table, live_flags, lengths, decay_floor, mixer_gain, feed_gain,
    trainer_mixer_in, trainer_mixer_out, trainer_gate_up, trainer_down,
):
    n_ctx = lax.axis_size("ctx")
    pages, page, _ = token_pages.shape
    tokens, half = pages * page, pages * page // 2
    wl = trainer_mixer_in.shape[1]
    cols = decay_floor.shape[0]
    hid = trainer_gate_up.shape[2] // 4
    block = D // 4
    dma = pltpu.SemaphoreType.DMA

    def bulk_sems(n, y):
        near = [dma(()), dma((3,))] if y else []
        return near + [dma(()), dma((n, 2)), dma((n, 2)), dma((n, 4)), dma((n,))]

    return pl.pallas_call(
        functools.partial(layer_kernel, n_ctx, pages),
        out_shape=jax.ShapeDtypeStruct((half, block), BF16),
        in_specs=[SM, SM, SM] + [VM] * 4 + [HB] * 4,
        out_specs=VM,
        scratch_shapes=[
            pltpu.VMEM((pages, page, D), BF16),
            pltpu.VMEM((wl, D), F32),
            pltpu.VMEM((2, wl, 4 * hid), F32),
            pltpu.VMEM((wl, 4 * hid), F32),
            pltpu.VMEM((n_ctx, 4, wl, 3 * cols), BF16),
            pltpu.VMEM((4, 4, wl // 2, 3 * cols), BF16),
            pltpu.VMEM((n_ctx, 1, wl, D), BF16),
            pltpu.VMEM((n_ctx, 4, wl, 3 * hid), BF16),
            pltpu.VMEM((4, wl, 3 * cols), BF16),
            pltpu.VMEM((4, wl // 2, 3 * cols), BF16),
            pltpu.VMEM((4, wl, 3 * hid), BF16),
            pltpu.VMEM((tokens, D), BF16),
            pltpu.VMEM((half, block), F32),
            pltpu.VMEM((tokens, cols), BF16),
            pltpu.VMEM((tokens, cols), BF16),
            pltpu.VMEM((tokens, cols), BF16),
            pltpu.VMEM((pages, cols), F32),
            pltpu.VMEM((16, PAGE), F32),
            pltpu.VMEM((pages, 2, PAGE, PAGE), F32),
            pltpu.VMEM((1, cols), F32),
            pltpu.VMEM((2, PAGE, PAGE), F32),
            pltpu.VMEM((tokens, cols), F32),
            pltpu.VMEM((4, PAGE + 16, PAGE), BF16),
            pltpu.VMEM((6, PAGE + 16, PAGE), BF16),
            pltpu.VMEM((3, pages, PAGE), jnp.int32),
            pltpu.VMEM((5, pages, PAGE), jnp.int32),
            pltpu.VMEM((half, cols), BF16),
            pltpu.VMEM((2, 2, half // 4, cols), BF16),
            pltpu.VMEM((half, D), BF16),
            pltpu.VMEM((4, half, block), BF16),
            pltpu.VMEM((2, 4, 8, half // 2), F32),
            pltpu.VMEM((half, D), F32),
            pltpu.VMEM((half, hid), BF16),
            pltpu.VMEM((half, PAGE), F32),
            pltpu.VMEM((6, half, 256), F32),
            pltpu.VMEM((3, half, block), BF16),
            pltpu.VMEM((4, half, block), BF16),
            dma((4,)), dma(()), dma((3,)), dma(()), dma((4,)),
            dma(()), dma((6,)), dma((4,)), dma((4, 3)), dma((2,)), dma((2, 3)),
            dma((2,)), dma((6,)), dma((2,)), dma((6,)),
        ]
        + [dma(()), dma((3,)), dma(()), dma((4,)), dma((4,))]
        + bulk_sems(4, True) + bulk_sems(1, False) + bulk_sems(4, True),
        compiler_params=pltpu.CompilerParams(
            collective_id=0, has_side_effects=True, vmem_limit_bytes=VMEM_LIMIT
        ),
        name="layer",
    )(
        page_table, live_flags, lengths, decay_floor.reshape(1, cols),
        mixer_gain.reshape(1, D), feed_gain.reshape(1, D),
        trainer_mixer_in, token_pages, trainer_mixer_out.T, trainer_gate_up, trainer_down.T,
    )


def solution(mesh):
    in_specs = (
        P("ctx", None, None),
        P("ctx"),
        P("ctx"),
        P(),
        P(("mp", "rep")),
        P(),
        P(),
        P(None, ("ctx", "mp"), None),
        P(None, ("ctx", "mp")),
        P(None, ("ctx", "mp"), None),
        P(None, ("ctx", "mp")),
    )
    out_specs = P(("ctx", "rep"), "mp")
    return jax.shard_map(shards, mesh=mesh, in_specs=in_specs, out_specs=out_specs, check_vma=False)
```

```python
import functools

import jax
import jax.numpy as jnp
from jax import lax
from jax.experimental import pallas as pl
from jax.experimental.pallas import tpu as pltpu
from jax.sharding import PartitionSpec as P

D = 2048
HEADS = 16
PAGE = 128
EPS = 1e-05
VMEM_LIMIT = 67043328
NT = (((1,), (1,)), ((), ()))
TN = (((0,), (0,)), ((), ()))
F32 = jnp.float32
BF16 = jnp.bfloat16


def remote(src, dst, ssem, rsem, **where):
    return pltpu.make_async_remote_copy(
        src_ref=src,
        dst_ref=dst,
        send_sem=ssem,
        recv_sem=rsem,
        device_id=where,
        device_id_type=pl.DeviceIdType.MESH,
    )


def dot(a, b, dims=None):
    if dims is None:
        return jnp.dot(a, b, preferred_element_type=F32)
    return lax.dot_general(a, b, dims, preferred_element_type=F32)


def ring_neighbours():
    mp = lax.axis_size("mp")
    me = lax.axis_index("mp")
    return lax.rem(me + mp - 1, mp), me, lax.rem(me + 1, mp), lax.rem(me + 2, mp)


class Ring:
    def __init__(self, view, rows, whole, ssem, rsem, n):
        self.view, self.half, self.whole = view, rows // 2, whole
        self.ssem, self.rsem, self.n = ssem, rsem, n

    def copy(self, owner, part, k):
        left, _, right, _ = ring_neighbours()
        ref = self.view(owner, part * self.half, self.half)
        return remote(
            ref, ref, self.ssem.at[self.n], self.rsem.at[self.n, k // 2],
            mp=right if k % 2 == 0 else left,
        )

    def take(self, stage):
        left, _, right, _ = ring_neighbours()
        ref = self.view(0, 0, 2 * self.half)
        remote(ref, ref, self.ssem.at[self.n], self.rsem.at[self.n, stage], mp=right).wait_recv()

    def start(self):
        _, me, _, _ = ring_neighbours()
        for k, part in enumerate((0, 1, 1, 0)):
            self.copy(me, part, k).start()

    def relay(self):
        left, _, right, _ = ring_neighbours()
        self.take(0)
        self.copy(left, 0, 4).start()
        self.copy(right, 1, 5).start()

    def near(self):
        self.take(1)

    def finish(self):
        _, _, right, _ = ring_neighbours()
        self.take(2)
        remote(
            self.whole, self.whole, self.ssem.at[self.n], self.rsem.at[self.n, 2], mp=right
        ).wait_send()


class Bulk:
    def __init__(self, hold, w, pack, ysend, yrecv, send, near, far, xrecv, crecv):
        self.w, self.pack = w, pack
        self.ys, self.yr, self.send, self.zn, self.zf = ysend, yrecv, send, near, far
        self.xr, self.cr = xrecv, crecv
        self.pending, self.hold = [], hold
        self.at = Place()
        self.mp, self.me = lax.axis_size("mp"), lax.axis_index("mp")
        self.rows = w.shape[2]
        self.top, self.bottom = pl.ds(0, self.rows // 2), pl.ds(self.rows // 2, self.rows // 2)
        self.all = pl.ds(0, self.rows)

    def span(self, n):
        if self.w.shape[1] == 1:
            return self.w.at[pl.ds(0, n)]
        return self.w.at[0, pl.ds(0, n)] if n < 4 else self.w.at[pl.ds(0, n // 4)]

    def wait_in(self, ref, sem):
        remote(ref, ref, self.send, sem, **self.at.sibling()).wait_recv()

    def wait_out(self, ref, sem):
        remote(ref, ref, sem, self.cr.at[0], **self.at.sibling()).wait_send()

    def owner(self, i):
        return lax.rem(self.me + self.mp - (0, 1, 3, 2)[i], self.mp) if self.pack is not None else 0

    def piece(self, i, rows, xr=0, zr=0, other=0):
        return self.w.at[self.at.ctx(xr, (0, -1, 1, 2)[zr], other), self.owner(i), rows, :]

    def go(self, copy):
        copy.start()

    def y_copy(self, i):
        d = (0, 1, 3, 2)[i]
        to = lax.rem(self.me + d, self.mp)
        return remote(
            self.pack.at[to], self.w.at[self.at.ctx(), self.me], self.ys, self.yr.at[i - 1], mp=to,
        )

    def y_start(self, which=(1, 2, 3)):
        for i in which:
            self.go(self.y_copy(i))

    def z_copy(self, i, xr, k, zr, rows):
        ref = self.piece(i, rows, xr, zr)
        to = self.at.ctx(0, 1 if k in (0, 2) else -1)
        got = (self.zn if k < 2 else self.zf).at[i, xr]
        return remote(ref, ref, self.send, got, ctx=to)

    def x_copies(self, i, zr, xr):
        a, b = self.piece(i, self.top, xr, zr), self.piece(i, self.bottom, xr, zr)
        return [
            remote(a, a, self.send, self.xr.at[i, zr], **self.at.same()),
            remote(b, b, self.send, self.xr.at[i, zr], **self.at.cross()),
        ]

    def c_sem(self, i, xr):
        return self.cr.at[i]

    def c_copy(self, i, xr, zr):
        ref = self.piece(i, self.all, xr, zr)
        return remote(ref, ref, self.send, self.c_sem(i, xr), **self.at.sibling())

    def c_go(self, i, xr, zr):
        if self.hold:
            self.pending.append((i, xr, zr))
        else:
            self.go(self.c_copy(i, xr, zr))

    def flush(self, hold):
        for piece in self.pending:
            self.go(self.c_copy(*piece))
        self.pending, self.hold = [], hold

    def x_go(self, i, zr):
        for copy in self.x_copies(i, zr, 0):
            self.go(copy)

    def x_take(self, i, zr):
        self.wait_in(self.piece(i, self.all, 1, zr), self.xr.at[i, zr])
        self.c_go(i, 1, zr)

    def y_take(self, i):
        self.y_copy(i).wait_recv()

    def z_start(self, i, xr=0):
        self.go(self.z_copy(i, xr, 0, 0, self.all))
        self.go(self.z_copy(i, xr, 1, 0, self.all))
        if xr == 0:
            self.c_go(i, 0, 0)

    def z_relay(self, i, xr=0):
        self.wait_in(self.span(2), self.zn.at[i, xr])
        self.go(self.z_copy(i, xr, 2, 1, self.top))
        self.go(self.z_copy(i, xr, 3, 2, self.bottom))
        self.c_go(i, xr, 1)
        self.c_go(i, xr, 2)

    def z_far(self, i, xr=0):
        self.wait_in(self.piece(i, self.all, xr, 3), self.zf.at[i, xr])
        self.c_go(i, xr, 3)

    def c_take(self, i):
        self.wait_in(self.span(8), self.cr.at[i])

    def drain(self):
        if self.pack is None:
            self.wait_out(self.span(15), self.send)
        else:
            self.wait_out(self.span(60), self.send)
            self.wait_out(self.span(3), self.ys)


class RepBulk(Bulk):
    def __init__(self, w, pack, wx, packx, ysx, yrx, zsx, znx, zfx, *sems):
        super().__init__(False, w, pack, *sems)
        self.wx, self.packx = wx, packx
        self.ysx, self.yrx, self.zsx, self.znx, self.zfx = ysx, yrx, zsx, znx, zfx

    def extra(self, i, zr):
        return self.wx.at[self.at.zi((0, -1, 1, 2)[zr]), self.owner(i)]

    def yx_copy(self, i):
        to = lax.rem(self.me + (0, 1, 3, 2)[i], self.mp)
        return remote(
            self.packx.at[to], self.wx.at[self.at.zi(0), self.me], self.ysx, self.yrx.at[i - 1],
            mp=to,
        )

    def y_start(self, which=(1, 2, 3)):
        for i in which:
            self.go(self.y_copy(i))
            self.go(self.yx_copy(i))

    def y_take(self, i):
        self.y_copy(i).wait_recv()
        self.yx_copy(i).wait_recv()

    def zx_copy(self, i, k, zr):
        ref = self.extra(i, zr)
        to = self.at.ctx(0, 1 if k == 0 or (k == 2 and i % 2 == 0) else -1)
        return remote(ref, ref, self.zsx, (self.znx if k < 2 else self.zfx).at[i], ctx=to)

    def x_copies(self, i, zr, xr):
        a = self.piece(i, self.top, xr, zr)
        b = self.extra(i, zr)
        dst = self.piece(i, self.bottom, xr, zr)
        return [
            remote(a, a, self.send, self.xr.at[i, zr], **self.at.same()),
            remote(b, dst, self.send, self.xr.at[i, zr], **self.at.cross()),
        ]

    def c_sem(self, i, xr):
        return self.cr.at[xr]

    def c_take(self, xr):
        self.wait_in(self.span(16), self.cr.at[xr])

    def z_start(self, i, xr=0):
        super().z_start(i)
        self.go(self.zx_copy(i, 0, 0))
        self.go(self.zx_copy(i, 1, 0))
        self.x_go(i, 0)

    def z_relay(self, i, xr=0):
        super().z_relay(i)
        self.wait_in(self.wx.at[0, pl.ds(0, 2)], self.znx.at[i])
        self.go(self.zx_copy(i, 2, 1 if i % 2 == 0 else 2))
        self.x_go(i, 1)
        self.x_go(i, 2)

    def z_far(self, i, xr=0):
        super().z_far(i)
        self.zx_copy(i, 2, 3).wait_recv()
        self.x_go(i, 3)

    def drain(self):
        super().drain()
        self.wait_out(self.wx.at[pl.ds(0, 3)], self.zsx)
        self.wait_out(self.wx.at[0, pl.ds(0, 3)], self.ysx)


class Place:
    def __init__(self):
        c = lax.axis_index("ctx")
        self.n_z = lax.axis_size("ctx") // 4
        self.core, self.z, self.x = lax.rem(c, 2), lax.rem(c // 2, self.n_z), c // (2 * self.n_z)
        self.rep = lax.axis_index("rep")

    def zi(self, dz):
        return lax.rem(self.z + dz + self.n_z, self.n_z)

    def ctx(self, xr=0, dz=0, other=0):
        x = self.x if xr == 0 else 1 - self.x
        core = self.core if other == 0 else 1 - self.core
        return x * (2 * self.n_z) + self.zi(dz) * 2 + core

    def same(self):
        return dict(ctx=self.ctx(1))

    def cross(self):
        return dict(ctx=self.ctx(1), rep=1 - self.rep)

    def sibling(self):
        return dict(ctx=self.ctx(0, 0, 1))


def greet(peers):
    barrier = pltpu.get_barrier_semaphore()
    for where in peers:
        pl.semaphore_signal(
            barrier, inc=1, device_id=where, device_id_type=pl.DeviceIdType.MESH
        )
    pl.semaphore_wait(barrier, len(peers))


def layer_kernel(
    n_ctx, pages,
    pt_ref, live_ref, len_ref, floor_hbm, mgain_hbm, fgain_hbm,
    tin_hbm, tok_hbm, tout_hbm, tgu_hbm, tdn_hbm,
    out_ref,
    tok_ref, tout_ref, tgu_ref, tdn_ref, tin_ref, floor_ref, mgain_ref, fgain_ref,
    wq_ref, wqx_ref, wo_ref, wf_ref, pkq_ref, pkqx_ref, pkf_ref, x_ref, ord_ref,
    q_ref, k_ref, v_ref, ctot_ref, cnt_ref, st_ref, dec_ref, run_ref, mix_ref,
    msg_ref, in_ref, num_ref, nin_ref, oth_ref, via_ref, head_ref, xall_ref, ss_ref, res_ref,
    hid_ref, rs_ref, acc_ref, send_ref, rin_ref,
    *sems,
):
    (l_sem, n_ssem, n_rsem, s_sem, r_sem, p_ssem, p_rsem, g_ssem, g_rsem, a_ssem, a_rsem,
     b_ssem, b_rsem, t_ssem, t_rsem) = sems[:15]
    sq, so, sf = sems[15:27], sems[27:32], sems[32:39]
    width = 2 * PAGE
    cols, hid = width, tdn_ref.shape[1] // 4
    ctx, rep = lax.axis_index("ctx"), lax.axis_index("rep")
    left, me, right, far = ring_neighbours()
    half_pages = pages // 2
    rows = half_pages * PAGE
    wl = tin_ref.shape[1]
    at = Place()
    bq = RepBulk(wq_ref, pkq_ref, wqx_ref, pkqx_ref, *sq)
    bo = Bulk(True, wo_ref, None, None, None, *so)
    bf = Bulk(True, wf_ref, pkf_ref, *sf)
    loads = [
        pltpu.make_async_copy(a, b, l_sem.at[k])
        for k, (a, b) in enumerate(
            [
                (tin_hbm, tin_ref), (tgu_hbm, tgu_ref), (tdn_hbm, tdn_ref), (tout_hbm, tout_ref),
                (mgain_hbm, mgain_ref), (floor_hbm, floor_ref), (fgain_hbm, fgain_ref),
                (tok_hbm, tok_ref),
            ]
        )
    ]
    for load in loads:
        load.start()

    greet(
        [at.sibling(), at.same(), at.cross()]
        + [dict(ctx=at.ctx(0, dz)) for dz in (1, 2, 3)]
        + [dict(mp=left), dict(mp=right), dict(mp=far)]
    )
    loads[0].wait()
    for y in range(4):
        for t in range(3):
            lane = pl.multiple_of((y * 2 + rep) * cols, cols)
            pkq_ref[y, :, pl.ds(t * cols, cols)] = tin_ref[t, :, pl.ds(lane, cols)].astype(BF16)
            lane = pl.multiple_of((y * 2 + 1 - rep) * cols, cols)
            pkqx_ref[y, :, pl.ds(t * cols, cols)] = tin_ref[
                t, pl.ds(wl // 2, wl // 2), pl.ds(lane, cols)
            ].astype(BF16)
    wq_ref[ctx, me] = pkq_ref[me]
    wqx_ref[at.z, me] = pkqx_ref[me]

    bq.y_start((1, 2))
    bq.z_start(0)

    row8 = lax.broadcasted_iota(jnp.int32, (pages, PAGE), 0)
    lane8 = lax.broadcasted_iota(jnp.int32, (pages, PAGE), 1)
    upto = jnp.zeros((pages, PAGE), jnp.int32)
    alive = jnp.zeros((pages, PAGE), F32)
    so_far = jnp.int32(0)
    for b in range(pages):
        flag = live_ref[b]
        upto = jnp.where(row8 == b, so_far * PAGE + flag * (lane8 + 1), upto)
        alive = jnp.where(row8 == b, flag.astype(F32), alive)
        so_far = so_far + flag
    def num_copy(k):
        to = at.sibling() if k == 0 else at.same() if k == 4 else dict(ctx=at.ctx(0, k))
        src = num_ref.at[0 if k == 0 else 2 if k == 4 else 1]
        return remote(src, nin_ref.at[k], n_ssem, n_rsem.at[(k + 2) // 3], **to)

    num_ref[0] = jnp.zeros((pages, PAGE), jnp.int32) + so_far * PAGE
    num_copy(0).start()

    for load in loads[1:4]:
        load.wait()
    wo_ref[ctx, 0] = tout_ref[...].astype(BF16)
    for y in range(4):
        for j in range(hid // PAGE):
            for t in range(2):
                pkf_ref[y, :, pl.ds(j * 2 * PAGE + t * PAGE, PAGE)] = tgu_ref[
                    t, :, pl.ds(y * hid + j * PAGE, PAGE)
                ].astype(BF16)
        pkf_ref[y, :, pl.ds(2 * hid, hid)] = tdn_ref[:, pl.ds(y * hid, hid)].astype(BF16)
    wf_ref[ctx, me] = pkf_ref[me]
    bf.x_go(0, 0)
    bo.x_go(0, 0)
    for load in loads[4:]:
        load.wait()

    def norm(b):
        x = tok_ref[pt_ref[b]].astype(F32)
        scale = lax.rsqrt(jnp.mean(x * x, axis=-1, keepdims=True) + EPS)
        x_ref[pl.ds(b * PAGE, PAGE), :] = (x * scale * mgain_ref[...]).astype(BF16)

    lane1 = lax.broadcasted_iota(jnp.int32, (1, PAGE), 1) // wl

    def my_columns(read, t):
        tile = None
        for k in range(4):
            turned = pltpu.roll(read(t * 4 + k), lax.rem(wl * (k + 4) - wl * me, PAGE), 1)
            tile = turned if tile is None else jnp.where(lane1 == k, turned, tile)
        return tile

    def pick(j):
        page = pt_ref[rep * half_pages + j]
        for t in range(4):
            tile = my_columns(
                lambda c: tok_ref[page, :, pl.ds(c * PAGE, PAGE)].astype(F32), t
            )
            ord_ref[pl.ds(j * PAGE, PAGE), pl.ds(t * PAGE, PAGE)] = tile

    def project_first(part):
        near = pl.ds(pl.multiple_of(at.x * (D // 2), D // 2), D // 2)
        w = wq_ref[pl.ds(at.x * (n_ctx // 2), n_ctx // 2)].reshape(D // 2, 3 * width)
        x = x_ref[pl.ds(part * rows, rows), near]
        for t in range(3):
            acc_ref[part * 3 + t] = dot(x, w[:, t * width : (t + 1) * width])

    norm(0)
    norm(1)
    norm(2)
    bq.y_start((3,))
    bq.y_take(1)
    bq.z_start(1)
    bq.y_take(2)
    bq.z_start(2)
    num_copy(0).wait_recv()
    num_ref[1] = num_ref[0] + nin_ref[0]
    for k in (1, 2, 3):
        num_copy(k).start()
    norm(3)
    norm(4)
    bq.y_take(3)
    bq.z_start(3)
    bf.y_start((1, 2))
    bq.z_relay(0)
    bf.y_start((3,))
    norm(5)
    bq.x_take(0, 0)
    bq.z_relay(1)
    bq.z_relay(2)
    norm(6)
    bq.x_take(1, 0)
    norm(7)
    bq.x_take(2, 0)
    bq.z_relay(3)
    bo.z_start(0)
    bq.x_take(0, 1)
    bq.x_take(0, 2)
    bq.x_take(3, 0)
    there = nin_ref.at[pl.ds(1, 3)]
    remote(there, there, n_ssem, n_rsem.at[1], **at.sibling()).wait_recv()
    num_ref[2] = num_ref[1] + nin_ref[1] + nin_ref[2] + nin_ref[3]
    num_copy(4).start()
    bq.z_far(0)
    bq.x_take(1, 1)
    bq.x_take(1, 2)
    bq.z_far(1)
    bq.x_take(2, 1)
    bq.x_take(2, 2)
    bq.z_far(2)
    bq.x_take(3, 1)
    bq.x_take(3, 2)
    bq.x_take(0, 3)
    bq.z_far(3)
    bq.x_take(1, 3)
    bo.x_take(0, 0)
    bo.z_start(0, 1)
    bf.y_take(1)
    bf.z_start(1)
    bf.y_take(2)
    bq.c_take(0)
    project_first(0)
    bq.x_take(2, 3)
    bq.x_take(3, 3)
    project_first(1)
    num_copy(4).wait_recv()
    base = jnp.where(at.core == 1, nin_ref[0], 0) + jnp.where(at.x == 1, nin_ref[4], 0)
    for k in (1, 2, 3):
        base = base + jnp.where(k <= at.z, nin_ref[k], 0)
    count = jnp.zeros((pages, PAGE), F32)
    start = jnp.int32(0)
    for j in range(len_ref.shape[0]):
        count = count + jnp.where((base <= start) & (start < base + upto), 1.0, 0.0)
        start = start + len_ref[j]
    cnt_ref[pl.ds(0, 1), :] = jnp.zeros((1, PAGE), F32)
    for b in range(pages):
        cnt_ref[pl.ds(b + 1, 1), :] = count[b : b + 1, :]
    run_ref[...] = jnp.zeros_like(run_ref)
    dec_ref[...] = jnp.ones_like(dec_ref)
    row = lax.broadcasted_iota(jnp.int32, (PAGE, PAGE), 0)
    col = lax.broadcasted_iota(jnp.int32, (PAGE, PAGE), 1)
    lower = row >= col
    tri = jnp.where(lower, 1.0, 0.0).astype(BF16)
    tri = jnp.concatenate([tri, tri], axis=1)
    floor = floor_ref[...]
    bq.c_take(1)
    bf.x_take(0, 0)
    bf.flush(True)
    bo.flush(True)
    for i in (1, 2):
        bf.x_go(i, 0)

    def wide(b):
        return jnp.broadcast_to(cnt_ref[pl.ds(b + 1, 1), :], (PAGE, PAGE))

    def ends(b):
        return cnt_ref[pl.ds(b, 1), :][:, PAGE - 1 :], cnt_ref[pl.ds(b + 1, 1), :][:, PAGE - 1 :]

    def project(i):
        here2 = pl.ds(i * 256, 256)
        away = pl.ds(pl.multiple_of((1 - at.x) * (D // 2), D // 2), D // 2)
        w = wq_ref[pl.ds((1 - at.x) * (n_ctx // 2), n_ctx // 2)].reshape(D // 2, 3 * width)
        p = dot(x_ref[here2, away], w)
        pq, pf, pv = (
            p[:, t * width : (t + 1) * width] + acc_ref[i // 2 * 3 + t, pl.ds(i % 2 * 256, 256), :]
            for t in range(3)
        )
        q = pq / (1.0 + jnp.exp(-pq))
        forget = floor + (1.0 - floor) / (1.0 + jnp.exp(-pf))
        logd, key = jnp.log(forget), 1.0 - forget
        v_ref[here2, :] = pv.astype(BF16)
        for h2 in range(2):
            b = 2 * i + h2
            part = slice(h2 * PAGE, (h2 + 1) * PAGE)
            here = pl.ds(b * PAGE, PAGE)
            live = alive[b : b + 1, :]
            live = jnp.concatenate([live, live], axis=1)
            lg, kk = logd[part] * live, key[part] * live
            hi = lg.astype(BF16)
            lo = (lg - hi.astype(F32)).astype(BF16)
            c = dot(tri, jnp.concatenate([hi, lo], axis=0))
            final = c[PAGE - 1 :, :]
            before, last = ends(b)
            keep = jnp.where(wide(b).T == last, 1.0, 0.0)
            keep = jnp.concatenate([keep, keep], axis=1)
            same = jnp.where(before == last, 1.0, 0.0)
            decay = jnp.exp(final) * same
            q_ref[here, :] = (q[part] * jnp.exp(c)).astype(BF16)
            k_ref[here, :] = (kk * jnp.exp(-c)).astype(BF16)
            ke = (kk * jnp.exp(final - c) * keep).astype(BF16)
            dec = dec_ref[...]
            ctot_ref[pl.ds(b, 1), :] = dec
            dec_ref[...] = dec * decay
            for h in range(2):
                lanes = slice(h * PAGE, (h + 1) * PAGE)
                state = run_ref[h]
                st_ref[b, h] = state
                add = dot(v_ref[here, lanes], ke[:, lanes], TN)
                run_ref[h] = state * decay[:, lanes] + add

    def block_in(ref):
        tail = ref[pl.ds(PAGE, 16), :].astype(F32)
        return ref[pl.ds(0, PAGE), :].astype(F32), tail[0:1, :] + tail[1:2, :]

    def block_out(ref, block):
        state, decay = block
        ref[pl.ds(0, PAGE), :] = state.astype(BF16)
        hi = decay.astype(BF16)
        lo = (decay - hi.astype(F32)).astype(BF16)
        line = lax.broadcasted_iota(jnp.int32, (16, PAGE), 0)
        both = jnp.where(line == 0, hi.astype(F32), jnp.where(line == 1, lo.astype(F32), 0.0))
        ref[pl.ds(PAGE, 16), :] = both.astype(BF16)

    def join(early, late):
        return early[0] * late[1] + late[0], early[1] * late[1]

    def choose(flag, a, b):
        return jnp.where(flag, a[0], b[0]), jnp.where(flag, a[1], b[1])

    def state_copy(k):
        to = at.sibling() if k in (0, 5) else at.same() if k == 4 else dict(ctx=at.ctx(0, k))
        src = msg_ref.at[{0: 0, 4: 2, 5: 3}.get(k, 1)]
        return remote(src, in_ref.at[k], s_sem, r_sem.at[(0, 1, 1, 1, 2, 3)[k]], **to)

    def local_block(h):
        return run_ref[h], dec_ref[:, pl.ds(pl.multiple_of(h * PAGE, PAGE), PAGE)]

    project(0)
    project(1)
    project(2)
    bf.y_take(3)
    bf.x_go(3, 0)
    project(3)
    block_out(msg_ref.at[0], local_block(1 - at.core))
    state_copy(0).start()

    def within(b, _):
        here = pl.ds(pl.multiple_of(b * PAGE, PAGE), PAGE)
        rowwise = wide(b)
        allowed = lower & (rowwise.T == rowwise)
        for h in range(2):
            lanes = slice(h * PAGE, (h + 1) * PAGE)
            scores = dot(q_ref[here, lanes], k_ref[here, lanes], NT)
            scores = jnp.where(allowed, scores, 0.0).astype(BF16)
            mix_ref[here, lanes] = dot(scores, v_ref[here, lanes])
        return 0

    lax.fori_loop(0, 2, within, 0)
    state_copy(0).wait_recv()
    own, sib = local_block(at.core), block_in(in_ref.at[0])
    first, second = choose(at.core == 0, own, sib), choose(at.core == 0, sib, own)
    chip = join(first, second)
    block_out(msg_ref.at[1], chip)
    for k in (1, 2, 3):
        state_copy(k).start()
    bf.z_start(2)
    bf.z_start(3)
    lax.fori_loop(2, pages, within, 0)
    there = in_ref.at[pl.ds(1, 3)]
    remote(there, there, s_sem, r_sem.at[1], **at.sibling()).wait_recv()
    whole = (jnp.zeros((PAGE, PAGE), F32), jnp.ones((1, PAGE), F32))
    ahead = whole
    for z in range(at.n_z):
        there = block_in(msg_ref.at[1])
        for k in (1, 2, 3):
            there = choose(lax.rem(at.z + at.n_z - z, at.n_z) == k, block_in(in_ref.at[k]), there)
        whole = join(whole, there)
        ahead = choose(z < at.z, whole, ahead)
    block_out(msg_ref.at[2], whole)
    state_copy(4).start()
    bf.z_relay(1)
    bo.z_relay(0)
    bo.z_relay(0, 1)
    bf.x_go(1, 1)
    for j in range(half_pages):
        pick(j)
    state_copy(4).wait_recv()
    before = choose(at.x == 1, block_in(in_ref.at[4]), (jnp.zeros((PAGE, PAGE), F32), jnp.ones((1, PAGE), F32)))
    enter0 = join(before, ahead)
    enter1 = join(enter0, first)
    block_out(msg_ref.at[3], choose(at.core == 0, enter1, enter0))
    state_copy(5).start()
    run_ref[at.core] = choose(at.core == 0, enter0, enter1)[0]
    state_copy(5).wait_recv()
    run_ref[1 - at.core] = block_in(in_ref.at[5])[0]

    def outputs(b, dst, dst_row, dst_lane):
        here = pl.ds(pl.multiple_of(b * PAGE, PAGE), PAGE)
        before, _ = ends(b)
        open_rows = wide(b).T == before
        total = ctot_ref[pl.ds(b, 1), :]
        for h in range(2):
            lanes = slice(h * PAGE, (h + 1) * PAGE)
            state = st_ref[b, h] + total[:, lanes] * run_ref[h]
            old = dot(q_ref[here, lanes], state.astype(BF16), NT)
            mixed = mix_ref[here, lanes] + jnp.where(open_rows, old, 0.0)
            scale = lax.rsqrt(jnp.mean(mixed * mixed, axis=-1, keepdims=True) + EPS)
            dst[dst_row, pl.ds(dst_lane + h * PAGE, PAGE)] = (mixed * scale).astype(BF16)

    def lane_of(owner, which):
        return pl.multiple_of((owner * 2 + which) * width, width)

    def swap_out(k, n):
        to = at.same() if k == 0 else at.cross()
        return remote(
            oth_ref.at[pl.ds((2 * n + k) * PAGE, PAGE), :], via_ref.at[k, n],
            p_ssem, p_rsem.at[2 * k + n], **to,
        )

    def swap_on(k, n):
        to = at.cross() if k == 0 else at.same()
        which = rep if k == 0 else 1 - rep
        dst = head_ref.at[pl.ds((2 * n + k) * PAGE, PAGE), pl.ds(lane_of(me, which), width)]
        return remote(
            via_ref.at[k, n], dst, p_ssem, p_rsem.at[4 + n], **to
        )

    for n in range(2):
        for k in range(2):
            j = 2 * n + k
            outputs((1 - rep) * half_pages + j, oth_ref, pl.ds(j * PAGE, PAGE), 0)
            swap_out(k, n).start()
    bf.flush(False)
    bo.flush(False)
    bf.z_relay(2)
    bf.z_start(0)
    mine = lane_of(me, rep)
    part = rows // 2

    def own_half(j, _):
        outputs(rep * half_pages + j, head_ref, pl.ds(pl.multiple_of(j * PAGE, PAGE), PAGE), mine)
        return 0

    def view(which, n):
        return lambda owner, r, count: head_ref.at[
            pl.ds(n * part + r, count), pl.ds(lane_of(owner, which), width)
        ]

    three = head_ref.at[pl.ds(0, part), pl.ds(0, 3 * width)]
    ring_a = [Ring(view(rep, n), part, three, g_ssem, g_rsem, n) for n in range(2)]
    ring_b = [Ring(view(1 - rep, n), part, three, g_ssem, g_rsem, 2 + n) for n in range(2)]
    ring_x = [
        Ring(
            lambda owner, r, count, n=n: xall_ref.at[owner, pl.ds(n * part + r, count), :],
            part, xall_ref.at[pl.ds(0, 3), pl.ds(0, part), :], a_ssem, a_rsem, n,
        )
        for n in range(2)
    ]
    for n in range(2):
        lax.fori_loop(n * (half_pages // 2), (n + 1) * (half_pages // 2), own_half, 0)
        ring_a[n].start()
    for n in range(2):
        for k in range(2):
            swap_out(k, n).wait_recv()
            swap_on(k, n).start()
    bf.x_go(1, 2)
    bf.x_go(2, 1)
    bf.x_go(2, 2)
    bf.z_start(0, 1)
    ring_a[0].relay()
    remote(via_ref.at[0], via_ref.at[0], p_ssem, p_rsem.at[4], **at.sibling()).wait_recv()
    ring_b[0].start()
    ring_a[1].relay()
    remote(via_ref.at[0], via_ref.at[0], p_ssem, p_rsem.at[5], **at.sibling()).wait_recv()
    ring_b[0].relay()
    ring_b[1].start()
    bo.z_far(0)
    bo.z_far(0, 1)
    bf.z_relay(3)
    bf.z_far(1)
    bf.x_go(1, 3)
    ring_b[1].relay()
    bf.z_far(2)
    bf.x_go(2, 3)
    bf.x_go(3, 1)
    bf.x_go(3, 2)
    bo.c_take(0)
    for i in (1, 2, 3):
        bf.x_take(i, 0)
    gain = jnp.concatenate(
        [my_columns(lambda c: jnp.broadcast_to(fgain_ref[:, pl.ds(c * PAGE, PAGE)], (8, PAGE)), t)[0:1] for t in range(4)],
        axis=1,
    )

    def ss_copy(n, k, owner):
        ref = ss_ref.at[n, owner]
        to = left if k == 1 else right
        return remote(ref, ref, b_ssem.at[n], b_rsem.at[3 * n + k], mp=to)

    def out_proj(n):
        here = pl.ds(n * part, part)
        res = ord_ref[here, :] + dot(head_ref[here, :], wo_ref[...].reshape(4 * PAGE, D), NT)
        sqr = res * res
        hi = sqr.astype(BF16)
        lo = (sqr - hi.astype(F32)).astype(BF16)
        ones = jnp.ones((8, sqr.shape[1]), BF16)
        ss_ref[n, me] = dot(ones, hi, NT) + dot(ones, lo, NT)
        ss_copy(n, 0, me).start()
        ss_copy(n, 1, me).start()
        xall_ref[me, here, :] = (res * gain).astype(BF16)
        ring_x[n].start()
        for t in range(4):
            tile = res[:, t * PAGE : (t + 1) * PAGE]
            for k in range(4):
                turned = pltpu.roll(tile, lax.rem(wl * (4 - k) + wl * me, PAGE), 1)
                res_ref[here, pl.ds((t * 4 + k) * PAGE, PAGE)] = jnp.where(lane1 == me, turned, 0.0)

    def x_relay(n):
        ss_copy(n, 0, left).wait_recv()
        ss_copy(n, 2, left).start()
        ss_copy(n, 1, right).wait_recv()
        ring_x[n].relay()

    def x_rest(n):
        ring_x[n].near()
        ss_copy(n, 2, far).wait_recv()
        ring_x[n].finish()
        ss = ss_ref[n, 0]
        for y in range(1, 4):
            ss = ss + ss_ref[n, y]
        scale = lax.rsqrt(ss / D + EPS)[0:1, :]
        rs_ref[pl.ds(n * part, part), :] = jnp.broadcast_to(scale, (PAGE, part)).T

    for ring in (ring_a[0], ring_b[0]):
        ring.near()
        ring.finish()
    out_proj(0)
    bf.z_relay(0, 0)
    for ring in (ring_a[1], ring_b[1]):
        ring.near()
        ring.finish()
    out_proj(1)
    x_relay(0)
    bf.z_far(3)
    bf.x_go(3, 3)
    bf.z_relay(0, 1)
    bf.x_take(1, 1)
    bf.x_take(1, 2)
    bf.x_take(2, 1)
    bf.x_take(2, 2)
    x_relay(1)
    bf.z_far(0, 0)
    bf.x_take(1, 3)
    bf.x_take(2, 3)
    bf.x_take(3, 1)
    bf.x_take(3, 2)
    bf.x_take(3, 3)
    bf.z_far(0, 1)
    bq.drain()
    bo.drain()
    remote(v_ref, v_ref, p_ssem, p_rsem.at[0], **at.sibling()).wait_send()
    remote(in_ref, in_ref, s_sem, r_sem.at[0], **at.sibling()).wait_send()
    remote(nin_ref, nin_ref, n_ssem, n_rsem.at[0], **at.sibling()).wait_send()
    x_rest(0)
    for i in range(4):
        bf.c_take(i)

    def gate_up(n, first, last):
        here = pl.ds(n * part, part)
        for j in range(first, last):
            lanes = pl.ds(j * 256, 256)
            acc = None
            for y in range(4):
                term = dot(xall_ref[y, here, :], wf_ref[:, y, :, lanes].reshape(D // 4, 256))
                acc = term if acc is None else acc + term
            rs = rs_ref[here, :]
            g, u = acc[:, :PAGE] * rs, acc[:, PAGE:] * rs
            hid_ref[here, pl.ds(j * PAGE, PAGE)] = (g / (1.0 + jnp.exp(-g)) * u).astype(BF16)

    def block_of(owner):
        return pl.ds(pl.multiple_of(owner * 4 * PAGE, PAGE), 4 * PAGE)

    def partial(n, owner):
        here = pl.ds(n * part, part)
        w = wf_ref[pl.ds(owner * 4, 4), :, :, pl.ds(2 * hid, hid)].reshape(4 * PAGE, hid)
        res_ref[here, block_of(owner)] = res_ref[here, block_of(owner)] + dot(hid_ref[here, :], w, NT)

    half = part // 2

    class Reduce:
        def __init__(self, n):
            self.n = n
            self.upper, self.under = pl.ds(n * part, half), pl.ds(n * part + half, half)
            self.far_r = self.hop(0, self.upper, 0, 0, right)
            self.far_l = self.hop(0, self.under, 1, 1, left)
            self.near_r1 = self.hop(1, self.under, 2, 2, right)
            self.near_r2 = self.hop(1, self.upper, 2, 3, right)
            self.near_l1 = self.hop(2, self.upper, 3, 4, left)
            self.near_l2 = self.hop(2, self.under, 3, 5, left)

        def hop(self, slot, where, to_slot, k, to):
            return remote(
                send_ref.at[slot, where, :], rin_ref.at[to_slot, where, :],
                t_ssem.at[self.n], t_rsem.at[3 * self.n + min(k, 2)], mp=to,
            )

        def first(self):
            here = pl.ds(self.n * part, part)
            partial(self.n, far)
            send_ref[0, here, :] = res_ref[here, block_of(far)].astype(BF16)
            self.far_r.start()
            self.far_l.start()
            partial(self.n, right)
            send_ref[1, self.under, :] = res_ref[self.under, block_of(right)].astype(BF16)
            self.near_r1.start()
            partial(self.n, left)
            send_ref[2, self.upper, :] = res_ref[self.upper, block_of(left)].astype(BF16)
            self.near_l1.start()

        def second(self):
            self.far_r.wait_recv()
            send_ref[1, self.upper, :] = (
                res_ref[self.upper, block_of(right)] + rin_ref[0, self.upper, :].astype(F32)
            ).astype(BF16)
            self.near_r2.start()
            self.far_l.wait_recv()
            send_ref[2, self.under, :] = (
                res_ref[self.under, block_of(left)] + rin_ref[1, self.under, :].astype(F32)
            ).astype(BF16)
            self.near_l2.start()

        def last(self):
            two = rin_ref.at[pl.ds(0, 2), pl.ds(0, part), :]
            remote(two, two, t_ssem.at[self.n], t_rsem.at[3 * self.n + 2], mp=right).wait_recv()
            for p in range(half_pages // 2):
                page = self.n * (half_pages // 2) + p
                r = pl.ds(page * PAGE, PAGE)
                total = (
                    res_ref[r, block_of(me)] + rin_ref[2, r, :].astype(F32)
                    + rin_ref[3, r, :].astype(F32)
                )
                out_ref[r, :] = jnp.where(
                    live_ref[rep * half_pages + page] == 1, total, 0.0
                ).astype(BF16)

        def drain(self):
            three = send_ref.at[:, pl.ds(0, part), :]
            remote(three, three, t_ssem.at[self.n], t_rsem.at[3 * self.n], mp=right).wait_send()

    reduce = [Reduce(n) for n in range(2)]
    tiles = hid // PAGE
    gate_up(0, 0, tiles)
    reduce[0].first()
    x_rest(1)
    gate_up(1, 0, tiles // 2)
    reduce[0].second()
    gate_up(1, tiles // 2, tiles)
    reduce[1].first()
    partial(0, me)
    partial(1, me)
    reduce[1].second()
    bf.drain()
    for n in range(2):
        three = ss_ref.at[n, pl.ds(0, 3)]
        remote(three, three, b_ssem.at[n], b_rsem.at[0], mp=right).wait_send()
    reduce[0].last()
    reduce[1].last()
    for n in range(2):
        reduce[n].drain()


VM = pl.BlockSpec(memory_space=pltpu.VMEM)
HB = pl.BlockSpec(memory_space=pl.ANY)
SM = pl.BlockSpec(memory_space=pltpu.SMEM)


def shards(
    token_pages, page_table, live_flags, lengths, decay_floor, mixer_gain, feed_gain,
    trainer_mixer_in, trainer_mixer_out, trainer_gate_up, trainer_down,
):
    n_ctx = lax.axis_size("ctx")
    pages, page, _ = token_pages.shape
    tokens, half = pages * page, pages * page // 2
    wl = trainer_mixer_in.shape[1]
    cols = decay_floor.shape[0]
    hid = trainer_gate_up.shape[2] // 4
    block = D // 4
    dma = pltpu.SemaphoreType.DMA

    def bulk_sems(n, y):
        near = [dma(()), dma((3,))] if y else []
        return near + [dma(()), dma((n, 2)), dma((n, 2)), dma((n, 4)), dma((n,))]

    return pl.pallas_call(
        functools.partial(layer_kernel, n_ctx, pages),
        out_shape=jax.ShapeDtypeStruct((half, block), BF16),
        in_specs=[SM, SM, SM] + [HB] * 8,
        out_specs=VM,
        scratch_shapes=[
            pltpu.VMEM((pages, page, D), BF16),
            pltpu.VMEM((wl, D), F32),
            pltpu.VMEM((2, wl, 4 * hid), F32),
            pltpu.VMEM((wl, 4 * hid), F32),
            pltpu.VMEM((3, wl, D), F32),
            pltpu.VMEM((1, cols), F32),
            pltpu.VMEM((1, D), F32),
            pltpu.VMEM((1, D), F32),
            pltpu.VMEM((n_ctx, 4, wl, 3 * cols), BF16),
            pltpu.VMEM((4, 4, wl // 2, 3 * cols), BF16),
            pltpu.VMEM((n_ctx, 1, wl, D), BF16),
            pltpu.VMEM((n_ctx, 4, wl, 3 * hid), BF16),
            pltpu.VMEM((4, wl, 3 * cols), BF16),
            pltpu.VMEM((4, wl // 2, 3 * cols), BF16),
            pltpu.VMEM((4, wl, 3 * hid), BF16),
            pltpu.VMEM((tokens, D), BF16),
            pltpu.VMEM((half, block), F32),
            pltpu.VMEM((tokens, cols), BF16),
            pltpu.VMEM((tokens, cols), BF16),
            pltpu.VMEM((tokens, cols), BF16),
            pltpu.VMEM((pages, cols), F32),
            pltpu.VMEM((16, PAGE), F32),
            pltpu.VMEM((pages, 2, PAGE, PAGE), F32),
            pltpu.VMEM((1, cols), F32),
            pltpu.VMEM((2, PAGE, PAGE), F32),
            pltpu.VMEM((tokens, cols), F32),
            pltpu.VMEM((4, PAGE + 16, PAGE), BF16),
            pltpu.VMEM((6, PAGE + 16, PAGE), BF16),
            pltpu.VMEM((3, pages, PAGE), jnp.int32),
            pltpu.VMEM((5, pages, PAGE), jnp.int32),
            pltpu.VMEM((half, cols), BF16),
            pltpu.VMEM((2, 2, half // 4, cols), BF16),
            pltpu.VMEM((half, D), BF16),
            pltpu.VMEM((4, half, block), BF16),
            pltpu.VMEM((2, 4, 8, half // 2), F32),
            pltpu.VMEM((half, D), F32),
            pltpu.VMEM((half, hid), BF16),
            pltpu.VMEM((half, PAGE), F32),
            pltpu.VMEM((6, half, 256), F32),
            pltpu.VMEM((3, half, block), BF16),
            pltpu.VMEM((4, half, block), BF16),
            dma((8,)), dma(()), dma((3,)), dma(()), dma((4,)),
            dma(()), dma((6,)), dma((4,)), dma((4, 3)), dma((2,)), dma((2, 3)),
            dma((2,)), dma((6,)), dma((2,)), dma((6,)),
        ]
        + [dma(()), dma((3,)), dma(()), dma((4,)), dma((4,))]
        + bulk_sems(4, True) + bulk_sems(1, False) + bulk_sems(4, True),
        compiler_params=pltpu.CompilerParams(
            collective_id=0, has_side_effects=True, vmem_limit_bytes=VMEM_LIMIT
        ),
        name="layer",
    )(
        page_table, live_flags, lengths, decay_floor.reshape(1, cols),
        mixer_gain.reshape(1, D), feed_gain.reshape(1, D),
        trainer_mixer_in, token_pages, trainer_mixer_out.T, trainer_gate_up, trainer_down.T,
    )


def solution(mesh):
    in_specs = (
        P("ctx", None, None),
        P("ctx"),
        P("ctx"),
        P(),
        P(("mp", "rep")),
        P(),
        P(),
        P(None, ("ctx", "mp"), None),
        P(None, ("ctx", "mp")),
        P(None, ("ctx", "mp"), None),
        P(None, ("ctx", "mp")),
    )
    out_specs = P(("ctx", "rep"), "mp")
    return jax.shard_map(shards, mesh=mesh, in_specs=in_specs, out_specs=out_specs, check_vma=False)
```

```python
import functools

import jax
import jax.numpy as jnp
from jax import lax
from jax.experimental import pallas as pl
from jax.experimental.pallas import tpu as pltpu
from jax.sharding import PartitionSpec as P

D = 2048
HEADS = 16
PAGE = 128
EPS = 1e-05
VMEM_LIMIT = 67043328
NT = (((1,), (1,)), ((), ()))
TN = (((0,), (0,)), ((), ()))
F32 = jnp.float32
BF16 = jnp.bfloat16


def remote(src, dst, ssem, rsem, **where):
    return pltpu.make_async_remote_copy(
        src_ref=src,
        dst_ref=dst,
        send_sem=ssem,
        recv_sem=rsem,
        device_id=where,
        device_id_type=pl.DeviceIdType.MESH,
    )


def dot(a, b, dims=None):
    if dims is None:
        return jnp.dot(a, b, preferred_element_type=F32)
    return lax.dot_general(a, b, dims, preferred_element_type=F32)


def ring_neighbours():
    mp = lax.axis_size("mp")
    me = lax.axis_index("mp")
    return lax.rem(me + mp - 1, mp), me, lax.rem(me + 1, mp), lax.rem(me + 2, mp)


class Ring:
    def __init__(self, view, rows, whole, ssem, rsem, n):
        self.view, self.half, self.whole = view, rows // 2, whole
        self.ssem, self.rsem, self.n = ssem, rsem, n

    def copy(self, owner, part, k):
        left, _, right, _ = ring_neighbours()
        ref = self.view(owner, part * self.half, self.half)
        return remote(
            ref, ref, self.ssem.at[self.n], self.rsem.at[self.n, k // 2],
            mp=right if k % 2 == 0 else left,
        )

    def take(self, stage):
        left, _, right, _ = ring_neighbours()
        ref = self.view(0, 0, 2 * self.half)
        remote(ref, ref, self.ssem.at[self.n], self.rsem.at[self.n, stage], mp=right).wait_recv()

    def start(self):
        _, me, _, _ = ring_neighbours()
        for k, part in enumerate((0, 1, 1, 0)):
            self.copy(me, part, k).start()

    def relay(self):
        left, _, right, _ = ring_neighbours()
        self.take(0)
        self.copy(left, 0, 4).start()
        self.copy(right, 1, 5).start()

    def near(self):
        self.take(1)

    def finish(self):
        _, _, right, _ = ring_neighbours()
        self.take(2)
        remote(
            self.whole, self.whole, self.ssem.at[self.n], self.rsem.at[self.n, 2], mp=right
        ).wait_send()


class Bulk:
    def __init__(self, hold, w, pack, ysend, yrecv, send, near, far, xrecv, crecv):
        self.w, self.pack = w, pack
        self.ys, self.yr, self.send, self.zn, self.zf = ysend, yrecv, send, near, far
        self.xr, self.cr = xrecv, crecv
        self.pending, self.hold = [], hold
        self.at = Place()
        self.mp, self.me = lax.axis_size("mp"), lax.axis_index("mp")
        self.rows = w.shape[2]
        self.top, self.bottom = pl.ds(0, self.rows // 2), pl.ds(self.rows // 2, self.rows // 2)
        self.all = pl.ds(0, self.rows)

    def span(self, n):
        if self.w.shape[1] == 1:
            return self.w.at[pl.ds(0, n)]
        return self.w.at[0, pl.ds(0, n)] if n < 4 else self.w.at[pl.ds(0, n // 4)]

    def wait_in(self, ref, sem):
        remote(ref, ref, self.send, sem, **self.at.sibling()).wait_recv()

    def wait_out(self, ref, sem):
        remote(ref, ref, sem, self.cr.at[0], **self.at.sibling()).wait_send()

    def owner(self, i):
        return lax.rem(self.me + self.mp - (0, 1, 3, 2)[i], self.mp) if self.pack is not None else 0

    def piece(self, i, rows, xr=0, zr=0, other=0):
        return self.w.at[self.at.ctx(xr, (0, -1, 1, 2)[zr], other), self.owner(i), rows, :]

    def go(self, copy):
        copy.start()

    def y_copy(self, i):
        d = (0, 1, 3, 2)[i]
        to = lax.rem(self.me + d, self.mp)
        return remote(
            self.pack.at[to], self.w.at[self.at.ctx(), self.me], self.ys, self.yr.at[i - 1], mp=to,
        )

    def y_start(self, which=(1, 2, 3)):
        for i in which:
            self.go(self.y_copy(i))

    def z_copy(self, i, xr, k, zr, rows):
        ref = self.piece(i, rows, xr, zr)
        to = self.at.ctx(0, 1 if k in (0, 2) else -1)
        got = (self.zn if k < 2 else self.zf).at[i, xr]
        return remote(ref, ref, self.send, got, ctx=to)

    def x_copies(self, i, zr, xr):
        a, b = self.piece(i, self.top, xr, zr), self.piece(i, self.bottom, xr, zr)
        return [
            remote(a, a, self.send, self.xr.at[i, zr], **self.at.same()),
            remote(b, b, self.send, self.xr.at[i, zr], **self.at.cross()),
        ]

    def c_sem(self, i, xr):
        return self.cr.at[i]

    def c_copy(self, i, xr, zr):
        ref = self.piece(i, self.all, xr, zr)
        return remote(ref, ref, self.send, self.c_sem(i, xr), **self.at.sibling())

    def c_go(self, i, xr, zr):
        if self.hold:
            self.pending.append((i, xr, zr))
        else:
            self.go(self.c_copy(i, xr, zr))

    def flush(self, hold):
        for piece in self.pending:
            self.go(self.c_copy(*piece))
        self.pending, self.hold = [], hold

    def x_go(self, i, zr):
        for copy in self.x_copies(i, zr, 0):
            self.go(copy)

    def x_take(self, i, zr):
        self.wait_in(self.piece(i, self.all, 1, zr), self.xr.at[i, zr])
        self.c_go(i, 1, zr)

    def y_take(self, i):
        self.y_copy(i).wait_recv()

    def z_start(self, i, xr=0):
        self.go(self.z_copy(i, xr, 0, 0, self.all))
        self.go(self.z_copy(i, xr, 1, 0, self.all))
        if xr == 0:
            self.c_go(i, 0, 0)

    def z_relay(self, i, xr=0):
        self.wait_in(self.span(2), self.zn.at[i, xr])
        self.go(self.z_copy(i, xr, 2, 1, self.top))
        self.go(self.z_copy(i, xr, 3, 2, self.bottom))
        self.c_go(i, xr, 1)
        self.c_go(i, xr, 2)

    def z_far(self, i, xr=0):
        self.wait_in(self.piece(i, self.all, xr, 3), self.zf.at[i, xr])
        self.c_go(i, xr, 3)

    def c_take(self, i):
        self.wait_in(self.span(8), self.cr.at[i])

    def drain(self):
        if self.pack is None:
            self.wait_out(self.span(15), self.send)
        else:
            self.wait_out(self.span(60), self.send)
            self.wait_out(self.span(3), self.ys)


class RepBulk(Bulk):
    def __init__(self, w, pack, wx, packx, ysx, yrx, zsx, znx, zfx, *sems):
        super().__init__(False, w, pack, *sems)
        self.wx, self.packx = wx, packx
        self.ysx, self.yrx, self.zsx, self.znx, self.zfx = ysx, yrx, zsx, znx, zfx

    def extra(self, i, zr):
        return self.wx.at[self.at.zi((0, -1, 1, 2)[zr]), self.owner(i)]

    def yx_copy(self, i):
        to = lax.rem(self.me + (0, 1, 3, 2)[i], self.mp)
        return remote(
            self.packx.at[to], self.wx.at[self.at.zi(0), self.me], self.ysx, self.yrx.at[i - 1],
            mp=to,
        )

    def y_start(self, which=(1, 2, 3)):
        for i in which:
            self.go(self.y_copy(i))
            self.go(self.yx_copy(i))

    def y_take(self, i):
        self.y_copy(i).wait_recv()
        self.yx_copy(i).wait_recv()

    def zx_copy(self, i, k, zr):
        ref = self.extra(i, zr)
        to = self.at.ctx(0, 1 if k == 0 or (k == 2 and i % 2 == 0) else -1)
        return remote(ref, ref, self.zsx, (self.znx if k < 2 else self.zfx).at[i], ctx=to)

    def x_copies(self, i, zr, xr):
        a = self.piece(i, self.top, xr, zr)
        b = self.extra(i, zr)
        dst = self.piece(i, self.bottom, xr, zr)
        return [
            remote(a, a, self.send, self.xr.at[i, zr], **self.at.same()),
            remote(b, dst, self.send, self.xr.at[i, zr], **self.at.cross()),
        ]

    def c_sem(self, i, xr):
        return self.cr.at[xr]

    def c_take(self, xr):
        self.wait_in(self.span(16), self.cr.at[xr])

    def z_start(self, i, xr=0):
        super().z_start(i)
        self.go(self.zx_copy(i, 0, 0))
        self.go(self.zx_copy(i, 1, 0))
        self.x_go(i, 0)

    def z_relay(self, i, xr=0):
        super().z_relay(i)
        self.wait_in(self.wx.at[0, pl.ds(0, 2)], self.znx.at[i])
        self.go(self.zx_copy(i, 2, 1 if i % 2 == 0 else 2))
        self.x_go(i, 1)
        self.x_go(i, 2)

    def z_far(self, i, xr=0):
        super().z_far(i)
        self.zx_copy(i, 2, 3).wait_recv()
        self.x_go(i, 3)

    def drain(self):
        super().drain()
        self.wait_out(self.wx.at[pl.ds(0, 3)], self.zsx)
        self.wait_out(self.wx.at[0, pl.ds(0, 3)], self.ysx)


class Place:
    def __init__(self):
        c = lax.axis_index("ctx")
        self.n_z = lax.axis_size("ctx") // 4
        self.core, self.z, self.x = lax.rem(c, 2), lax.rem(c // 2, self.n_z), c // (2 * self.n_z)
        self.rep = lax.axis_index("rep")

    def zi(self, dz):
        return lax.rem(self.z + dz + self.n_z, self.n_z)

    def ctx(self, xr=0, dz=0, other=0):
        x = self.x if xr == 0 else 1 - self.x
        core = self.core if other == 0 else 1 - self.core
        return x * (2 * self.n_z) + self.zi(dz) * 2 + core

    def same(self):
        return dict(ctx=self.ctx(1))

    def cross(self):
        return dict(ctx=self.ctx(1), rep=1 - self.rep)

    def sibling(self):
        return dict(ctx=self.ctx(0, 0, 1))


def greet(peers):
    barrier = pltpu.get_barrier_semaphore()
    for where in peers:
        pl.semaphore_signal(
            barrier, inc=1, device_id=where, device_id_type=pl.DeviceIdType.MESH
        )
    pl.semaphore_wait(barrier, len(peers))


def layer_kernel(
    n_ctx, pages,
    pt_ref, live_ref, len_ref, floor_hbm, mgain_hbm, fgain_hbm,
    tin_hbm, tok_hbm, tout_hbm, tgu_hbm, tdn_hbm,
    out_ref,
    tok_ref, tout_ref, tgu_ref, tdn_ref, tin_ref, floor_ref, mgain_ref, fgain_ref,
    wq_ref, wqx_ref, wo_ref, wf_ref, pkq_ref, pkqx_ref, pkf_ref, x_ref, ord_ref,
    q_ref, k_ref, v_ref, ctot_ref, cnt_ref, st_ref, dec_ref, run_ref, mix_ref,
    msg_ref, in_ref, num_ref, nin_ref, oth_ref, via_ref, head_ref, xall_ref, ss_ref, res_ref,
    hid_ref, rs_ref, acc_ref, send_ref, rin_ref,
    *sems,
):
    (l_sem, n_ssem, n_rsem, s_sem, r_sem, p_ssem, p_rsem, g_ssem, g_rsem, a_ssem, a_rsem,
     b_ssem, b_rsem, t_ssem, t_rsem) = sems[:15]
    sq, so, sf = sems[15:27], sems[27:32], sems[32:39]
    width = 2 * PAGE
    cols, hid = width, tdn_ref.shape[1] // 4
    ctx, rep = lax.axis_index("ctx"), lax.axis_index("rep")
    left, me, right, far = ring_neighbours()
    half_pages = pages // 2
    rows = half_pages * PAGE
    wl = tin_ref.shape[1]
    at = Place()
    bq = RepBulk(wq_ref, pkq_ref, wqx_ref, pkqx_ref, *sq)
    bo = Bulk(True, wo_ref, None, None, None, *so)
    bf = Bulk(True, wf_ref, pkf_ref, *sf)
    loads = [
        pltpu.make_async_copy(a, b, l_sem.at[k])
        for k, (a, b) in enumerate(
            [
                (tin_hbm, tin_ref), (tgu_hbm, tgu_ref), (tdn_hbm, tdn_ref), (tout_hbm, tout_ref),
                (mgain_hbm, mgain_ref), (floor_hbm, floor_ref), (fgain_hbm, fgain_ref),
                (tok_hbm, tok_ref),
            ]
        )
    ]
    for load in loads:
        load.start()

    greet(
        [at.sibling(), at.same(), at.cross()]
        + [dict(ctx=at.ctx(0, dz)) for dz in (1, 2, 3)]
        + [dict(mp=left), dict(mp=right), dict(mp=far)]
    )
    loads[0].wait()
    for y in range(4):
        for t in range(3):
            lane = pl.multiple_of((y * 2 + rep) * cols, cols)
            pkq_ref[y, :, pl.ds(t * cols, cols)] = tin_ref[t, :, pl.ds(lane, cols)].astype(BF16)
            lane = pl.multiple_of((y * 2 + 1 - rep) * cols, cols)
            pkqx_ref[y, :, pl.ds(t * cols, cols)] = tin_ref[
                t, pl.ds(wl // 2, wl // 2), pl.ds(lane, cols)
            ].astype(BF16)
    wq_ref[ctx, me] = pkq_ref[me]
    wqx_ref[at.z, me] = pkqx_ref[me]

    bq.y_start((1, 2))
    bq.z_start(0)

    row8 = lax.broadcasted_iota(jnp.int32, (pages, PAGE), 0)
    lane8 = lax.broadcasted_iota(jnp.int32, (pages, PAGE), 1)
    upto = jnp.zeros((pages, PAGE), jnp.int32)
    alive = jnp.zeros((pages, PAGE), F32)
    so_far = jnp.int32(0)
    for b in range(pages):
        flag = live_ref[b]
        upto = jnp.where(row8 == b, so_far * PAGE + flag * (lane8 + 1), upto)
        alive = jnp.where(row8 == b, flag.astype(F32), alive)
        so_far = so_far + flag
    def num_copy(k):
        to = at.sibling() if k == 0 else at.same() if k == 4 else dict(ctx=at.ctx(0, k))
        src = num_ref.at[0 if k == 0 else 2 if k == 4 else 1]
        return remote(src, nin_ref.at[k], n_ssem, n_rsem.at[(k + 2) // 3], **to)

    num_ref[0] = jnp.zeros((pages, PAGE), jnp.int32) + so_far * PAGE
    num_copy(0).start()

    for load in loads[1:4]:
        load.wait()
    wo_ref[ctx, 0] = tout_ref[...].astype(BF16)
    for y in range(4):
        for j in range(hid // PAGE):
            for t in range(2):
                pkf_ref[y, :, pl.ds(j * 2 * PAGE + t * PAGE, PAGE)] = tgu_ref[
                    t, :, pl.ds(y * hid + j * PAGE, PAGE)
                ].astype(BF16)
        pkf_ref[y, :, pl.ds(2 * hid, hid)] = tdn_ref[:, pl.ds(y * hid, hid)].astype(BF16)
    wf_ref[ctx, me] = pkf_ref[me]
    bf.x_go(0, 0)
    bo.x_go(0, 0)
    for load in loads[4:]:
        load.wait()

    def norm(b):
        x = tok_ref[pt_ref[b]].astype(F32)
        scale = lax.rsqrt(jnp.mean(x * x, axis=-1, keepdims=True) + EPS)
        x_ref[pl.ds(b * PAGE, PAGE), :] = (x * scale * mgain_ref[...]).astype(BF16)

    lane1 = lax.broadcasted_iota(jnp.int32, (1, PAGE), 1) // wl

    def my_columns(read, t):
        tile = None
        for k in range(4):
            turned = pltpu.roll(read(t * 4 + k), lax.rem(wl * (k + 4) - wl * me, PAGE), 1)
            tile = turned if tile is None else jnp.where(lane1 == k, turned, tile)
        return tile

    def pick(j):
        page = pt_ref[rep * half_pages + j]
        for t in range(4):
            tile = my_columns(
                lambda c: tok_ref[page, :, pl.ds(c * PAGE, PAGE)].astype(F32), t
            )
            ord_ref[pl.ds(j * PAGE, PAGE), pl.ds(t * PAGE, PAGE)] = tile

    def project_first(part):
        near = pl.ds(pl.multiple_of(at.x * (D // 2), D // 2), D // 2)
        w = wq_ref[pl.ds(at.x * (n_ctx // 2), n_ctx // 2)].reshape(D // 2, 3 * width)
        x = x_ref[pl.ds(part * rows, rows), near]
        for t in range(3):
            acc_ref[part * 3 + t] = dot(x, w[:, t * width : (t + 1) * width])

    norm(0)
    norm(1)
    norm(2)
    bq.y_start((3,))
    bq.y_take(1)
    bq.z_start(1)
    bq.y_take(2)
    bq.z_start(2)
    num_copy(0).wait_recv()
    num_ref[1] = num_ref[0] + nin_ref[0]
    for k in (1, 2, 3):
        num_copy(k).start()
    norm(3)
    norm(4)
    bq.y_take(3)
    bq.z_start(3)
    bf.y_start((1, 2))
    bq.z_relay(0)
    bf.y_start((3,))
    norm(5)
    bq.x_take(0, 0)
    bq.z_relay(1)
    bq.z_relay(2)
    norm(6)
    bq.x_take(1, 0)
    norm(7)
    bq.x_take(2, 0)
    bq.z_relay(3)
    bo.z_start(0)
    bq.x_take(0, 1)
    bq.x_take(0, 2)
    bq.x_take(3, 0)
    there = nin_ref.at[pl.ds(1, 3)]
    remote(there, there, n_ssem, n_rsem.at[1], **at.sibling()).wait_recv()
    num_ref[2] = num_ref[1] + nin_ref[1] + nin_ref[2] + nin_ref[3]
    num_copy(4).start()
    bq.z_far(0)
    bq.x_take(1, 1)
    bq.x_take(1, 2)
    bq.z_far(1)
    bq.x_take(2, 1)
    bq.x_take(2, 2)
    bq.z_far(2)
    bq.x_take(3, 1)
    bq.x_take(3, 2)
    bq.x_take(0, 3)
    bq.z_far(3)
    bq.x_take(1, 3)
    bo.x_take(0, 0)
    bo.z_start(0, 1)
    bf.y_take(1)
    bf.z_start(1)
    bf.y_take(2)
    bq.c_take(0)
    project_first(0)
    bq.x_take(2, 3)
    bq.x_take(3, 3)
    project_first(1)
    num_copy(4).wait_recv()
    base = jnp.where(at.core == 1, nin_ref[0], 0) + jnp.where(at.x == 1, nin_ref[4], 0)
    for k in (1, 2, 3):
        base = base + jnp.where(k <= at.z, nin_ref[k], 0)
    count = jnp.zeros((pages, PAGE), F32)
    start = jnp.int32(0)
    for j in range(len_ref.shape[0]):
        count = count + jnp.where((base <= start) & (start < base + upto), 1.0, 0.0)
        start = start + len_ref[j]
    cnt_ref[pl.ds(0, 1), :] = jnp.zeros((1, PAGE), F32)
    for b in range(pages):
        cnt_ref[pl.ds(b + 1, 1), :] = count[b : b + 1, :]
    run_ref[...] = jnp.zeros_like(run_ref)
    dec_ref[...] = jnp.ones_like(dec_ref)
    row = lax.broadcasted_iota(jnp.int32, (PAGE, PAGE), 0)
    col = lax.broadcasted_iota(jnp.int32, (PAGE, PAGE), 1)
    lower = row >= col
    tri = jnp.where(lower, 1.0, 0.0).astype(BF16)
    tri = jnp.concatenate([tri, tri], axis=1)
    floor = floor_ref[...]
    bq.c_take(1)
    bf.x_take(0, 0)
    bf.flush(True)
    bo.flush(True)
    for i in (1, 2):
        bf.x_go(i, 0)

    def wide(b):
        return jnp.broadcast_to(cnt_ref[pl.ds(b + 1, 1), :], (PAGE, PAGE))

    def ends(b):
        return cnt_ref[pl.ds(b, 1), :][:, PAGE - 1 :], cnt_ref[pl.ds(b + 1, 1), :][:, PAGE - 1 :]

    def project(i):
        here2 = pl.ds(i * 256, 256)
        away = pl.ds(pl.multiple_of((1 - at.x) * (D // 2), D // 2), D // 2)
        w = wq_ref[pl.ds((1 - at.x) * (n_ctx // 2), n_ctx // 2)].reshape(D // 2, 3 * width)
        p = dot(x_ref[here2, away], w)
        pq, pf, pv = (
            p[:, t * width : (t + 1) * width] + acc_ref[i // 2 * 3 + t, pl.ds(i % 2 * 256, 256), :]
            for t in range(3)
        )
        q = pq / (1.0 + jnp.exp(-pq))
        forget = floor + (1.0 - floor) / (1.0 + jnp.exp(-pf))
        logd, key = jnp.log(forget), 1.0 - forget
        v_ref[here2, :] = pv.astype(BF16)
        for h2 in range(2):
            b = 2 * i + h2
            part = slice(h2 * PAGE, (h2 + 1) * PAGE)
            here = pl.ds(b * PAGE, PAGE)
            live = alive[b : b + 1, :]
            live = jnp.concatenate([live, live], axis=1)
            lg, kk = logd[part] * live, key[part] * live
            hi = lg.astype(BF16)
            lo = (lg - hi.astype(F32)).astype(BF16)
            c = dot(tri, jnp.concatenate([hi, lo], axis=0))
            final = c[PAGE - 1 :, :]
            before, last = ends(b)
            keep = jnp.where(wide(b).T == last, 1.0, 0.0)
            keep = jnp.concatenate([keep, keep], axis=1)
            same = jnp.where(before == last, 1.0, 0.0)
            decay = jnp.exp(final) * same
            q_ref[here, :] = (q[part] * jnp.exp(c)).astype(BF16)
            k_ref[here, :] = (kk * jnp.exp(-c)).astype(BF16)
            ke = (kk * jnp.exp(final - c) * keep).astype(BF16)
            dec = dec_ref[...]
            ctot_ref[pl.ds(b, 1), :] = dec
            dec_ref[...] = dec * decay
            for h in range(2):
                lanes = slice(h * PAGE, (h + 1) * PAGE)
                state = run_ref[h]
                st_ref[b, h] = state
                add = dot(v_ref[here, lanes], ke[:, lanes], TN)
                run_ref[h] = state * decay[:, lanes] + add

    def block_in(ref):
        tail = ref[pl.ds(PAGE, 16), :].astype(F32)
        return ref[pl.ds(0, PAGE), :].astype(F32), tail[0:1, :] + tail[1:2, :]

    def block_out(ref, block):
        state, decay = block
        ref[pl.ds(0, PAGE), :] = state.astype(BF16)
        hi = decay.astype(BF16)
        lo = (decay - hi.astype(F32)).astype(BF16)
        line = lax.broadcasted_iota(jnp.int32, (16, PAGE), 0)
        both = jnp.where(line == 0, hi.astype(F32), jnp.where(line == 1, lo.astype(F32), 0.0))
        ref[pl.ds(PAGE, 16), :] = both.astype(BF16)

    def join(early, late):
        return early[0] * late[1] + late[0], early[1] * late[1]

    def choose(flag, a, b):
        return jnp.where(flag, a[0], b[0]), jnp.where(flag, a[1], b[1])

    def state_copy(k):
        to = at.sibling() if k in (0, 5) else at.same() if k == 4 else dict(ctx=at.ctx(0, k))
        src = msg_ref.at[{0: 0, 4: 2, 5: 3}.get(k, 1)]
        return remote(src, in_ref.at[k], s_sem, r_sem.at[(0, 1, 1, 1, 2, 3)[k]], **to)

    def local_block(h):
        return run_ref[h], dec_ref[:, pl.ds(pl.multiple_of(h * PAGE, PAGE), PAGE)]

    project(0)
    project(1)
    project(2)
    bf.y_take(3)
    bf.x_go(3, 0)
    project(3)
    block_out(msg_ref.at[0], local_block(1 - at.core))
    state_copy(0).start()

    def within(b, _):
        here = pl.ds(pl.multiple_of(b * PAGE, PAGE), PAGE)
        rowwise = wide(b)
        allowed = lower & (rowwise.T == rowwise)
        for h in range(2):
            lanes = slice(h * PAGE, (h + 1) * PAGE)
            scores = dot(q_ref[here, lanes], k_ref[here, lanes], NT)
            scores = jnp.where(allowed, scores, 0.0).astype(BF16)
            mix_ref[here, lanes] = dot(scores, v_ref[here, lanes])
        return 0

    lax.fori_loop(0, 2, within, 0)
    state_copy(0).wait_recv()
    own, sib = local_block(at.core), block_in(in_ref.at[0])
    first, second = choose(at.core == 0, own, sib), choose(at.core == 0, sib, own)
    chip = join(first, second)
    block_out(msg_ref.at[1], chip)
    for k in (1, 2, 3):
        state_copy(k).start()
    bf.z_start(2)
    bf.z_start(3)
    lax.fori_loop(2, pages, within, 0)
    there = in_ref.at[pl.ds(1, 3)]
    remote(there, there, s_sem, r_sem.at[1], **at.sibling()).wait_recv()
    whole = (jnp.zeros((PAGE, PAGE), F32), jnp.ones((1, PAGE), F32))
    ahead = whole
    for z in range(at.n_z):
        there = block_in(msg_ref.at[1])
        for k in (1, 2, 3):
            there = choose(lax.rem(at.z + at.n_z - z, at.n_z) == k, block_in(in_ref.at[k]), there)
        whole = join(whole, there)
        ahead = choose(z < at.z, whole, ahead)
    block_out(msg_ref.at[2], whole)
    state_copy(4).start()
    bf.z_relay(1)
    bo.z_relay(0)
    bo.z_relay(0, 1)
    for j in range(half_pages):
        pick(j)
    state_copy(4).wait_recv()
    before = choose(at.x == 1, block_in(in_ref.at[4]), (jnp.zeros((PAGE, PAGE), F32), jnp.ones((1, PAGE), F32)))
    enter0 = join(before, ahead)
    enter1 = join(enter0, first)
    block_out(msg_ref.at[3], choose(at.core == 0, enter1, enter0))
    state_copy(5).start()
    run_ref[at.core] = choose(at.core == 0, enter0, enter1)[0]
    state_copy(5).wait_recv()
    run_ref[1 - at.core] = block_in(in_ref.at[5])[0]

    def outputs(b, dst, dst_row, dst_lane):
        here = pl.ds(pl.multiple_of(b * PAGE, PAGE), PAGE)
        before, _ = ends(b)
        open_rows = wide(b).T == before
        total = ctot_ref[pl.ds(b, 1), :]
        for h in range(2):
            lanes = slice(h * PAGE, (h + 1) * PAGE)
            state = st_ref[b, h] + total[:, lanes] * run_ref[h]
            old = dot(q_ref[here, lanes], state.astype(BF16), NT)
            mixed = mix_ref[here, lanes] + jnp.where(open_rows, old, 0.0)
            scale = lax.rsqrt(jnp.mean(mixed * mixed, axis=-1, keepdims=True) + EPS)
            dst[dst_row, pl.ds(dst_lane + h * PAGE, PAGE)] = (mixed * scale).astype(BF16)

    def lane_of(owner, which):
        return pl.multiple_of((owner * 2 + which) * width, width)

    def swap_out(k, n):
        to = at.same() if k == 0 else at.cross()
        return remote(
            oth_ref.at[pl.ds((2 * n + k) * PAGE, PAGE), :], via_ref.at[k, n],
            p_ssem, p_rsem.at[2 * k + n], **to,
        )

    def swap_on(k, n):
        to = at.cross() if k == 0 else at.same()
        which = rep if k == 0 else 1 - rep
        dst = head_ref.at[pl.ds((2 * n + k) * PAGE, PAGE), pl.ds(lane_of(me, which), width)]
        return remote(
            via_ref.at[k, n], dst, p_ssem, p_rsem.at[4 + n], **to
        )

    for n in range(2):
        for k in range(2):
            j = 2 * n + k
            outputs((1 - rep) * half_pages + j, oth_ref, pl.ds(j * PAGE, PAGE), 0)
            swap_out(k, n).start()
    bf.flush(False)
    bo.flush(False)
    bf.z_relay(2)
    bf.z_start(0)
    mine = lane_of(me, rep)
    part = rows // 2

    def own_half(j, _):
        outputs(rep * half_pages + j, head_ref, pl.ds(pl.multiple_of(j * PAGE, PAGE), PAGE), mine)
        return 0

    def view(which, n):
        return lambda owner, r, count: head_ref.at[
            pl.ds(n * part + r, count), pl.ds(lane_of(owner, which), width)
        ]

    three = head_ref.at[pl.ds(0, part), pl.ds(0, 3 * width)]
    ring_a = [Ring(view(rep, n), part, three, g_ssem, g_rsem, n) for n in range(2)]
    ring_b = [Ring(view(1 - rep, n), part, three, g_ssem, g_rsem, 2 + n) for n in range(2)]
    ring_x = [
        Ring(
            lambda owner, r, count, n=n: xall_ref.at[owner, pl.ds(n * part + r, count), :],
            part, xall_ref.at[pl.ds(0, 3), pl.ds(0, part), :], a_ssem, a_rsem, n,
        )
        for n in range(2)
    ]
    for n in range(2):
        lax.fori_loop(n * (half_pages // 2), (n + 1) * (half_pages // 2), own_half, 0)
        ring_a[n].start()
    for n in range(2):
        for k in range(2):
            swap_out(k, n).wait_recv()
            swap_on(k, n).start()
    bf.x_go(1, 1)
    bf.x_go(1, 2)
    bf.x_go(2, 1)
    bf.x_go(2, 2)
    bf.z_start(0, 1)
    ring_a[0].relay()
    remote(via_ref.at[0], via_ref.at[0], p_ssem, p_rsem.at[4], **at.sibling()).wait_recv()
    ring_b[0].start()
    ring_a[1].relay()
    remote(via_ref.at[0], via_ref.at[0], p_ssem, p_rsem.at[5], **at.sibling()).wait_recv()
    ring_b[0].relay()
    ring_b[1].start()
    bo.z_far(0)
    bo.z_far(0, 1)
    bf.z_relay(3)
    bf.z_far(1)
    bf.x_go(1, 3)
    ring_b[1].relay()
    bf.z_far(2)
    bf.x_go(2, 3)
    bf.x_go(3, 1)
    bf.x_go(3, 2)
    bo.c_take(0)
    for i in (1, 2, 3):
        bf.x_take(i, 0)
    gain = jnp.concatenate(
        [my_columns(lambda c: jnp.broadcast_to(fgain_ref[:, pl.ds(c * PAGE, PAGE)], (8, PAGE)), t)[0:1] for t in range(4)],
        axis=1,
    )

    def ss_copy(n, k, owner):
        ref = ss_ref.at[n, owner]
        to = left if k == 1 else right
        return remote(ref, ref, b_ssem.at[n], b_rsem.at[3 * n + k], mp=to)

    def out_proj(n):
        here = pl.ds(n * part, part)
        res = ord_ref[here, :] + dot(head_ref[here, :], wo_ref[...].reshape(4 * PAGE, D), NT)
        sqr = res * res
        hi = sqr.astype(BF16)
        lo = (sqr - hi.astype(F32)).astype(BF16)
        ones = jnp.ones((8, sqr.shape[1]), BF16)
        ss_ref[n, me] = dot(ones, hi, NT) + dot(ones, lo, NT)
        ss_copy(n, 0, me).start()
        ss_copy(n, 1, me).start()
        xall_ref[me, here, :] = (res * gain).astype(BF16)
        ring_x[n].start()
        for t in range(4):
            tile = res[:, t * PAGE : (t + 1) * PAGE]
            for k in range(4):
                turned = pltpu.roll(tile, lax.rem(wl * (4 - k) + wl * me, PAGE), 1)
                res_ref[here, pl.ds((t * 4 + k) * PAGE, PAGE)] = jnp.where(lane1 == me, turned, 0.0)

    def x_relay(n):
        ss_copy(n, 0, left).wait_recv()
        ss_copy(n, 2, left).start()
        ss_copy(n, 1, right).wait_recv()
        ring_x[n].relay()

    def x_rest(n):
        ring_x[n].near()
        ss_copy(n, 2, far).wait_recv()
        ring_x[n].finish()
        ss = ss_ref[n, 0]
        for y in range(1, 4):
            ss = ss + ss_ref[n, y]
        scale = lax.rsqrt(ss / D + EPS)[0:1, :]
        rs_ref[pl.ds(n * part, part), :] = jnp.broadcast_to(scale, (PAGE, part)).T

    for ring in (ring_a[0], ring_b[0]):
        ring.near()
        ring.finish()
    out_proj(0)
    bf.z_relay(0, 0)
    for ring in (ring_a[1], ring_b[1]):
        ring.near()
        ring.finish()
    out_proj(1)
    x_relay(0)
    bf.z_far(3)
    bf.x_go(3, 3)
    bf.z_relay(0, 1)
    bf.x_take(1, 1)
    bf.x_take(1, 2)
    bf.x_take(2, 1)
    bf.x_take(2, 2)
    x_relay(1)
    bf.z_far(0, 0)
    bf.x_take(1, 3)
    bf.x_take(2, 3)
    bf.x_take(3, 1)
    bf.x_take(3, 2)
    bf.x_take(3, 3)
    bf.z_far(0, 1)
    bq.drain()
    bo.drain()
    remote(v_ref, v_ref, p_ssem, p_rsem.at[0], **at.sibling()).wait_send()
    remote(in_ref, in_ref, s_sem, r_sem.at[0], **at.sibling()).wait_send()
    remote(nin_ref, nin_ref, n_ssem, n_rsem.at[0], **at.sibling()).wait_send()
    x_rest(0)
    for i in range(4):
        bf.c_take(i)

    def gate_up(n, first, last):
        here = pl.ds(n * part, part)
        for j in range(first, last):
            lanes = pl.ds(j * 256, 256)
            acc = None
            for y in range(4):
                term = dot(xall_ref[y, here, :], wf_ref[:, y, :, lanes].reshape(D // 4, 256))
                acc = term if acc is None else acc + term
            rs = rs_ref[here, :]
            g, u = acc[:, :PAGE] * rs, acc[:, PAGE:] * rs
            hid_ref[here, pl.ds(j * PAGE, PAGE)] = (g / (1.0 + jnp.exp(-g)) * u).astype(BF16)

    def block_of(owner):
        return pl.ds(pl.multiple_of(owner * 4 * PAGE, PAGE), 4 * PAGE)

    def partial(n, owner):
        here = pl.ds(n * part, part)
        w = wf_ref[pl.ds(owner * 4, 4), :, :, pl.ds(2 * hid, hid)].reshape(4 * PAGE, hid)
        res_ref[here, block_of(owner)] = res_ref[here, block_of(owner)] + dot(hid_ref[here, :], w, NT)

    half = part // 2

    class Reduce:
        def __init__(self, n):
            self.n = n
            self.upper, self.under = pl.ds(n * part, half), pl.ds(n * part + half, half)
            self.far_r = self.hop(0, self.upper, 0, 0, right)
            self.far_l = self.hop(0, self.under, 1, 1, left)
            self.near_r1 = self.hop(1, self.under, 2, 2, right)
            self.near_r2 = self.hop(1, self.upper, 2, 3, right)
            self.near_l1 = self.hop(2, self.upper, 3, 4, left)
            self.near_l2 = self.hop(2, self.under, 3, 5, left)

        def hop(self, slot, where, to_slot, k, to):
            return remote(
                send_ref.at[slot, where, :], rin_ref.at[to_slot, where, :],
                t_ssem.at[self.n], t_rsem.at[3 * self.n + min(k, 2)], mp=to,
            )

        def first(self):
            here = pl.ds(self.n * part, part)
            partial(self.n, far)
            send_ref[0, here, :] = res_ref[here, block_of(far)].astype(BF16)
            self.far_r.start()
            self.far_l.start()
            partial(self.n, right)
            send_ref[1, self.under, :] = res_ref[self.under, block_of(right)].astype(BF16)
            self.near_r1.start()
            partial(self.n, left)
            send_ref[2, self.upper, :] = res_ref[self.upper, block_of(left)].astype(BF16)
            self.near_l1.start()

        def second(self):
            self.far_r.wait_recv()
            send_ref[1, self.upper, :] = (
                res_ref[self.upper, block_of(right)] + rin_ref[0, self.upper, :].astype(F32)
            ).astype(BF16)
            self.near_r2.start()
            self.far_l.wait_recv()
            send_ref[2, self.under, :] = (
                res_ref[self.under, block_of(left)] + rin_ref[1, self.under, :].astype(F32)
            ).astype(BF16)
            self.near_l2.start()

        def last(self):
            two = rin_ref.at[pl.ds(0, 2), pl.ds(0, part), :]
            remote(two, two, t_ssem.at[self.n], t_rsem.at[3 * self.n + 2], mp=right).wait_recv()
            for p in range(half_pages // 2):
                page = self.n * (half_pages // 2) + p
                r = pl.ds(page * PAGE, PAGE)
                total = (
                    res_ref[r, block_of(me)] + rin_ref[2, r, :].astype(F32)
                    + rin_ref[3, r, :].astype(F32)
                )
                out_ref[r, :] = jnp.where(
                    live_ref[rep * half_pages + page] == 1, total, 0.0
                ).astype(BF16)

        def drain(self):
            three = send_ref.at[:, pl.ds(0, part), :]
            remote(three, three, t_ssem.at[self.n], t_rsem.at[3 * self.n], mp=right).wait_send()

    reduce = [Reduce(n) for n in range(2)]
    tiles = hid // PAGE
    gate_up(0, 0, tiles)
    reduce[0].first()
    x_rest(1)
    gate_up(1, 0, tiles // 2)
    reduce[0].second()
    gate_up(1, tiles // 2, tiles)
    reduce[1].first()
    partial(0, me)
    partial(1, me)
    reduce[1].second()
    bf.drain()
    for n in range(2):
        three = ss_ref.at[n, pl.ds(0, 3)]
        remote(three, three, b_ssem.at[n], b_rsem.at[0], mp=right).wait_send()
    reduce[0].last()
    reduce[1].last()
    for n in range(2):
        reduce[n].drain()


VM = pl.BlockSpec(memory_space=pltpu.VMEM)
HB = pl.BlockSpec(memory_space=pl.ANY)
SM = pl.BlockSpec(memory_space=pltpu.SMEM)


def shards(
    token_pages, page_table, live_flags, lengths, decay_floor, mixer_gain, feed_gain,
    trainer_mixer_in, trainer_mixer_out, trainer_gate_up, trainer_down,
):
    n_ctx = lax.axis_size("ctx")
    pages, page, _ = token_pages.shape
    tokens, half = pages * page, pages * page // 2
    wl = trainer_mixer_in.shape[1]
    cols = decay_floor.shape[0]
    hid = trainer_gate_up.shape[2] // 4
    block = D // 4
    dma = pltpu.SemaphoreType.DMA

    def bulk_sems(n, y):
        near = [dma(()), dma((3,))] if y else []
        return near + [dma(()), dma((n, 2)), dma((n, 2)), dma((n, 4)), dma((n,))]

    return pl.pallas_call(
        functools.partial(layer_kernel, n_ctx, pages),
        out_shape=jax.ShapeDtypeStruct((half, block), BF16),
        in_specs=[SM, SM, SM] + [HB] * 8,
        out_specs=VM,
        scratch_shapes=[
            pltpu.VMEM((pages, page, D), BF16),
            pltpu.VMEM((wl, D), F32),
            pltpu.VMEM((2, wl, 4 * hid), F32),
            pltpu.VMEM((wl, 4 * hid), F32),
            pltpu.VMEM((3, wl, D), F32),
            pltpu.VMEM((1, cols), F32),
            pltpu.VMEM((1, D), F32),
            pltpu.VMEM((1, D), F32),
            pltpu.VMEM((n_ctx, 4, wl, 3 * cols), BF16),
            pltpu.VMEM((4, 4, wl // 2, 3 * cols), BF16),
            pltpu.VMEM((n_ctx, 1, wl, D), BF16),
            pltpu.VMEM((n_ctx, 4, wl, 3 * hid), BF16),
            pltpu.VMEM((4, wl, 3 * cols), BF16),
            pltpu.VMEM((4, wl // 2, 3 * cols), BF16),
            pltpu.VMEM((4, wl, 3 * hid), BF16),
            pltpu.VMEM((tokens, D), BF16),
            pltpu.VMEM((half, block), F32),
            pltpu.VMEM((tokens, cols), BF16),
            pltpu.VMEM((tokens, cols), BF16),
            pltpu.VMEM((tokens, cols), BF16),
            pltpu.VMEM((pages, cols), F32),
            pltpu.VMEM((16, PAGE), F32),
            pltpu.VMEM((pages, 2, PAGE, PAGE), F32),
            pltpu.VMEM((1, cols), F32),
            pltpu.VMEM((2, PAGE, PAGE), F32),
            pltpu.VMEM((tokens, cols), F32),
            pltpu.VMEM((4, PAGE + 16, PAGE), BF16),
            pltpu.VMEM((6, PAGE + 16, PAGE), BF16),
            pltpu.VMEM((3, pages, PAGE), jnp.int32),
            pltpu.VMEM((5, pages, PAGE), jnp.int32),
            pltpu.VMEM((half, cols), BF16),
            pltpu.VMEM((2, 2, half // 4, cols), BF16),
            pltpu.VMEM((half, D), BF16),
            pltpu.VMEM((4, half, block), BF16),
            pltpu.VMEM((2, 4, 8, half // 2), F32),
            pltpu.VMEM((half, D), F32),
            pltpu.VMEM((half, hid), BF16),
            pltpu.VMEM((half, PAGE), F32),
            pltpu.VMEM((6, half, 256), F32),
            pltpu.VMEM((3, half, block), BF16),
            pltpu.VMEM((4, half, block), BF16),
            dma((8,)), dma(()), dma((3,)), dma(()), dma((4,)),
            dma(()), dma((6,)), dma((4,)), dma((4, 3)), dma((2,)), dma((2, 3)),
            dma((2,)), dma((6,)), dma((2,)), dma((6,)),
        ]
        + [dma(()), dma((3,)), dma(()), dma((4,)), dma((4,))]
        + bulk_sems(4, True) + bulk_sems(1, False) + bulk_sems(4, True),
        compiler_params=pltpu.CompilerParams(
            collective_id=0, has_side_effects=True, vmem_limit_bytes=VMEM_LIMIT
        ),
        name="layer",
    )(
        page_table, live_flags, lengths, decay_floor.reshape(1, cols),
        mixer_gain.reshape(1, D), feed_gain.reshape(1, D),
        trainer_mixer_in, token_pages, trainer_mixer_out.T, trainer_gate_up, trainer_down.T,
    )


def solution(mesh):
    in_specs = (
        P("ctx", None, None),
        P("ctx"),
        P("ctx"),
        P(),
        P(("mp", "rep")),
        P(),
        P(),
        P(None, ("ctx", "mp"), None),
        P(None, ("ctx", "mp")),
        P(None, ("ctx", "mp"), None),
        P(None, ("ctx", "mp")),
    )
    out_specs = P(("ctx", "rep"), "mp")
    return jax.shard_map(shards, mesh=mesh, in_specs=in_specs, out_specs=out_specs, check_vma=False)
```
